32 devices in a mesh: fields: 8 (over y, x, core), blk: 4 (over z).
Axes of the slice: x: 2, y: 2, z: 4, core: 2. Of those that a mesh axis runs over, the one named last changes fastest.
Arguments:
- tokens: bfloat16 [32, 1024, 768], P('fields', 'blk'), may hold values from -6 to 6
- keep_index: int32 [32, 1024], P('fields', 'blk'), may hold values from 0 to 2047, as said below
- counts: int32 [32], P('fields'), may hold values from 205 to 1024, as said below
- norm1_gain: bfloat16 [768], replicated, may hold values from 0.099609375 to 1.8984375
- norm1_bias: bfloat16 [768], replicated, may hold values from -1.75 to 1.75
- qkv_weight: bfloat16 [768, 2304], replicated, may hold values from -0.21875 to 0.21875
- query_bias: bfloat16 [768], replicated, may hold values from -1.75 to 1.75
- value_bias: bfloat16 [768], replicated, may hold values from -1.75 to 1.75
- out_weight: bfloat16 [768, 768], replicated, may hold values from -0.875 to 0.875
- out_bias: bfloat16 [768], replicated, may hold values from -1.75 to 1.75
- norm2_gain: bfloat16 [768], replicated, may hold values from 0.099609375 to 1.8984375
- norm2_bias: bfloat16 [768], replicated, may hold values from -1.75 to 1.75
- up_weight: bfloat16 [768, 3072], replicated, may hold values from -0.21875 to 0.21875
- up_bias: bfloat16 [3072], replicated, may hold values from -1.75 to 1.75
- down_weight: bfloat16 [3072, 768], replicated, may hold values from -0.109375 to 0.109375
- down_bias: bfloat16 [768], replicated, may hold values from -1.75 to 1.75
- cotangent: bfloat16 [32, 1024, 768], P('fields', 'blk'), may hold values from -6 to 6
Outputs:
- output: bfloat16 [32, 1024, 768], P('fields', 'blk')
- input_grad: bfloat16 [32, 1024, 768], P('fields', 'blk')
- norm1_gain_grad: float32 [768], replicated
- norm1_bias_grad: float32 [768], replicated
- qkv_weight_grad: float32 [768, 2304], replicated
- query_bias_grad: float32 [768], replicated
- value_bias_grad: float32 [768], replicated
- out_weight_grad: float32 [768, 768], replicated
- out_bias_grad: float32 [768], replicated
- norm2_gain_grad: float32 [768], replicated
- norm2_bias_grad: float32 [768], replicated
- up_weight_grad: float32 [768, 3072], replicated
- up_bias_grad: float32 [3072], replicated
- down_weight_grad: float32 [3072, 768], replicated
- down_bias_grad: float32 [768], replicated
The draws below stay inside these ranges and needn't reach their ends.
Inputs may be any that keep to these rules, and one draw needn't show every extreme that they name: `keep_index`: within a field the slots carry distinct patch numbers below 2048. `counts`: each field keeps ceil(2048 (100 - m) / 100) patches for an integer mask percentage m of 50 to 90; key slots at or past it are padding.
All inputs are finite; a program needn't handle non-finite values.
Results may differ from the reference program's by a relative error of at most 0.025.
Values may be sent and summed in bfloat16 or wider, within the bound.
A program may use at most 320 MiB of HBM per device.

```python
import jax
import jax.numpy as jnp
from jax import lax

D = 768
HEADS = 12
HEAD_DIM = 64
FF = 3072
SLOTS = 1024
GRID_W = 64
PATCHES = 2048
FIELDS = 32


def draw_counts(key, part):
    percent = jax.random.randint(jax.random.fold_in(key, 11), (FIELDS,), 50, 91).astype(jnp.int32)
    percent = percent.at[0].set(50).at[1].set(90)
    return ((PATCHES * (100 - percent) + 99) // 100).astype(jnp.int32)


def draw_keep_index(key, part):
    field_keys = jax.random.split(jax.random.fold_in(key, 23), FIELDS)
    orders = jax.vmap(lambda one: jax.random.permutation(one, PATCHES))(field_keys)
    return orders[:, :SLOTS].astype(jnp.int32)


def steps_of(own_key, shape, cuts, least, high):
    loudness, own = 1.0, jax.random.fold_in(own_key, 6)
    for dim, shards_of in cuts:
        heights = jnp.exp(jax.random.uniform(jax.random.fold_in(own, dim), (shards_of,), jnp.float32, least / len(cuts), high / len(cuts)))
        loudness = loudness * jnp.repeat(heights, shape[dim] // shards_of).reshape([-1 if axis == dim else 1 for axis in range(len(shape))])
    return loudness


def bell_draw(stream_key, extent, scale, reach, cuts=(), held_as=jnp.bfloat16):
    level = steps_of(stream_key, extent, cuts, -0.22, 0.18) if cuts else 1.0
    values = jax.random.normal(stream_key, extent, jnp.float32) * scale * level
    return jnp.minimum(jnp.maximum(values, -reach), reach).astype(held_as)


def setup_inputs(seed: int = 0) -> dict:
    streams_of = jax.random.split(jax.random.key(seed), 18)
    return {
        "tokens": bell_draw(streams_of[0], (FIELDS, SLOTS, D), 1.0, 6.0, ((0, 8), (1, 4))),
        "keep_index": draw_keep_index(jax.random.fold_in(streams_of[17], 71), 0),
        "counts": draw_counts(jax.random.fold_in(streams_of[17], 71), 0),
        "norm1_gain": jnp.clip(1.0 + 0.18 * jax.random.normal(streams_of[3], (D,), jnp.float32), 0.099609375, 1.8984375).astype(jnp.bfloat16),
        "norm1_bias": bell_draw(streams_of[4], (D,), 0.3, 1.75),
        "qkv_weight": bell_draw(streams_of[5], (D, 3 * D), D ** -0.5, 0.21875),
        "query_bias": bell_draw(streams_of[6], (D,), 0.3, 1.75),
        "value_bias": bell_draw(streams_of[7], (D,), 0.3, 1.75),
        "out_weight": bell_draw(streams_of[8], (D, D), (D // 16) ** -0.5, 0.875),
        "out_bias": bell_draw(streams_of[9], (D,), 0.3, 1.75),
        "norm2_gain": jnp.clip(1.0 + 0.18 * jax.random.normal(streams_of[10], (D,), jnp.float32), 0.099609375, 1.8984375).astype(jnp.bfloat16),
        "norm2_bias": bell_draw(streams_of[11], (D,), 0.3, 1.75),
        "up_weight": bell_draw(streams_of[12], (D, FF), D ** -0.5, 0.21875),
        "up_bias": bell_draw(streams_of[13], (FF,), 0.3, 1.75),
        "down_weight": bell_draw(streams_of[14], (FF, D), FF ** -0.5, 0.109375),
        "down_bias": bell_draw(streams_of[15], (D,), 0.3, 1.75),
        "cotangent": bell_draw(streams_of[16], (FIELDS, SLOTS, D), 1.0, 6.0, ((0, 8), (1, 4))),
    }


@jax.custom_vjp
def low(v):
    return lax.optimization_barrier(v.astype(jnp.bfloat16)).astype(jnp.float32)

@jax.custom_vjp
def low_back(v):
    return v

def low_keep(v):
    return (low(v), None)

def low_pass(kept, grad):
    return (grad,)

def back_keep(v):
    return (v, None)

def back_low(kept, grad):
    return (low(grad),)
low.defvjp(low_keep, low_pass)
low_back.defvjp(back_keep, back_low)
epsilon = 1e-06
negative = -1e+30
highest = lax.Precision.HIGHEST

def positional(keep, width):
    row_pos = (keep // GRID_W).astype(jnp.float32)
    col_pos = (keep % GRID_W).astype(jnp.float32)
    quarter = width // 4
    omega = 1.0 / 10000.0 ** (jnp.arange(quarter).astype(jnp.float32) / quarter)
    row_ang = row_pos[..., None] * omega
    col_ang = col_pos[..., None] * omega
    return jnp.concatenate([jnp.sin(row_ang), jnp.cos(row_ang), jnp.sin(col_ang), jnp.cos(col_ang)], -1)

def layer_norm(values, gain, bias):
    centre = lax.optimization_barrier(jnp.mean(values, -1, keepdims=True))
    centred = values - centre
    spread = lax.optimization_barrier(jnp.mean(centred * centred, -1, keepdims=True))
    return centred * lax.rsqrt(spread + epsilon) * gain + bias

def attend(query, key_rows, value_rows, count):
    scores = jnp.einsum('qhd,khd->hqk', query, key_rows, precision=highest) * HEAD_DIM ** (-0.5)
    scores = low_back(scores)
    visible = jnp.arange(key_rows.shape[0]).astype(jnp.int32) < count
    scores = jnp.where(visible[None, None, :], scores, negative)
    probs = low(jax.nn.softmax(scores, -1))
    mixed = jnp.einsum('hqk,khd->qhd', probs, value_rows, precision=highest)
    return mixed.reshape(query.shape[0], HEADS * HEAD_DIM)

def forward(tokens, keep_index, counts, norm1_gain, norm1_bias, qkv_weight, query_bias, value_bias, out_weight, out_bias, norm2_gain, norm2_bias, up_weight, up_bias, down_weight, down_bias):
    x_zero = (tokens + positional(keep_index, D)).reshape(FIELDS * SLOTS, D)
    a_one = low(layer_norm(x_zero, norm1_gain, norm1_bias))
    qkv = jnp.dot(a_one, qkv_weight, precision=highest)
    query = low(low_back(qkv[:, :D] + query_bias)).reshape(FIELDS, SLOTS, HEADS, HEAD_DIM)
    keys = low(low_back(qkv[:, D:2 * D])).reshape(FIELDS, SLOTS, HEADS, HEAD_DIM)
    values = low(low_back(qkv[:, 2 * D:] + value_bias)).reshape(FIELDS, SLOTS, HEADS, HEAD_DIM)
    checked = jax.checkpoint(attend)
    mixed = lax.map(lambda item: checked(item[0], item[1], item[2], item[3]), (query, keys, values, counts))
    attn_out = low(low_back(mixed.reshape(FIELDS * SLOTS, D)))
    branch = low_back(jnp.dot(attn_out, out_weight, precision=highest) + out_bias)
    x_one = x_zero + branch
    a_two = low(layer_norm(x_one, norm2_gain, norm2_bias))
    hidden = low_back(jnp.dot(a_two, up_weight, precision=highest) + up_bias)
    gelu_out = low(jax.nn.gelu(hidden, approximate=False))
    result = x_one + jnp.dot(gelu_out, down_weight, precision=highest) + down_bias
    return result.reshape(FIELDS, SLOTS, D)

def reference(tokens, keep_index, counts, norm1_gain, norm1_bias, qkv_weight, query_bias, value_bias, out_weight, out_bias, norm2_gain, norm2_bias, up_weight, up_bias, down_weight, down_bias, cotangent):
    floats = [a.astype(jnp.float32) for a in (tokens, norm1_gain, norm1_bias, qkv_weight, query_bias, value_bias, out_weight, out_bias, norm2_gain, norm2_bias, up_weight, up_bias, down_weight, down_bias)]

    def wrapped(tok, g_one, b_one, w_qkv_f, b_query_f, b_value_f, w_out_f, b_out_f, g_two, b_two, w_up_f, b_up_f, w_down_f, b_down_f):
        return forward(tok, keep_index, counts, g_one, b_one, w_qkv_f, b_query_f, b_value_f, w_out_f, b_out_f, g_two, b_two, w_up_f, b_up_f, w_down_f, b_down_f)
    result, pull = jax.vjp(wrapped, *floats)
    grads = pull(cotangent.astype(jnp.float32))
    return (result.astype(jnp.bfloat16), grads[0].astype(jnp.bfloat16), grads[1], grads[2], grads[3], grads[4], grads[5], grads[6], grads[7], grads[8], grads[9], grads[10], grads[11], grads[12], grads[13])
```

```python
from functools import partial
import math
import jax
import jax.numpy as jnp
from jax import lax
from jax.experimental import pallas as pl
from jax.experimental.pallas import tpu as pltpu
from jax.sharding import PartitionSpec as P

HEAD_DIM = 64
GRID_W = 64
epsilon = 1e-06
negative = -1e30
VMEM_BYTES = 60 * 1024 * 1024
LOG2E = math.log2(math.e)
F32 = jnp.float32
BF16 = jnp.bfloat16


def mm(a, b, ca, cb):
    return lax.dot_general(a, b, (((ca,), (cb,)), ((), ())), preferred_element_type=F32)


def whole(shape):
    return pl.BlockSpec(shape, lambda *_: (0,) * len(shape), pipeline_mode=pl.Buffered(1))


def norm_parts(values):
    centre = jnp.mean(values, -1, keepdims=True)
    centred = values - centre
    spread = jnp.mean(centred * centred, -1, keepdims=True)
    scale = lax.rsqrt(spread + epsilon)
    return centred * scale, scale


def norm_back(grad, hat, scale, gain):
    scaled = grad * gain
    return scale * (
        scaled
        - jnp.mean(scaled, -1, keepdims=True)
        - hat * jnp.mean(scaled * hat, -1, keepdims=True)
    )


def thirds(row):
    high = row.astype(BF16)
    rest = row - high.astype(F32)
    mid = rest.astype(BF16)
    low = (rest - mid.astype(F32)).astype(BF16)
    return high, mid, low


def project_kernel(tok, keep, row_table, col_table, gain, bias, weight, qb, vb, x0, a1t, qt, k, kt, v, vt):
    width = tok.shape[1]
    rows = tok.shape[0]
    patch = keep[...]
    tall = row_table.shape[0]
    wide = col_table.shape[0]
    row_hot = (lax.broadcasted_iota(jnp.int32, (rows, tall), 1) == patch // GRID_W).astype(F32)
    col_hot = (lax.broadcasted_iota(jnp.int32, (rows, wide), 1) == patch % GRID_W).astype(F32)
    pos_row = jnp.dot(row_hot, row_table[...], precision=lax.Precision.HIGHEST, preferred_element_type=F32)
    pos_col = jnp.dot(col_hot, col_table[...], precision=lax.Precision.HIGHEST, preferred_element_type=F32)
    x = tok[...].astype(F32) + jnp.concatenate([pos_row, pos_col], -1)
    x0[...] = x
    hat, _ = norm_parts(x)
    a = (hat * gain[...].astype(F32) + bias[...].astype(F32)).astype(BF16)
    a1t[...] = a.T
    q = (jnp.dot(a, weight[:, :width], preferred_element_type=F32) + qb[...].astype(F32)).astype(BF16)
    qt[...] = q.T
    kk = jnp.dot(a, weight[:, width : 2 * width], preferred_element_type=F32).astype(BF16)
    k[...] = kk
    kt[...] = kk.T
    vv = (jnp.dot(a, weight[:, 2 * width :], preferred_element_type=F32) + vb[...].astype(F32)).astype(BF16)
    v[...] = vv
    vt[...] = vv.T


def project(tok, keep, tables, gain, bias, weight, qb, vb, block=256):
    slots, width = tok.shape
    nat = pl.BlockSpec((block, width), lambda i: (i, 0))
    tra = pl.BlockSpec((width, block), lambda i: (0, i))
    sn = jax.ShapeDtypeStruct((slots, width), BF16)
    st = jax.ShapeDtypeStruct((width, slots), BF16)
    return pl.pallas_call(
        project_kernel,
        grid=(slots // block,),
        in_specs=[
            nat,
            pl.BlockSpec((block, 1), lambda i: (i, 0)),
            whole(tables[0].shape),
            whole(tables[1].shape),
            whole((1, width)),
            whole((1, width)),
            whole(weight.shape),
            whole((1, width)),
            whole((1, width)),
        ],
        out_specs=[nat, tra, tra, nat, tra, nat, tra],
        out_shape=[jax.ShapeDtypeStruct((slots, width), F32), st, st, sn, st, sn, st],
        compiler_params=pltpu.CompilerParams(vmem_limit_bytes=VMEM_BYTES),
        cost_estimate=pl.CostEstimate(flops=2 * slots * width * 3 * width, bytes_accessed=20 * slots * width, transcendentals=0),
        name="project",
    )(tok, keep[:, None], *tables, gain[None], bias[None], weight, qb[None], vb[None])


def augment_cols(block, extra, second):
    lane = lax.broadcasted_iota(jnp.int32, block.shape, 1)
    return jnp.where((lane >= HEAD_DIM) if second else (lane < HEAD_DIM), block, extra)


def augment_rows(block, extra, second):
    if second:
        return jnp.concatenate([extra, block[HEAD_DIM:]], 0)
    return jnp.concatenate([block[:HEAD_DIM], extra], 0)


def key_bias(count, slots):
    return jnp.where(lax.broadcasted_iota(jnp.int32, (slots, 1), 0) < count, 0.0, negative)


def attend_kernel(block, count, qt, k, vt, o, ot, lse):
    slots = k.shape[0]
    c = HEAD_DIM**-0.5 * LOG2E
    lane = lax.broadcasted_iota(jnp.int32, (slots, 2 * HEAD_DIM), 1)
    kb = key_bias(count[0, 0], slots)
    extra_col = jnp.where(lane % HEAD_DIM == 0, kb, 0.0).astype(BF16)
    sub = lax.broadcasted_iota(jnp.int32, (HEAD_DIM, block), 0)
    extra_row = jnp.where(sub == 0, 1.0, 0.0).astype(BF16)
    subv = lax.broadcasted_iota(jnp.int32, (16, slots), 0)
    ones = jnp.where(subv == 0, 1.0, 0.0).astype(BF16)
    for head in range(2):
        ka = augment_cols(k[...], extra_col, head == 1)
        va = jnp.concatenate([vt[head * HEAD_DIM : (head + 1) * HEAD_DIM, :], ones], 0)
        for i in range(slots // block):
            cols = slice(i * block, (i + 1) * block)
            qa = augment_rows(qt[:, cols], extra_row, head == 1)
            s = mm(ka, qa, 1, 0)
            top = jnp.max(s, 0, keepdims=True)
            p = jnp.exp2((s - top) * c).astype(BF16)
            r = mm(va, p, 1, 0)
            total = r[HEAD_DIM : HEAD_DIM + 1]
            mixed = (r[:HEAD_DIM] / total).astype(BF16)
            ot[head * HEAD_DIM : (head + 1) * HEAD_DIM, cols] = mixed
            lse[0, head : head + 1, cols] = top * HEAD_DIM**-0.5 + jnp.log(total)
    o[...] = ot[...].T


def attend(count, qt, k, vt, block=256):
    slots, width = k.shape
    pairs = width // (2 * HEAD_DIM)
    tra = pl.BlockSpec((2 * HEAD_DIM, slots), lambda j: (j, 0))
    nat = pl.BlockSpec((slots, 2 * HEAD_DIM), lambda j: (0, j))
    return pl.pallas_call(
        partial(attend_kernel, block),
        grid=(pairs,),
        in_specs=[pl.BlockSpec(memory_space=pltpu.SMEM), tra, nat, tra],
        out_specs=[nat, tra, pl.BlockSpec((1, 2, slots), lambda j: (j, 0, 0))],
        out_shape=[
            jax.ShapeDtypeStruct((slots, width), BF16),
            jax.ShapeDtypeStruct((width, slots), BF16),
            jax.ShapeDtypeStruct((pairs, 2, slots), F32),
        ],
        compiler_params=pltpu.CompilerParams(vmem_limit_bytes=VMEM_BYTES),
        cost_estimate=pl.CostEstimate(flops=16 * slots * slots * width, bytes_accessed=12 * slots * width, transcendentals=slots * slots * 12),
        name="attend",
    )(count, qt, k, vt)


def middle_kernel(
    o, ot, x0, y, w_out, b_out, gain, bias, up, up_bias, down, down_bias,
    out, d_up, d_up_bias, d_down, d_out, dx1, dot_, vecs,
    x1, hat, scale, a2, a2t, acc, dacc,
):
    step = pl.program_id(0)
    last = pl.num_programs(0) - 1

    @pl.when(step == 0)
    def _():
        x = x0[...] + jnp.dot(o[...], w_out[...], preferred_element_type=F32) + b_out[...].astype(F32)
        x1[...] = x
        h, s = norm_parts(x)
        hat[...] = h
        scale[...] = s
        a = (h * gain[...].astype(F32) + bias[...].astype(F32)).astype(BF16)
        a2[...] = a
        a2t[...] = a.T
        acc[...] = jnp.zeros_like(acc)
        dacc[...] = jnp.zeros_like(dacc)

    h = jnp.dot(a2[...], up[...], preferred_element_type=F32) + up_bias[...].astype(F32)
    phi = 0.5 + 0.5 * lax.erf(h * (0.5**0.5))
    slope = phi + h * (jnp.exp2(h * h * (-0.5 * LOG2E)) * (2 * math.pi) ** -0.5)
    g = (h * phi).astype(BF16)
    dg = mm(y[...], down[...], 1, 1)
    dh = (dg * slope).astype(BF16)
    d_up_bias[...] = jnp.sum(dh.astype(F32), 0, keepdims=True)
    acc[...] += jnp.dot(g, down[...], preferred_element_type=F32)
    dacc[...] += mm(dh, up[...], 1, 1)
    d_up[...] = jnp.dot(a2t[...], dh, preferred_element_type=F32).astype(BF16)
    d_down[...] = jnp.dot(g.T, y[...], preferred_element_type=F32).astype(BF16)

    @pl.when(step == last)
    def _():
        out[...] = (x1[...] + acc[...] + down_bias[...].astype(F32)).astype(BF16)
        grad = dacc[...]
        yf = y[...].astype(F32)
        dx = yf + norm_back(grad, hat[...], scale[...], gain[...].astype(F32))
        dx1[...] = dx
        dz = dx.astype(BF16)
        vecs[0:1, :] = jnp.sum(grad * hat[...], 0, keepdims=True)
        vecs[1:2, :] = jnp.sum(grad, 0, keepdims=True)
        vecs[2:3, :] = jnp.sum(yf, 0, keepdims=True)
        vecs[3:4, :] = jnp.sum(dz.astype(F32), 0, keepdims=True)
        vecs[4:8, :] = jnp.zeros_like(vecs[4:8, :])
        d_out[...] = jnp.dot(ot[...], dz, preferred_element_type=F32).astype(BF16)
        dot_[...] = mm(dz, w_out[...], 1, 1).astype(BF16).T


def middle(o, ot, x0, y, w_out, b_out, gain, bias, up, up_bias, down, down_bias, block=256):
    slots, width = o.shape
    ff = up.shape[1]
    return pl.pallas_call(
        middle_kernel,
        grid=(ff // block,),
        in_specs=[
            whole((slots, width)),
            whole((width, slots)),
            whole((slots, width)),
            whole((slots, width)),
            whole((width, width)),
            whole((1, width)),
            whole((1, width)),
            whole((1, width)),
            pl.BlockSpec((width, block), lambda i: (0, i)),
            pl.BlockSpec((1, block), lambda i: (0, i)),
            pl.BlockSpec((block, width), lambda i: (i, 0)),
            whole((1, width)),
        ],
        out_specs=[
            whole((slots, width)),
            pl.BlockSpec((width, block), lambda i: (0, i)),
            pl.BlockSpec((1, block), lambda i: (0, i)),
            pl.BlockSpec((block, width), lambda i: (i, 0)),
            whole((width, width)),
            whole((slots, width)),
            whole((width, slots)),
            whole((8, width)),
        ],
        out_shape=[
            jax.ShapeDtypeStruct((slots, width), BF16),
            jax.ShapeDtypeStruct((width, ff), BF16),
            jax.ShapeDtypeStruct((1, ff), F32),
            jax.ShapeDtypeStruct((ff, width), BF16),
            jax.ShapeDtypeStruct((width, width), BF16),
            jax.ShapeDtypeStruct((slots, width), F32),
            jax.ShapeDtypeStruct((width, slots), BF16),
            jax.ShapeDtypeStruct((8, width), F32),
        ],
        scratch_shapes=[
            pltpu.VMEM((slots, width), F32),
            pltpu.VMEM((slots, width), F32),
            pltpu.VMEM((slots, 1), F32),
            pltpu.VMEM((slots, width), BF16),
            pltpu.VMEM((width, slots), BF16),
            pltpu.VMEM((slots, width), F32),
            pltpu.VMEM((slots, width), F32),
        ],
        compiler_params=pltpu.CompilerParams(vmem_limit_bytes=VMEM_BYTES),
        cost_estimate=pl.CostEstimate(flops=12 * slots * width * ff, bytes_accessed=20 * slots * width, transcendentals=2 * slots * ff),
        name="middle",
    )(o, ot, x0, y, w_out, b_out[None], gain[None], bias[None], up, up_bias[None], down, down_bias[None])


def back_kernel(
    block, count, qt, k, kt, v, dot_, ot, lse, a1t, wq, wk, wv, x0, dx1, gain,
    dwq, dwk, dwv, dqb, dvb, din, vecs,
    acc, dt,
):
    step = pl.program_id(0)
    last = pl.num_programs(0) - 1
    slots = k.shape[0]
    pair = 2 * HEAD_DIM
    c = HEAD_DIM**-0.5 * LOG2E
    scale = HEAD_DIM**-0.5
    lane = lax.broadcasted_iota(jnp.int32, (slots, pair), 1) % HEAD_DIM
    kb = key_bias(count[0, 0], slots)
    extra_k = jnp.where(lane == 0, kb, jnp.where(lane < 4, 1.0, 0.0)).astype(BF16)
    extra_v = jnp.where(lane < 3, 1.0, 0.0).astype(BF16)
    zeros = jnp.zeros((HEAD_DIM - 4, slots), F32)
    one = jnp.ones((1, slots), F32)
    for head in range(2):
        rows = slice(head * HEAD_DIM, (head + 1) * HEAD_DIM)
        ka = augment_cols(k[...], extra_k, head == 1)
        va = augment_cols(v[...], extra_v, head == 1)
        delta = jnp.sum(dot_[rows, :].astype(F32) * ot[rows, :].astype(F32), 0, keepdims=True)
        l3 = [t.astype(F32) for t in thirds(lse[0, head : head + 1, :] * -(HEAD_DIM**0.5))]
        d3 = [t.astype(F32) for t in thirds(-delta)]
        extra_q = jnp.concatenate([one, *l3, zeros], 0).astype(BF16)
        extra_d = jnp.concatenate([*d3, zeros, 0.0 * one], 0).astype(BF16)
        qa = augment_rows(qt[...], extra_q, head == 1)
        da = augment_rows(dot_[...], extra_d, head == 1)
        for i in range(slots // block):
            cols = slice(i * block, (i + 1) * block)
            s = mm(ka, qa[:, cols], 1, 0)
            dp = mm(va, da[:, cols], 1, 0)
            p = jnp.exp2(s * c)
            ds = (p * dp).astype(BF16)
            p = p.astype(BF16)
            dt[head * HEAD_DIM : (head + 1) * HEAD_DIM, cols] = (mm(kt[rows, :], ds, 1, 0) * scale).astype(BF16)
            dv = mm(dot_[rows, cols], p, 1, 1)
            dk = mm(qt[rows, cols], ds, 1, 1)
            if i == 0:
                dv_sum, dk_sum = dv, dk
            else:
                dv_sum, dk_sum = dv_sum + dv, dk_sum + dk
        dt[pair + head * HEAD_DIM : pair + (head + 1) * HEAD_DIM, :] = (dk_sum * scale).astype(BF16)
        dt[2 * pair + head * HEAD_DIM : 2 * pair + (head + 1) * HEAD_DIM, :] = dv_sum.astype(BF16)

    d = dt[...]
    grads = mm(a1t[...], d, 1, 1).astype(BF16)
    dwq[...] = grads[:, :pair]
    dwk[...] = grads[:, pair : 2 * pair]
    dwv[...] = grads[:, 2 * pair :]
    dqb[...] = jnp.broadcast_to(jnp.sum(d[:pair].astype(F32), 1, keepdims=True), dqb.shape)
    dvb[...] = jnp.broadcast_to(jnp.sum(d[2 * pair :].astype(F32), 1, keepdims=True), dvb.shape)
    w = jnp.concatenate([wq[...], wk[...], wv[...]], 1)
    part = mm(d.T, w, 1, 1)

    @pl.when(step == 0)
    def _():
        acc[...] = part

    @pl.when(step > 0)
    def _():
        acc[...] += part

    @pl.when(step == last)
    def _():
        grad = acc[...]
        hat, sc = norm_parts(x0[...])
        dn = norm_back(grad, hat, sc, gain[...].astype(F32))
        din[...] = (dx1[...] + dn).astype(BF16)
        vecs[0:1, :] = jnp.sum(grad * hat, 0, keepdims=True)
        vecs[1:2, :] = jnp.sum(grad, 0, keepdims=True)
        vecs[2:8, :] = jnp.zeros_like(vecs[2:8, :])


def back(count, qt, k, kt, v, dot_, ot, lse, a1t, weight, x0, dx1, gain, block=256):
    slots, width = k.shape
    pair = 2 * HEAD_DIM
    pairs = width // pair
    tra = pl.BlockSpec((pair, slots), lambda j: (j, 0))
    nat = pl.BlockSpec((slots, pair), lambda j: (0, j))

    def cols(part):
        return pl.BlockSpec((width, pair), lambda j: (0, part * pairs + j))

    sw = jax.ShapeDtypeStruct((width, width), BF16)
    sb = jax.ShapeDtypeStruct((width, 128), F32)
    return pl.pallas_call(
        partial(back_kernel, block),
        grid=(pairs,),
        in_specs=[
            pl.BlockSpec(memory_space=pltpu.SMEM),
            tra, nat, tra, nat, tra, tra,
            pl.BlockSpec((1, 2, slots), lambda j: (j, 0, 0)),
            whole((width, slots)),
            cols(0), cols(1), cols(2),
            whole((slots, width)),
            whole((slots, width)),
            whole((1, width)),
        ],
        out_specs=[cols(0), cols(0), cols(0), pl.BlockSpec((pair, 128), lambda j: (j, 0)), pl.BlockSpec((pair, 128), lambda j: (j, 0)),
            whole((slots, width)), whole((8, width))],
        out_shape=[sw, sw, sw, sb, sb, jax.ShapeDtypeStruct((slots, width), BF16), jax.ShapeDtypeStruct((8, width), F32)],
        scratch_shapes=[pltpu.VMEM((slots, width), F32), pltpu.VMEM((3 * pair, slots), BF16)],
        compiler_params=pltpu.CompilerParams(vmem_limit_bytes=VMEM_BYTES),
        cost_estimate=pl.CostEstimate(flops=40 * slots * slots * width, bytes_accessed=30 * slots * width, transcendentals=slots * slots * 12),
        name="back",
    )(count, qt, k, kt, v, dot_, ot, lse, a1t, weight, weight, weight, x0, dx1, gain[None])


def tables(width):
    quarter = width // 4
    omega = 1.0 / 10000.0 ** (jnp.arange(quarter).astype(F32) / quarter)

    def table(length):
        ang = jnp.arange(length).astype(F32)[:, None] * omega
        return jnp.concatenate([jnp.sin(ang), jnp.cos(ang)], -1)

    return table(2048 // GRID_W), table(GRID_W)


def to_field(part):
    return lax.all_to_all(part, "blk", 0, 1, tiled=True)[0]


def to_slots(whole_field):
    return lax.all_to_all(whole_field[None], "blk", 1, 0, tiled=True)


def per_device(
    tokens, keep_index, counts, norm1_gain, norm1_bias, qkv_weight, query_bias, value_bias, out_weight, out_bias,
    norm2_gain, norm2_bias, up_weight, up_bias, down_weight, down_bias, cotangent,
):
    width = tokens.shape[2]
    both = ("fields", "blk")
    count = lax.dynamic_slice(counts, (lax.axis_index("blk"),), (1,))[None]
    x0, a1t, qt, k, kt, v, vt = project(
        to_field(tokens), to_field(keep_index), tables(width), norm1_gain, norm1_bias, qkv_weight, query_bias, value_bias
    )
    y = to_field(cotangent)
    o, ot, lse = attend(count, qt, k, vt)
    out, d_up, d_up_bias, d_down, d_out, dx1, dot_, vecs_two = middle(
        o, ot, x0, y, out_weight, out_bias, norm2_gain, norm2_bias, up_weight, up_bias, down_weight, down_bias
    )
    d_up, d_down, d_out = lax.psum((d_up, d_down, d_out), both)
    output = to_slots(out)
    dwq, dwk, dwv, dqb, dvb, din, vecs_one = back(
        count, qt, k, kt, v, dot_, ot, lse, a1t, qkv_weight, x0, dx1, norm1_gain
    )
    dwq, dwk, dwv = lax.psum((dwq, dwk, dwv), both)
    input_grad = to_slots(din)
    vecs = jnp.concatenate(
        [vecs_one[:2], vecs_two[:4], dqb[:, 0][None], dvb[:, 0][None], d_up_bias.reshape(-1, width)], 0
    )
    vecs = lax.psum(vecs, both)
    return (
        output,
        input_grad,
        vecs[0],
        vecs[1],
        jnp.concatenate([dwq, dwk, dwv], 1).astype(F32),
        vecs[6],
        vecs[7],
        d_out.astype(F32),
        vecs[5],
        vecs[2],
        vecs[3],
        d_up.astype(F32),
        vecs[8:].reshape(-1),
        d_down.astype(F32),
        vecs[4],
    )


def solution(mesh):
    rows = P("fields", "blk", None)
    return jax.shard_map(
        per_device,
        mesh=mesh,
        in_specs=(rows, P("fields", "blk"), P("fields"), *[P()] * 13, rows),
        out_specs=(rows, rows, *[P()] * 13),
        check_vma=False,
    )
```

```python
from functools import partial
import math
import jax
import jax.numpy as jnp
from jax import lax
from jax.experimental import pallas as pl
from jax.experimental.pallas import tpu as pltpu
from jax.sharding import PartitionSpec as P

HEAD_DIM = 64
GRID_W = 64
epsilon = 1e-06
negative = -1e30
VMEM_BYTES = 60 * 1024 * 1024
LOG2E = math.log2(math.e)
F32 = jnp.float32
BF16 = jnp.bfloat16


def mm(a, b, ca, cb):
    return lax.dot_general(a, b, (((ca,), (cb,)), ((), ())), preferred_element_type=F32)


def whole(shape):
    return pl.BlockSpec(shape, lambda *_: (0,) * len(shape), pipeline_mode=pl.Buffered(1))


def norm_parts(values):
    centre = jnp.mean(values, -1, keepdims=True)
    centred = values - centre
    spread = jnp.mean(centred * centred, -1, keepdims=True)
    scale = lax.rsqrt(spread + epsilon)
    return centred * scale, scale


def norm_back(grad, hat, scale, gain):
    scaled = grad * gain
    return scale * (
        scaled
        - jnp.mean(scaled, -1, keepdims=True)
        - hat * jnp.mean(scaled * hat, -1, keepdims=True)
    )


def thirds(row):
    high = row.astype(BF16)
    rest = row - high.astype(F32)
    mid = rest.astype(BF16)
    low = (rest - mid.astype(F32)).astype(BF16)
    return high, mid, low


def project_kernel(tok, keep, row_table, col_table, gain, bias, weight, qb, vb, x0, a1t, qt, k, kt, v, vt):
    width = tok.shape[1]
    rows = tok.shape[0]
    patch = keep[...]
    tall = row_table.shape[0]
    wide = col_table.shape[0]
    row_hot = (lax.broadcasted_iota(jnp.int32, (rows, tall), 1) == patch // GRID_W).astype(F32)
    col_hot = (lax.broadcasted_iota(jnp.int32, (rows, wide), 1) == patch % GRID_W).astype(F32)
    pos_row = jnp.dot(row_hot, row_table[...], precision=lax.Precision.HIGHEST, preferred_element_type=F32)
    pos_col = jnp.dot(col_hot, col_table[...], precision=lax.Precision.HIGHEST, preferred_element_type=F32)
    x = tok[...].astype(F32) + jnp.concatenate([pos_row, pos_col], -1)
    x0[...] = x
    hat, _ = norm_parts(x)
    a = (hat * gain[...].astype(F32) + bias[...].astype(F32)).astype(BF16)
    a1t[...] = a.T
    q = (jnp.dot(a, weight[:, :width], preferred_element_type=F32) + qb[...].astype(F32)).astype(BF16)
    qt[...] = q.T
    kk = jnp.dot(a, weight[:, width : 2 * width], preferred_element_type=F32).astype(BF16)
    k[...] = kk
    kt[...] = kk.T
    vv = (jnp.dot(a, weight[:, 2 * width :], preferred_element_type=F32) + vb[...].astype(F32)).astype(BF16)
    v[...] = vv
    vt[...] = vv.T


def project(tok, keep, tables, gain, bias, weight, qb, vb, block=256):
    slots, width = tok.shape
    nat = pl.BlockSpec((block, width), lambda i: (i, 0))
    tra = pl.BlockSpec((width, block), lambda i: (0, i))
    sn = jax.ShapeDtypeStruct((slots, width), BF16)
    st = jax.ShapeDtypeStruct((width, slots), BF16)
    return pl.pallas_call(
        project_kernel,
        grid=(slots // block,),
        in_specs=[
            nat,
            pl.BlockSpec((block, 1), lambda i: (i, 0)),
            whole(tables[0].shape),
            whole(tables[1].shape),
            whole((1, width)),
            whole((1, width)),
            whole(weight.shape),
            whole((1, width)),
            whole((1, width)),
        ],
        out_specs=[nat, tra, tra, nat, tra, nat, tra],
        out_shape=[jax.ShapeDtypeStruct((slots, width), F32), st, st, sn, st, sn, st],
        compiler_params=pltpu.CompilerParams(vmem_limit_bytes=VMEM_BYTES),
        cost_estimate=pl.CostEstimate(flops=2 * slots * width * 3 * width, bytes_accessed=20 * slots * width, transcendentals=0),
        name="project",
    )(tok, keep[:, None], *tables, gain[None], bias[None], weight, qb[None], vb[None])


def augment_cols(block, extra, second):
    lane = lax.broadcasted_iota(jnp.int32, block.shape, 1)
    return jnp.where((lane >= HEAD_DIM) if second else (lane < HEAD_DIM), block, extra)


def augment_rows(block, extra, second):
    if second:
        return jnp.concatenate([extra, block[HEAD_DIM:]], 0)
    return jnp.concatenate([block[:HEAD_DIM], extra], 0)


def key_bias(count, slots):
    return jnp.where(lax.broadcasted_iota(jnp.int32, (slots, 1), 0) < count, 0.0, negative)


def attend_kernel(block, count, qt, k, vt, o, ot, lse):
    slots = k.shape[0]
    c = HEAD_DIM**-0.5 * LOG2E
    lane = lax.broadcasted_iota(jnp.int32, (slots, 2 * HEAD_DIM), 1)
    kb = key_bias(count[0, 0], slots)
    extra_col = jnp.where(lane % HEAD_DIM == 0, kb, 0.0).astype(BF16)
    sub = lax.broadcasted_iota(jnp.int32, (HEAD_DIM, block), 0)
    extra_row = jnp.where(sub == 0, 1.0, 0.0).astype(BF16)
    subv = lax.broadcasted_iota(jnp.int32, (16, slots), 0)
    ones = jnp.where(subv == 0, 1.0, 0.0).astype(BF16)
    for head in range(2):
        ka = augment_cols(k[...], extra_col, head == 1)
        va = jnp.concatenate([vt[head * HEAD_DIM : (head + 1) * HEAD_DIM, :], ones], 0)
        for i in range(slots // block):
            cols = slice(i * block, (i + 1) * block)
            qa = augment_rows(qt[:, cols], extra_row, head == 1)
            s = mm(ka, qa, 1, 0)
            top = jnp.max(s, 0, keepdims=True)
            p = jnp.exp2((s - top) * c).astype(BF16)
            r = mm(va, p, 1, 0)
            total = r[HEAD_DIM : HEAD_DIM + 1]
            mixed = (r[:HEAD_DIM] / total).astype(BF16)
            ot[head * HEAD_DIM : (head + 1) * HEAD_DIM, cols] = mixed
            lse[0, head : head + 1, cols] = top * HEAD_DIM**-0.5 + jnp.log(total)
    o[...] = ot[...].T


def attend(count, qt, k, vt, block=256):
    slots, width = k.shape
    pairs = width // (2 * HEAD_DIM)
    tra = pl.BlockSpec((2 * HEAD_DIM, slots), lambda j: (j, 0))
    nat = pl.BlockSpec((slots, 2 * HEAD_DIM), lambda j: (0, j))
    return pl.pallas_call(
        partial(attend_kernel, block),
        grid=(pairs,),
        in_specs=[pl.BlockSpec(memory_space=pltpu.SMEM), tra, nat, tra],
        out_specs=[nat, tra, pl.BlockSpec((1, 2, slots), lambda j: (j, 0, 0))],
        out_shape=[
            jax.ShapeDtypeStruct((slots, width), BF16),
            jax.ShapeDtypeStruct((width, slots), BF16),
            jax.ShapeDtypeStruct((pairs, 2, slots), F32),
        ],
        compiler_params=pltpu.CompilerParams(vmem_limit_bytes=VMEM_BYTES),
        cost_estimate=pl.CostEstimate(flops=16 * slots * slots * width, bytes_accessed=12 * slots * width, transcendentals=slots * slots * 12),
        name="attend",
    )(count, qt, k, vt)


SLOTS_AHEAD = 4
LANES = 128


class Sums:
    def __init__(self, fields, blk, rows, count, grads, recv, recv_blk, sems, free, free_blk):
        self.fields, self.blk, self.rows, self.count = fields, blk, rows, count
        self.bits = fields.bit_length() - 1
        self.grads, self.recv, self.recv_blk = grads, recv, recv_blk
        self.free, self.free_blk = free, free_blk
        self.send_rs, self.recv_rs, self.send_ag, self.recv_ag, self.blk_sems = sems
        self.f, self.z = lax.axis_index("fields"), lax.axis_index("blk")
        self.actions = 2 * self.bits + 3

    def weight(self, block, stage):
        even = 1 << stage
        odd = 1 << (stage if stage == 0 else self.bits - stage)
        odd_block = block % 2
        bit_even, bit_odd = (self.f // even) % 2, (self.f // odd) % 2
        bit = bit_even + odd_block * (bit_odd - bit_even)
        width = even + odd_block * (odd - even)
        return bit, self.f + width * (1 - 2 * bit)

    def start(self, block, stage):
        off = 0
        for k in range(stage):
            bit, _ = self.weight(block, k)
            off = off + bit * (self.rows >> (k + 1))
        return off

    def area(self, block, off, size):
        return self.grads.at[block, pl.ds(pl.multiple_of(off, 16), size)]

    def scatter_copy(self, block, stage):
        bit, partner = self.weight(block, stage)
        size = self.rows >> (stage + 1)
        off = self.start(block, stage) + (1 - bit) * size
        slot = block % SLOTS_AHEAD
        return pltpu.make_async_remote_copy(
            src_ref=self.area(block, off, size),
            dst_ref=self.recv[stage].at[slot],
            send_sem=self.send_rs.at[stage, slot],
            recv_sem=self.recv_rs.at[stage, slot],
            device_id=(partner, self.z),
            device_id_type=pl.DeviceIdType.MESH,
        )

    def gather_copy(self, block, stage):
        _, partner = self.weight(block, stage)
        part = self.area(block, self.start(block, stage + 1), self.rows >> (stage + 1))
        slot = block % SLOTS_AHEAD
        return pltpu.make_async_remote_copy(
            src_ref=part,
            dst_ref=part,
            send_sem=self.send_ag.at[stage, slot],
            recv_sem=self.recv_ag.at[stage, slot],
            device_id=(partner, self.z),
            device_id_type=pl.DeviceIdType.MESH,
        )

    def gather_wait(self, block, stage):
        self.gather_copy(block, stage).wait_send()
        bit, partner = self.weight(block, stage)
        size = self.rows >> (stage + 1)
        part = self.area(block, self.start(block, stage) + (1 - bit) * size, size)
        slot = block % SLOTS_AHEAD
        pltpu.make_async_remote_copy(
            src_ref=part,
            dst_ref=part,
            send_sem=self.send_ag.at[stage, slot],
            recv_sem=self.recv_ag.at[stage, slot],
            device_id=(partner, self.z),
            device_id_type=pl.DeviceIdType.MESH,
        ).wait_recv()

    def blk_copy(self, block, step, kind):
        size = self.rows // (self.fields * self.blk)
        to = (self.z + step) % self.blk
        base = self.start(block, self.bits)
        slot = block % SLOTS_AHEAD
        if kind == 0:
            src = self.area(block, base + to * size, size)
            dst = self.recv_blk.at[slot, step - 1]
        else:
            src = self.area(block, base + self.z * size, size)
            dst = src
        return pltpu.make_async_remote_copy(
            src_ref=src,
            dst_ref=dst,
            send_sem=self.blk_sems.at[kind, 0, step - 1, slot],
            recv_sem=self.blk_sems.at[kind, 1, step - 1, slot],
            device_id=(self.f, to),
            device_id_type=pl.DeviceIdType.MESH,
        )

    def blk_gather_wait(self, block, step):
        self.blk_copy(block, step, 1).wait_send()
        size = self.rows // (self.fields * self.blk)
        came = (self.z + self.blk - step) % self.blk
        slot = block % SLOTS_AHEAD
        part = self.area(block, self.start(block, self.bits) + came * size, size)
        pltpu.make_async_remote_copy(
            src_ref=part,
            dst_ref=part,
            send_sem=self.blk_sems.at[1, 0, step - 1, slot],
            recv_sem=self.blk_sems.at[1, 1, step - 1, slot],
            device_id=(self.f, came),
            device_id_type=pl.DeviceIdType.MESH,
        ).wait_recv()

    def add(self, block, off, size, take):
        chunk = size
        while chunk > 256 or size % chunk:
            chunk -= 16

        @pl.loop(0, size // chunk)
        def _(i):
            at = pl.ds(pl.multiple_of(off + i * chunk, 16), chunk)
            self.grads[block, at, :] = take(self.grads[block, at, :], pl.ds(pl.multiple_of(i * chunk, 16), chunk))

    def act(self, kind, block):
        bits = self.bits
        slot = block % SLOTS_AHEAD
        if 1 <= kind <= bits:
            stage = kind - 1
            self.scatter_copy(block, stage).wait()
            _, partner = self.weight(block, stage)
            pl.semaphore_signal(
                self.free.at[stage, block], 1, device_id=(partner, self.z), device_id_type=pl.DeviceIdType.MESH
            )
            got = self.recv[stage]
            self.add(block, self.start(block, stage + 1), self.rows >> (stage + 1), lambda a, at: a + got[slot, at, :])
        if kind < bits:
            self.scatter_copy(block, kind).start()
        elif kind == bits:
            for step in range(1, self.blk):
                self.blk_copy(block, step, 0).start()
        elif kind == bits + 1:
            for step in range(1, self.blk):
                self.blk_copy(block, step, 0).wait()
                pl.semaphore_signal(
                    self.free_blk.at[self.blk - step - 1, block],
                    1,
                    device_id=(self.f, (self.z + step) % self.blk),
                    device_id_type=pl.DeviceIdType.MESH,
                )
            size = self.rows // (self.fields * self.blk)

            def take(a, at):
                total = a.astype(F32)
                for step in range(1, self.blk):
                    total = total + self.recv_blk[slot, step - 1, at, :].astype(F32)
                return total.astype(BF16)

            self.add(block, self.start(block, bits) + self.z * size, size, take)
            for step in range(1, self.blk):
                pl.semaphore_wait(self.free_blk.at[step - 1, block], 1)
                self.blk_copy(block, step, 1).start()
        else:
            if kind == bits + 2:
                for step in range(1, self.blk):
                    self.blk_gather_wait(block, step)
            else:
                self.gather_wait(block, 2 * bits + 2 - kind + 1 - 1)
            stage = 2 * bits + 1 - kind
            if stage >= 0:
                pl.semaphore_wait(self.free.at[stage, block], 1)
                self.gather_copy(block, stage).start()

    def tick(self, tick, done):
        for kind in range(self.actions):
            block = tick - kind

            @pl.when((block >= 0) & (block < self.count))
            def _():
                self.act(kind, block)
                if kind == self.actions - 1:
                    done(block)


def mega_kernel(
    fields, blk, rows, ff_steps, pairs, tail,
    count, ot, x0, y, w_out, b_out, gain_two, bias_two, up, up_bias, down, down_bias,
    qt, k, kt, v, lse, a1t, wq, wk, wv, gain_one,
    out, din, up_out, down_out, qkv_out, out_out, vec_out,
    x1, a2, a2t, acc, dacc, out_s, dot_s, dt, din_s, grads, vec, recv_blk, vec_recv, vec_recv_blk,
    send_rs, recv_rs, send_ag, recv_ag, blk_sems, vec_sems, vec_blk_sems, move_sems, flush_sems, free, free_blk, *recv,
):
    step = pl.program_id(0)
    slots, width = x0.shape
    pair = 2 * HEAD_DIM
    chunk = slots // blk
    cols_of = width // LANES
    f, z = lax.axis_index("fields"), lax.axis_index("blk")
    bits = fields.bit_length() - 1
    ff = up.shape[1]
    heads_from, heads_to = ff_steps, ff_steps + 2 * pairs
    sums = Sums(
        fields, blk, rows, ff_steps + pairs, grads, recv, recv_blk, (send_rs, recv_rs, send_ag, recv_ag, blk_sems),
        free, free_blk,
    )
    VEC_G1, VEC_B1, VEC_Q, VEC_V, VEC_OUT, VEC_G2, VEC_B2, VEC_DOWN, VEC_UP = range(9)

    def put_vec(index, value):
        for i in range(cols_of):
            vec[index * cols_of + i : index * cols_of + i + 1, :] = value[:, i * LANES : (i + 1) * LANES]

    def moves(src, dst, kind):
        got = []
        for s in range(1, blk):
            to = (z + s) % blk
            got.append(
                pltpu.make_async_remote_copy(
                    src_ref=src.at[pl.ds(pl.multiple_of(to * chunk, 16), chunk)],
                    dst_ref=dst.at[z],
                    send_sem=move_sems.at[kind, 0, s],
                    recv_sem=move_sems.at[kind, 1, s],
                    device_id=(f, to),
                    device_id_type=pl.DeviceIdType.MESH,
                )
            )
        got.append(
            pltpu.make_async_copy(
                src.at[pl.ds(pl.multiple_of(z * chunk, 16), chunk)], dst.at[z], move_sems.at[kind, 0, 0]
            )
        )
        return got

    def moves_wait(src, dst, kind):
        got = moves(src, dst, kind)
        for c in got[:-1]:
            c.wait_send()
        for s in range(1, blk):
            came = (z + blk - s) % blk
            pltpu.make_async_remote_copy(
                src_ref=src.at[pl.ds(0, chunk)],
                dst_ref=dst.at[came],
                send_sem=move_sems.at[kind, 0, s],
                recv_sem=move_sems.at[kind, 1, s],
                device_id=(f, came),
                device_id_type=pl.DeviceIdType.MESH,
            ).wait_recv()
        got[-1].wait()

    @pl.when(step == 0)
    def _():
        barrier = pltpu.get_barrier_semaphore()
        for b in range(bits):
            bit = (f // (1 << b)) % 2
            pl.semaphore_signal(
                barrier, 1, device_id=(f + (1 << b) * (1 - 2 * bit), z), device_id_type=pl.DeviceIdType.MESH
            )
        for s in range(1, blk):
            pl.semaphore_signal(barrier, 1, device_id=(f, (z + s) % blk), device_id_type=pl.DeviceIdType.MESH)
        pl.semaphore_wait(barrier, bits + blk - 1)

        for r in range(blk):
            at = slice(r * chunk, (r + 1) * chunk)
            x = x0[at, :] + jnp.dot(ot[:, at].T, w_out[...], preferred_element_type=F32) + b_out[...].astype(F32)
            x1[at, :] = x
            hat, _ = norm_parts(x)
            a = (hat * gain_two[...].astype(F32) + bias_two[...].astype(F32)).astype(BF16)
            a2[at, :] = a
            a2t[:, at] = a.T
        acc[...] = jnp.zeros_like(acc)
        dacc[...] = jnp.zeros_like(dacc)

    def feed_copies(block):
        base = ff // LANES * width
        got = []
        for i in range(ff // LANES):
            at = pl.ds(pl.multiple_of(block * ff + i * LANES, LANES), LANES)
            got.append((grads.at[block, pl.ds(i * width, width)], up_out.at[:, at]))
        at = pl.ds(pl.multiple_of(block * ff, ff), ff)
        for i in range(cols_of):
            got.append((grads.at[block, pl.ds(base + i * ff, ff)], down_out.at[at, pl.ds(i * LANES, LANES)]))
        return [pltpu.make_async_copy(a, b, flush_sems.at[block, i]) for i, (a, b) in enumerate(got)]

    def proj_copies(block):
        got = []
        for i in range(4):
            at = pl.ds(pl.multiple_of((block - ff_steps + (i % 3) * pairs) * pair, pair), pair)
            got.append((grads.at[block, pl.ds(i * width, width)], (qkv_out if i < 3 else out_out).at[:, at]))
        return [pltpu.make_async_copy(a, b, flush_sems.at[block, i]) for i, (a, b) in enumerate(got)]

    def done(block):
        @pl.when(block < ff_steps)
        def _():
            for c in feed_copies(block):
                c.start()

        @pl.when(block >= ff_steps)
        def _():
            for c in proj_copies(block):
                c.start()

    def tick_of(s):
        return jnp.where(s < heads_to, (2 * s - 2) // 3, (2 * heads_to - 2) // 3 + s - heads_to)

    @pl.when((step >= 1) & (tick_of(step) != tick_of(step - 1)))
    def _():
        sums.tick(tick_of(step), done)

    @pl.when(step < heads_from)
    def _():
        h = jnp.dot(a2[...], up[...], preferred_element_type=F32) + up_bias[...].astype(F32)
        phi = 0.5 + 0.5 * lax.erf(h * (0.5**0.5))
        slope = phi + h * (jnp.exp2(h * h * (-0.5 * LOG2E)) * (2 * math.pi) ** -0.5)
        g = (h * phi).astype(BF16)
        dg = mm(y[...], down[...], 1, 1)
        dh = (dg * slope).astype(BF16)
        sum_up = jnp.sum(dh.astype(F32), 0, keepdims=True)
        for i in range(ff // LANES):
            vec[pl.ds(VEC_UP * cols_of + step * (ff // LANES) + i, 1), :] = sum_up[:, i * LANES : (i + 1) * LANES]
        acc[...] += jnp.dot(g, down[...], preferred_element_type=F32)
        dacc[...] += mm(dh, up[...], 1, 1)
        d_up = jnp.dot(a2t[...], dh, preferred_element_type=F32).astype(BF16)
        for i in range(ff // LANES):
            grads[step, i * width : (i + 1) * width, :] = d_up[:, i * LANES : (i + 1) * LANES]
        d_down = jnp.dot(g.T, y[...], preferred_element_type=F32).astype(BF16)
        base = ff // LANES * width
        for i in range(cols_of):
            grads[step, base + i * ff : base + (i + 1) * ff, :] = d_down[:, i * LANES : (i + 1) * LANES]
        if 2 * base < rows:
            grads[step, 2 * base :, :] = jnp.zeros((rows - 2 * base, LANES), BF16)

    @pl.when(step == heads_from - 1)
    def _():
        totals = [jnp.zeros((1, width), F32) for _ in range(4)]
        for r in range(blk):
            at = slice(r * chunk, (r + 1) * chunk)
            grad = dacc[at, :]
            yf = y[at, :].astype(F32)
            xs = x1[at, :]
            out_s[at, :] = (xs + acc[at, :] + down_bias[...].astype(F32)).astype(BF16)
            hat, sc = norm_parts(xs)
            dx = yf + norm_back(grad, hat, sc, gain_two[...].astype(F32))
            x1[at, :] = dx
            dz = dx.astype(BF16)
            a2[at, :] = dz
            dot_s[:, at] = mm(dz, w_out[...], 1, 1).astype(BF16).T
            for i, value in enumerate((grad * hat, grad, yf, dz.astype(F32))):
                totals[i] = totals[i] + jnp.sum(value, 0, keepdims=True)
        for c in moves(out_s, out, 0):
            c.start()
        for index, value in zip((VEC_G2, VEC_B2, VEC_DOWN, VEC_OUT), totals):
            put_vec(index, value)
        d_out = jnp.dot(ot[...], a2[...], preferred_element_type=F32).astype(BF16)
        for j in range(pairs):
            grads[ff_steps + j, 3 * width : 4 * width, :] = d_out[:, j * pair : (j + 1) * pair]
            if 4 * width < rows:
                grads[ff_steps + j, 4 * width :, :] = jnp.zeros((rows - 4 * width, LANES), BF16)
        dacc[...] = jnp.zeros_like(dacc)

    @pl.when((step >= heads_from) & (step < heads_to))
    def _():
        index = step - heads_from
        j, head = index // 2, index % 2
        c = HEAD_DIM**-0.5 * LOG2E
        scale = HEAD_DIM**-0.5
        block = 256
        lane = lax.broadcasted_iota(jnp.int32, (slots, pair), 1)
        kb = key_bias(count[0, 0], slots)
        mine = lane // HEAD_DIM == head
        lane = lane % HEAD_DIM
        ka = jnp.where(mine, k[...], jnp.where(lane == 0, kb, jnp.where(lane < 4, 1.0, 0.0)).astype(BF16))
        va = jnp.where(mine, v[...], jnp.where(lane < 3, 1.0, 0.0).astype(BF16))
        rows_of = pl.ds(pl.multiple_of(head * HEAD_DIM, HEAD_DIM), HEAD_DIM)
        rows_all = pl.ds(pl.multiple_of(index * HEAD_DIM, HEAD_DIM), HEAD_DIM)
        do_h = dot_s[rows_all, :]
        q_h = qt[rows_of, :]
        k_h = kt[rows_of, :]
        delta = jnp.sum(do_h.astype(F32) * ot[rows_all, :].astype(F32), 0, keepdims=True)
        l3 = [t.astype(F32) for t in thirds(lse[0, pl.ds(head, 1), :] * -(HEAD_DIM**0.5))]
        d3 = [t.astype(F32) for t in thirds(-delta)]
        zeros = jnp.zeros((HEAD_DIM - 4, slots), F32)
        one = jnp.ones((1, slots), F32)
        extra_q = jnp.concatenate([one, *l3, zeros], 0).astype(BF16)
        extra_d = jnp.concatenate([*d3, zeros, 0.0 * one], 0).astype(BF16)
        first = lax.broadcasted_iota(jnp.int32, (pair, slots), 0) // HEAD_DIM == head
        qa = jnp.where(first, jnp.concatenate([q_h, q_h], 0), jnp.concatenate([extra_q, extra_q], 0))
        da = jnp.where(first, jnp.concatenate([do_h, do_h], 0), jnp.concatenate([extra_d, extra_d], 0))
        for i in range(slots // block):
            at = slice(i * block, (i + 1) * block)
            s = mm(ka, qa[:, at], 1, 0)
            dp = mm(va, da[:, at], 1, 0)
            p = jnp.exp2(s * c)
            ds = (p * dp).astype(BF16)
            p = p.astype(BF16)
            dt[rows_of, at] = (mm(k_h, ds, 1, 0) * scale).astype(BF16)
            dv = mm(do_h[:, at], p, 1, 1)
            dk = mm(q_h[:, at], ds, 1, 1)
            if i == 0:
                dv_sum, dk_sum = dv, dk
            else:
                dv_sum, dk_sum = dv_sum + dv, dk_sum + dk
        dt[pl.ds(pl.multiple_of(pair + head * HEAD_DIM, HEAD_DIM), HEAD_DIM), :] = (dk_sum * scale).astype(BF16)
        dt[pl.ds(pl.multiple_of(2 * pair + head * HEAD_DIM, HEAD_DIM), HEAD_DIM), :] = dv_sum.astype(BF16)

        @pl.when(head == 1)
        def _():
            d = dt[...]
            part = mm(a1t[...], d, 1, 1).astype(BF16)
            for i in range(3):
                grads[ff_steps + j, i * width : (i + 1) * width, :] = part[:, i * pair : (i + 1) * pair]
            total = mm(jnp.ones((8, slots), BF16), d, 1, 1)
            vec[pl.ds(VEC_Q * cols_of + j, 1), :] = total[:1, :pair]
            vec[pl.ds(VEC_V * cols_of + j, 1), :] = total[:1, 2 * pair :]
            w = jnp.concatenate([wq[...], wk[...], wv[...]], 1)
            dacc[...] += mm(d.T, w, 1, 1)

    @pl.when(step == heads_to - 1)
    def _():
        totals = [jnp.zeros((1, width), F32) for _ in range(2)]
        for r in range(blk):
            at = slice(r * chunk, (r + 1) * chunk)
            grad = dacc[at, :]
            hat, sc = norm_parts(x0[at, :])
            dn = norm_back(grad, hat, sc, gain_one[...].astype(F32))
            din_s[at, :] = (x1[at, :] + dn).astype(BF16)
            for i, value in enumerate((grad * hat, grad)):
                totals[i] = totals[i] + jnp.sum(value, 0, keepdims=True)
        moves_wait(out_s, out, 0)
        for c in moves(din_s, din, 1):
            c.start()
        put_vec(VEC_G1, totals[0])
        put_vec(VEC_B1, totals[1])

    def vec_copy(b):
        bit = (f // (1 << b)) % 2
        return pltpu.make_async_remote_copy(
            src_ref=vec,
            dst_ref=vec_recv.at[b],
            send_sem=vec_sems.at[0, b],
            recv_sem=vec_sems.at[1, b],
            device_id=(f + (1 << b) * (1 - 2 * bit), z),
            device_id_type=pl.DeviceIdType.MESH,
        )

    def vec_blk_copy(s):
        return pltpu.make_async_remote_copy(
            src_ref=vec,
            dst_ref=vec_recv_blk.at[s - 1],
            send_sem=vec_blk_sems.at[0, s - 1],
            recv_sem=vec_blk_sems.at[1, s - 1],
            device_id=(f, (z + s) % blk),
            device_id_type=pl.DeviceIdType.MESH,
        )

    for b in range(bits + 2):

        @pl.when(step == heads_to + b)
        def _():
            if 1 <= b <= bits:
                vec_copy(b - 1).wait()
                vec[...] += vec_recv[b - 1]
            if b < bits:
                vec_copy(b).start()
            elif b == bits:
                for s in range(1, blk):
                    vec_blk_copy(s).start()
            else:
                for s in range(1, blk):
                    vec_blk_copy(s).wait()
                total = vec[...]
                for s in range(1, blk):
                    total = total + vec_recv_blk[s - 1]
                vec_out[...] = total

    @pl.when(step == heads_to + tail - 1)
    def _():
        moves_wait(din_s, din, 1)

        @pl.loop(0, ff_steps)
        def _(block):
            for c in feed_copies(block):
                c.wait()

        @pl.loop(ff_steps, ff_steps + pairs)
        def _(block):
            for c in proj_copies(block):
                c.wait()


def mega(mesh_shape, count, ot, x0, y, w_out, b_out, gain_two, bias_two, up, up_bias, down, down_bias,
         qt, k, kt, v, lse, a1t, w_qkv, gain_one, ff_block=256):
    fields, blk = mesh_shape
    slots, width = x0.shape
    pair = 2 * HEAD_DIM
    pairs = width // pair
    ff_steps = up.shape[1] // ff_block
    bits = fields.bit_length() - 1
    n = fields * blk
    rows = 2 * ff_block // LANES * width
    rows = -(-rows // (16 * n)) * 16 * n
    blocks = ff_steps + pairs
    last_tick = blocks - 1 + 2 * bits + 2
    heads_to = ff_steps + 2 * pairs
    tail = max(last_tick - (2 * heads_to - 2) // 3 + 1, bits + 2)
    vec_rows = (8 + up.shape[1] // width) * (width // LANES)
    chunk = slots // blk
    cols_of = width // LANES

    def ff_at(i):
        return jnp.minimum(i, ff_steps - 1)

    def pair_at(i):
        return jnp.clip((i - ff_steps) // 2, 0, pairs - 1)

    tra = pl.BlockSpec((pair, slots), lambda i: (pair_at(i), 0))
    nat = pl.BlockSpec((slots, pair), lambda i: (0, pair_at(i)))

    def cols(part):
        return pl.BlockSpec((width, pair), lambda i: (0, part * pairs + pair_at(i)))

    hbm = pl.BlockSpec(memory_space=pl.ANY)
    one = (1, width)
    dma = pltpu.SemaphoreType.DMA
    ahead = SLOTS_AHEAD
    flops = 12 * slots * width * up.shape[1] + 10 * slots * slots * width + 12 * slots * width * width
    return pl.pallas_call(
        partial(mega_kernel, fields, blk, rows, ff_steps, pairs, tail),
        grid=(heads_to + tail,),
        in_specs=[
            pl.BlockSpec(memory_space=pltpu.SMEM),
            whole((width, slots)),
            whole((slots, width)),
            whole((slots, width)),
            whole((width, width)),
            whole(one),
            whole(one),
            whole(one),
            pl.BlockSpec((width, ff_block), lambda i: (0, ff_at(i))),
            pl.BlockSpec((1, ff_block), lambda i: (0, ff_at(i))),
            pl.BlockSpec((ff_block, width), lambda i: (ff_at(i), 0)),
            whole(one),
            tra, nat, tra, nat,
            pl.BlockSpec((1, 2, slots), lambda i: (pair_at(i), 0, 0)),
            whole((width, slots)),
            cols(0), cols(1), cols(2),
            whole(one),
        ],
        out_specs=[hbm, hbm, hbm, hbm, hbm, hbm, whole((vec_rows, LANES))],
        out_shape=[
            jax.ShapeDtypeStruct((blk, chunk, width), BF16),
            jax.ShapeDtypeStruct((blk, chunk, width), BF16),
            jax.ShapeDtypeStruct((width, up.shape[1]), BF16),
            jax.ShapeDtypeStruct((up.shape[1], width), BF16),
            jax.ShapeDtypeStruct((width, 3 * width), BF16),
            jax.ShapeDtypeStruct((width, width), BF16),
            jax.ShapeDtypeStruct((vec_rows, LANES), F32),
        ],
        scratch_shapes=[
            pltpu.VMEM((slots, width), F32),
            pltpu.VMEM((slots, width), BF16),
            pltpu.VMEM((width, slots), BF16),
            pltpu.VMEM((slots, width), F32),
            pltpu.VMEM((slots, width), F32),
            pltpu.VMEM((slots, width), BF16),
            pltpu.VMEM((width, slots), BF16),
            pltpu.VMEM((3 * pair, slots), BF16),
            pltpu.VMEM((slots, width), BF16),
            pltpu.VMEM((blocks, rows, LANES), BF16),
            pltpu.VMEM((vec_rows, LANES), F32),
            pltpu.VMEM((ahead, blk - 1, rows // n, LANES), BF16),
            pltpu.VMEM((bits, vec_rows, LANES), F32),
            pltpu.VMEM((blk - 1, vec_rows, LANES), F32),
            dma((bits, ahead)),
            dma((bits, ahead)),
            dma((bits, ahead)),
            dma((bits, ahead)),
            dma((2, 2, blk - 1, ahead)),
            dma((2, bits)),
            dma((2, blk - 1)),
            dma((2, 2, blk)),
            dma((blocks, 2 * cols_of)),
            pltpu.SemaphoreType.REGULAR((bits, blocks)),
            pltpu.SemaphoreType.REGULAR((blk - 1, blocks)),
            *[pltpu.VMEM((ahead, rows >> (s + 1), LANES), BF16) for s in range(bits)],
        ],
        compiler_params=pltpu.CompilerParams(
            vmem_limit_bytes=67_000_000, collective_id=0, has_side_effects=True
        ),
        cost_estimate=pl.CostEstimate(flops=flops, bytes_accessed=60 * slots * width, transcendentals=0),
        name="mega",
    )(
        count, ot, x0, y, w_out, b_out[None], gain_two[None], bias_two[None], up, up_bias[None], down, down_bias[None],
        qt, k, kt, v, lse, a1t, w_qkv, w_qkv, w_qkv, gain_one[None],
    )


def tables(width):
    quarter = width // 4
    omega = 1.0 / 10000.0 ** (jnp.arange(quarter).astype(F32) / quarter)

    def table(length):
        ang = jnp.arange(length).astype(F32)[:, None] * omega
        return jnp.concatenate([jnp.sin(ang), jnp.cos(ang)], -1)

    return table(2048 // GRID_W), table(GRID_W)


def to_field(part):
    return lax.all_to_all(part, "blk", 0, 1, tiled=True)[0]


def per_device(
    mesh_shape, tokens, keep_index, counts, norm1_gain, norm1_bias, qkv_weight, query_bias, value_bias, out_weight,
    out_bias, norm2_gain, norm2_bias, up_weight, up_bias, down_weight, down_bias, cotangent,
):
    width = tokens.shape[2]
    count = lax.dynamic_slice(counts, (lax.axis_index("blk"),), (1,))[None]
    x0, a1t, qt, k, kt, v, vt = project(
        to_field(tokens), to_field(keep_index), tables(width), norm1_gain, norm1_bias, qkv_weight, query_bias, value_bias
    )
    y = to_field(cotangent)
    _, ot, lse = attend(count, qt, k, vt)
    output, input_grad, d_up, d_down, d_qkv, d_out, vecs = mega(
        mesh_shape, count, ot, x0, y, out_weight, out_bias, norm2_gain, norm2_bias, up_weight, up_bias, down_weight,
        down_bias, qt, k, kt, v, lse, a1t, qkv_weight, norm1_gain,
    )
    vec = vecs.reshape(-1, width)
    return (
        output,
        input_grad,
        vec[0],
        vec[1],
        d_qkv.astype(F32),
        vec[2],
        vec[3],
        d_out.astype(F32),
        vec[4],
        vec[5],
        vec[6],
        d_up.astype(F32),
        vec[8:].reshape(-1),
        d_down.astype(F32),
        vec[7],
    )


def solution(mesh):
    rows = P("fields", "blk", None)
    return jax.shard_map(
        partial(per_device, (mesh.shape["fields"], mesh.shape["blk"])),
        mesh=mesh,
        in_specs=(rows, P("fields", "blk"), P("fields"), *[P()] * 13, rows),
        out_specs=(rows, rows, *[P()] * 13),
        check_vma=False,
    )
```

```python
from functools import partial
import math
import jax
import jax.numpy as jnp
from jax import lax
from jax.experimental import pallas as pl
from jax.experimental.pallas import tpu as pltpu
from jax.sharding import PartitionSpec as P

HEAD_DIM = 64
GRID_W = 64
epsilon = 1e-06
negative = -1e30
VMEM_BYTES = 60 * 1024 * 1024
LOG2E = math.log2(math.e)
F32 = jnp.float32
BF16 = jnp.bfloat16


def mm(a, b, ca, cb):
    return lax.dot_general(a, b, (((ca,), (cb,)), ((), ())), preferred_element_type=F32)


def whole(shape):
    return pl.BlockSpec(shape, lambda *_: (0,) * len(shape), pipeline_mode=pl.Buffered(1))


def norm_parts(values):
    centre = jnp.mean(values, -1, keepdims=True)
    centred = values - centre
    spread = jnp.mean(centred * centred, -1, keepdims=True)
    scale = lax.rsqrt(spread + epsilon)
    return centred * scale, scale


def norm_back(grad, hat, scale, gain):
    scaled = grad * gain
    return scale * (
        scaled
        - jnp.mean(scaled, -1, keepdims=True)
        - hat * jnp.mean(scaled * hat, -1, keepdims=True)
    )


def thirds(row):
    high = row.astype(BF16)
    rest = row - high.astype(F32)
    mid = rest.astype(BF16)
    low = (rest - mid.astype(F32)).astype(BF16)
    return high, mid, low


def project_kernel(tok, keep, row_table, col_table, gain, bias, weight, qb, vb, x0, a1t, qt, k, kt, v, vt):
    width = tok.shape[1]
    rows = tok.shape[0]
    patch = keep[...]
    tall = row_table.shape[0]
    wide = col_table.shape[0]
    row_hot = (lax.broadcasted_iota(jnp.int32, (rows, tall), 1) == patch // GRID_W).astype(F32)
    col_hot = (lax.broadcasted_iota(jnp.int32, (rows, wide), 1) == patch % GRID_W).astype(F32)
    pos_row = jnp.dot(row_hot, row_table[...], precision=lax.Precision.HIGHEST, preferred_element_type=F32)
    pos_col = jnp.dot(col_hot, col_table[...], precision=lax.Precision.HIGHEST, preferred_element_type=F32)
    x = tok[...].astype(F32) + jnp.concatenate([pos_row, pos_col], -1)
    x0[...] = x
    hat, _ = norm_parts(x)
    a = (hat * gain[...].astype(F32) + bias[...].astype(F32)).astype(BF16)
    a1t[...] = a.T
    q = (jnp.dot(a, weight[:, :width], preferred_element_type=F32) + qb[...].astype(F32)).astype(BF16)
    qt[...] = q.T
    kk = jnp.dot(a, weight[:, width : 2 * width], preferred_element_type=F32).astype(BF16)
    k[...] = kk
    kt[...] = kk.T
    vv = (jnp.dot(a, weight[:, 2 * width :], preferred_element_type=F32) + vb[...].astype(F32)).astype(BF16)
    v[...] = vv
    vt[...] = vv.T


def project(tok, keep, tables, gain, bias, weight, qb, vb, block=256):
    slots, width = tok.shape
    nat = pl.BlockSpec((block, width), lambda i: (i, 0))
    tra = pl.BlockSpec((width, block), lambda i: (0, i))
    sn = jax.ShapeDtypeStruct((slots, width), BF16)
    st = jax.ShapeDtypeStruct((width, slots), BF16)
    return pl.pallas_call(
        project_kernel,
        grid=(slots // block,),
        in_specs=[
            nat,
            pl.BlockSpec((block, 1), lambda i: (i, 0)),
            whole(tables[0].shape),
            whole(tables[1].shape),
            whole((1, width)),
            whole((1, width)),
            whole(weight.shape),
            whole((1, width)),
            whole((1, width)),
        ],
        out_specs=[nat, tra, tra, nat, tra, nat, tra],
        out_shape=[jax.ShapeDtypeStruct((slots, width), F32), st, st, sn, st, sn, st],
        compiler_params=pltpu.CompilerParams(vmem_limit_bytes=VMEM_BYTES),
        cost_estimate=pl.CostEstimate(flops=2 * slots * width * 3 * width, bytes_accessed=20 * slots * width, transcendentals=0),
        name="project",
    )(tok, keep[:, None], *tables, gain[None], bias[None], weight, qb[None], vb[None])


def augment_cols(block, extra, second):
    lane = lax.broadcasted_iota(jnp.int32, block.shape, 1)
    return jnp.where((lane >= HEAD_DIM) if second else (lane < HEAD_DIM), block, extra)


def augment_rows(block, extra, second):
    if second:
        return jnp.concatenate([extra, block[HEAD_DIM:]], 0)
    return jnp.concatenate([block[:HEAD_DIM], extra], 0)


def key_bias(count, slots):
    return jnp.where(lax.broadcasted_iota(jnp.int32, (slots, 1), 0) < count, 0.0, negative)


def attend_kernel(block, count, qt, k, vt, o, ot, lse):
    slots = k.shape[0]
    c = HEAD_DIM**-0.5 * LOG2E
    lane = lax.broadcasted_iota(jnp.int32, (slots, 2 * HEAD_DIM), 1)
    kb = key_bias(count[0, 0], slots)
    extra_col = jnp.where(lane % HEAD_DIM == 0, kb, 0.0).astype(BF16)
    sub = lax.broadcasted_iota(jnp.int32, (HEAD_DIM, block), 0)
    extra_row = jnp.where(sub == 0, 1.0, 0.0).astype(BF16)
    subv = lax.broadcasted_iota(jnp.int32, (16, slots), 0)
    ones = jnp.where(subv == 0, 1.0, 0.0).astype(BF16)
    for head in range(2):
        ka = augment_cols(k[...], extra_col, head == 1)
        va = jnp.concatenate([vt[head * HEAD_DIM : (head + 1) * HEAD_DIM, :], ones], 0)
        for i in range(slots // block):
            cols = slice(i * block, (i + 1) * block)
            qa = augment_rows(qt[:, cols], extra_row, head == 1)
            s = mm(ka, qa, 1, 0)
            top = jnp.max(s, 0, keepdims=True)
            p = jnp.exp2((s - top) * c).astype(BF16)
            r = mm(va, p, 1, 0)
            total = r[HEAD_DIM : HEAD_DIM + 1]
            mixed = (r[:HEAD_DIM] / total).astype(BF16)
            ot[head * HEAD_DIM : (head + 1) * HEAD_DIM, cols] = mixed
            lse[0, head : head + 1, cols] = top * HEAD_DIM**-0.5 + jnp.log(total)
    o[...] = ot[...].T


def attend(count, qt, k, vt, block=256):
    slots, width = k.shape
    pairs = width // (2 * HEAD_DIM)
    tra = pl.BlockSpec((2 * HEAD_DIM, slots), lambda j: (j, 0))
    nat = pl.BlockSpec((slots, 2 * HEAD_DIM), lambda j: (0, j))
    return pl.pallas_call(
        partial(attend_kernel, block),
        grid=(pairs,),
        in_specs=[pl.BlockSpec(memory_space=pltpu.SMEM), tra, nat, tra],
        out_specs=[nat, tra, pl.BlockSpec((1, 2, slots), lambda j: (j, 0, 0))],
        out_shape=[
            jax.ShapeDtypeStruct((slots, width), BF16),
            jax.ShapeDtypeStruct((width, slots), BF16),
            jax.ShapeDtypeStruct((pairs, 2, slots), F32),
        ],
        compiler_params=pltpu.CompilerParams(vmem_limit_bytes=VMEM_BYTES),
        cost_estimate=pl.CostEstimate(flops=16 * slots * slots * width, bytes_accessed=12 * slots * width, transcendentals=slots * slots * 12),
        name="attend",
    )(count, qt, k, vt)


SLOTS_AHEAD = 8
LAG = 2
LANES = 128


class Sums:
    def __init__(self, fields, blk, rows, count, grads, recv, sems):
        self.rows, self.count = rows, count
        self.near, self.far = fields.bit_length() - 1, blk.bit_length() - 1
        self.bits = self.near + self.far
        self.grads, self.recv = grads, recv
        self.send_rs, self.recv_rs, self.send_ag, self.recv_ag = sems
        self.f, self.z = lax.axis_index("fields"), lax.axis_index("blk")
        self.actions = 2 * self.bits + 1
        self.own = [lax.rem(lax.div(self.f, 1 << k), 2) for k in range(self.near)]
        self.own += [lax.rem(lax.div(self.z, 1 << k), 2) for k in range(self.far)]

    def route(self, odd):
        keep, route = 0, []
        for stage in range(self.bits):
            bit = self.own[stage]
            if stage < self.near:
                other = stage if stage == 0 else self.near - stage
                bit = bit + odd * (self.own[other] - bit)
                width = (1 << stage) + odd * ((1 << other) - (1 << stage))
                partner = (self.f + width * (1 - 2 * bit), self.z)
            else:
                partner = (self.f, self.z + (1 << (stage - self.near)) * (1 - 2 * bit))
            size = self.rows >> (stage + 1)
            route.append((partner, keep + bit * size, keep + (1 - bit) * size))
            keep = keep + bit * size
        return route

    def copy(self, gather, block, slot, route, stage):
        partner, kept, sent = route[stage]
        part = pl.ds(pl.multiple_of(kept if gather else sent, 16), self.rows >> (stage + 1))
        send, recv = (self.send_ag, self.recv_ag) if gather else (self.send_rs, self.recv_rs)
        return pltpu.make_async_remote_copy(
            src_ref=self.grads.at[block, part],
            dst_ref=self.recv[stage].at[gather, slot],
            send_sem=send.at[stage, slot],
            recv_sem=recv.at[stage, slot],
            device_id=partner,
            device_id_type=pl.DeviceIdType.MESH,
        )

    def take(self, gather, block, slot, route, stage):
        size = self.rows >> (stage + 1)
        off = route[stage][2 if gather else 1]
        chunk = size
        while chunk > 384 or size % chunk:
            chunk -= 16
        came = self.recv[stage]

        @pl.loop(0, size // chunk)
        def _(i):
            at = pl.ds(pl.multiple_of(off + i * chunk, 16), chunk)
            got = came[gather, slot, pl.ds(pl.multiple_of(i * chunk, 16), chunk), :]
            self.grads[block, at, :] = got if gather else self.grads[block, at, :] + got

    def act(self, kind, block, slot, route):
        bits = self.bits
        if kind > 0:
            gather = int(kind > bits)
            stage = 2 * bits - kind if gather else kind - 1
            self.copy(gather, block, slot, route, stage).wait()
            self.take(gather, block, slot, route, stage)
        if kind < 2 * bits:
            gather = int(kind >= bits)
            self.copy(gather, block, slot, route, 2 * bits - 1 - kind if gather else kind).start()

    def tick(self, tick, done):
        assert LAG == 2
        odd = lax.rem(lax.div(tick, 2), 2)
        routes = self.route(odd), self.route(1 - odd)
        for kind in range(self.actions):
            block = tick - LAG * kind

            @pl.when((block >= 0) & (block < self.count))
            def _():
                self.act(kind, block, lax.rem(block, SLOTS_AHEAD), routes[kind % 2])
                if kind == self.actions - 1:
                    done(block)


def mega_kernel(
    fields, blk, rows, ff_steps, pairs, tail,
    count, ot, x0, y, w_out, b_out, gain_two, bias_two, up, up_bias, down, down_bias,
    qt, k, kt, v, lse, a1t, wq, wk, wv, gain_one,
    out, din, up_out, down_out, qkv_out, out_out, vec_out,
    x1, a2, a2t, acc, dacc, out_s, dot_s, dt, din_s, grads, vec, vec_recv, vec_recv_blk,
    send_rs, recv_rs, send_ag, recv_ag, vec_sems, vec_blk_sems, move_sems, piece_sems, flush_sems, *recv,
):
    step = pl.program_id(0)
    slots, width = x0.shape
    pair = 2 * HEAD_DIM
    chunk = slots // blk
    cols_of = width // LANES
    f, z = lax.axis_index("fields"), lax.axis_index("blk")
    bits = fields.bit_length() - 1
    ff = up.shape[1]
    heads_from, heads_to = ff_steps, ff_steps + 2 * pairs
    sums = Sums(
        fields, blk, rows, 2 * (ff_steps + pairs), grads, recv, (send_rs, recv_rs, send_ag, recv_ag)
    )
    VEC_G1, VEC_B1, VEC_Q, VEC_V, VEC_OUT, VEC_G2, VEC_B2, VEC_DOWN, VEC_UP = range(9)

    def put_vec(index, value):
        for i in range(cols_of):
            vec[index * cols_of + i : index * cols_of + i + 1, :] = value[:, i * LANES : (i + 1) * LANES]

    def local_copy(src, dst, sem):
        return pltpu.make_async_copy(src.at[pl.ds(pl.multiple_of(z * chunk, 16), chunk)], dst.at[z], sem)

    def send_part(src, dst, s, part, size, sems):
        to = lax.rem(z + s, blk)
        return pltpu.make_async_remote_copy(
            src_ref=src.at[pl.ds(pl.multiple_of(to * chunk + part * size, 16), size)],
            dst_ref=dst.at[z, pl.ds(pl.multiple_of(part * size, 16), size)],
            send_sem=sems[0],
            recv_sem=sems[1],
            device_id=(f, to),
            device_id_type=pl.DeviceIdType.MESH,
        )

    def part_came(src, dst, s, part, size, sems):
        came = lax.rem(z + blk - s, blk)
        return pltpu.make_async_remote_copy(
            src_ref=src.at[pl.ds(0, size)],
            dst_ref=dst.at[came, pl.ds(pl.multiple_of(part * size, 16), size)],
            send_sem=sems[0],
            recv_sem=sems[1],
            device_id=(f, came),
            device_id_type=pl.DeviceIdType.MESH,
        )

    pieces = 2 * pairs // (blk - 1)

    def piece(maker, i):
        sems = piece_sems.at[0, i], piece_sems.at[1, i]
        return maker(out_s, out, lax.rem(i, blk - 1) + 1, lax.div(i, blk - 1), chunk // pieces, sems)

    def din_part(maker, s):
        return maker(din_s, din, s, 0, chunk, (move_sems.at[0, s], move_sems.at[1, s]))

    @pl.when(step == 0)
    def _():
        barrier = pltpu.get_barrier_semaphore()
        for b in range(bits):
            bit = lax.rem(lax.div(f, 1 << b), 2)
            pl.semaphore_signal(
                barrier, 1, device_id=(f + (1 << b) * (1 - 2 * bit), z), device_id_type=pl.DeviceIdType.MESH
            )
        for s in range(1, blk):
            pl.semaphore_signal(barrier, 1, device_id=(f, lax.rem(z + s, blk)), device_id_type=pl.DeviceIdType.MESH)
        pl.semaphore_wait(barrier, bits + blk - 1)

        for r in range(blk):
            at = slice(r * chunk, (r + 1) * chunk)
            x = x0[at, :] + jnp.dot(ot[:, at].T, w_out[...], preferred_element_type=F32) + b_out[...].astype(F32)
            x1[at, :] = x
            hat, _ = norm_parts(x)
            a = (hat * gain_two[...].astype(F32) + bias_two[...].astype(F32)).astype(BF16)
            a2[at, :] = a
            a2t[:, at] = a.T
        acc[...] = jnp.zeros_like(acc)
        dacc[...] = jnp.zeros_like(dacc)

    def flush_copies(block, proj):
        half = lax.rem(block, 2)
        got = []
        if proj:
            j = lax.div(block, 2) - ff_steps
            for i in range(2):
                at = pl.ds(pl.multiple_of((j + i * pairs) * pair, pair), pair)
                got.append((grads.at[block, pl.ds(i * width, width)], qkv_out.at[:, at]))
            at = pl.ds(pl.multiple_of((j + 2 * pairs) * pair, pair), pair)
            more = [(grads.at[block, pl.ds(0, width)], qkv_out.at[:, at])]
            at = pl.ds(pl.multiple_of(j * pair, pair), pair)
            more.append((grads.at[block, pl.ds(width, width)], out_out.at[:, at]))
        else:
            step_of = lax.div(block, 2)
            for i in range(ff // LANES):
                at = pl.ds(pl.multiple_of(step_of * ff + i * LANES, LANES), LANES)
                got.append((grads.at[block, pl.ds(i * width, width)], up_out.at[:, at]))
            at = pl.ds(pl.multiple_of(step_of * ff, ff), ff)
            more = []
            for i in range(cols_of):
                more.append((grads.at[block, pl.ds(i * ff, ff)], down_out.at[at, pl.ds(i * LANES, LANES)]))
        pick = lambda some: [pltpu.make_async_copy(a, b, flush_sems.at[block, i]) for i, (a, b) in enumerate(some)]
        return half, pick, got, more

    def flush(block, act):
        for proj in (False, True):

            @pl.when((block >= 2 * ff_steps) if proj else (block < 2 * ff_steps))
            def _():
                half, pick, got, more = flush_copies(block, proj)

                @pl.when(half == 0)
                def _():
                    for c in pick(got):
                        act(c)

                @pl.when(half == 1)
                def _():
                    for c in pick(more):
                        act(c)

    def done(block):
        flush(block, lambda c: c.start())

    ff_ticks = ff_steps - 1 + ff_steps // 3
    index_of = step - ff_steps
    in_feed, in_heads = step < ff_steps, step < heads_to
    first = jnp.where(
        in_feed,
        step - 1 + lax.div(step, 3),
        jnp.where(in_heads, ff_ticks + index_of + lax.div(index_of, 2), ff_ticks + pairs + index_of),
    )
    twice = jnp.where(in_feed, lax.rem(step, 3) == 2, in_heads & (lax.rem(index_of, 2) == 1))

    @pl.when(step >= 1)
    def _():
        @pl.loop(0, jnp.where(twice, 2, 1))
        def _(i):
            sums.tick(first + i, done)

    @pl.when(step < heads_from)
    def _():
        h = jnp.dot(a2[...], up[...], preferred_element_type=F32) + up_bias[...].astype(F32)
        phi = 0.5 + 0.5 * lax.erf(h * (0.5**0.5))
        slope = phi + h * (jnp.exp2(h * h * (-0.5 * LOG2E)) * (2 * math.pi) ** -0.5)
        g = (h * phi).astype(BF16)
        dg = mm(y[...], down[...], 1, 1)
        dh = (dg * slope).astype(BF16)
        sum_up = jnp.sum(dh.astype(F32), 0, keepdims=True)
        for i in range(ff // LANES):
            vec[pl.ds(VEC_UP * cols_of + step * (ff // LANES) + i, 1), :] = sum_up[:, i * LANES : (i + 1) * LANES]
        acc[...] += jnp.dot(g, down[...], preferred_element_type=F32)
        dacc[...] += mm(dh, up[...], 1, 1)
        d_up = jnp.dot(a2t[...], dh, preferred_element_type=F32).astype(BF16)
        for i in range(ff // LANES):
            grads[2 * step, i * width : (i + 1) * width, :] = d_up[:, i * LANES : (i + 1) * LANES]
        d_down = jnp.dot(g.T, y[...], preferred_element_type=F32).astype(BF16)
        for i in range(cols_of):
            grads[2 * step + 1, i * ff : (i + 1) * ff, :] = d_down[:, i * LANES : (i + 1) * LANES]
        if 2 * width < rows:
            for i in range(2):
                grads[2 * step + i, 2 * width :, :] = jnp.zeros((rows - 2 * width, LANES), BF16)

    @pl.when(step == heads_from - 1)
    def _():
        totals = [jnp.zeros((1, width), F32) for _ in range(4)]
        for r in range(blk):
            at = slice(r * chunk, (r + 1) * chunk)
            grad = dacc[at, :]
            yf = y[at, :].astype(F32)
            xs = x1[at, :]
            out_s[at, :] = (xs + acc[at, :] + down_bias[...].astype(F32)).astype(BF16)
            hat, sc = norm_parts(xs)
            dx = yf + norm_back(grad, hat, sc, gain_two[...].astype(F32))
            x1[at, :] = dx
            dz = dx.astype(BF16)
            a2[at, :] = dz
            dot_s[:, at] = mm(dz, w_out[...], 1, 1).astype(BF16).T
            for i, value in enumerate((grad * hat, grad, yf, dz.astype(F32))):
                totals[i] = totals[i] + jnp.sum(value, 0, keepdims=True)
        local_copy(out_s, out, move_sems.at[0, 0]).start()
        for index, value in zip((VEC_G2, VEC_B2, VEC_DOWN, VEC_OUT), totals):
            put_vec(index, value)
        d_out = jnp.dot(ot[...], a2[...], preferred_element_type=F32).astype(BF16)
        for j in range(pairs):
            grads[2 * (ff_steps + j) + 1, width : 2 * width, :] = d_out[:, j * pair : (j + 1) * pair]
            if 2 * width < rows:
                for i in range(2):
                    grads[2 * (ff_steps + j) + i, 2 * width :, :] = jnp.zeros((rows - 2 * width, LANES), BF16)
        dacc[...] = jnp.zeros_like(dacc)

    @pl.when((step >= heads_from) & (step < heads_to))
    def _():
        index = step - heads_from
        j, head = lax.div(index, 2), lax.rem(index, 2)

        @pl.when(index < pieces * (blk - 1))
        def _():
            piece(send_part, index).start()

        c = HEAD_DIM**-0.5 * LOG2E
        scale = HEAD_DIM**-0.5
        block = 256
        lane = lax.broadcasted_iota(jnp.int32, (slots, pair), 1)
        kb = key_bias(count[0, 0], slots)
        mine = lane // HEAD_DIM == head
        lane = lane % HEAD_DIM
        ka = jnp.where(mine, k[...], jnp.where(lane == 0, kb, jnp.where(lane < 4, 1.0, 0.0)).astype(BF16))
        va = jnp.where(mine, v[...], jnp.where(lane < 3, 1.0, 0.0).astype(BF16))
        rows_of = pl.ds(pl.multiple_of(head * HEAD_DIM, HEAD_DIM), HEAD_DIM)
        rows_all = pl.ds(pl.multiple_of(index * HEAD_DIM, HEAD_DIM), HEAD_DIM)
        do_h = dot_s[rows_all, :]
        q_h = qt[rows_of, :]
        k_h = kt[rows_of, :]
        delta = jnp.sum(do_h.astype(F32) * ot[rows_all, :].astype(F32), 0, keepdims=True)
        l3 = [t.astype(F32) for t in thirds(lse[0, pl.ds(head, 1), :] * -(HEAD_DIM**0.5))]
        d3 = [t.astype(F32) for t in thirds(-delta)]
        zeros = jnp.zeros((HEAD_DIM - 4, slots), F32)
        one = jnp.ones((1, slots), F32)
        extra_q = jnp.concatenate([one, *l3, zeros], 0).astype(BF16)
        extra_d = jnp.concatenate([*d3, zeros, 0.0 * one], 0).astype(BF16)
        first = lax.broadcasted_iota(jnp.int32, (pair, slots), 0) // HEAD_DIM == head
        qa = jnp.where(first, jnp.concatenate([q_h, q_h], 0), jnp.concatenate([extra_q, extra_q], 0))
        da = jnp.where(first, jnp.concatenate([do_h, do_h], 0), jnp.concatenate([extra_d, extra_d], 0))
        for i in range(slots // block):
            at = slice(i * block, (i + 1) * block)
            s = mm(ka, qa[:, at], 1, 0)
            dp = mm(va, da[:, at], 1, 0)
            p = jnp.exp2(s * c)
            ds = (p * dp).astype(BF16)
            p = p.astype(BF16)
            dt[rows_of, at] = (mm(k_h, ds, 1, 0) * scale).astype(BF16)
            dv = mm(do_h[:, at], p, 1, 1)
            dk = mm(q_h[:, at], ds, 1, 1)
            if i == 0:
                dv_sum, dk_sum = dv, dk
            else:
                dv_sum, dk_sum = dv_sum + dv, dk_sum + dk
        dt[pl.ds(pl.multiple_of(pair + head * HEAD_DIM, HEAD_DIM), HEAD_DIM), :] = (dk_sum * scale).astype(BF16)
        dt[pl.ds(pl.multiple_of(2 * pair + head * HEAD_DIM, HEAD_DIM), HEAD_DIM), :] = dv_sum.astype(BF16)

        @pl.when(head == 1)
        def _():
            d = dt[...]
            part = mm(a1t[...], d, 1, 1).astype(BF16)
            for i in range(3):
                at = slice(i % 2 * width, (i % 2 + 1) * width)
                grads[2 * (ff_steps + j) + i // 2, at, :] = part[:, i * pair : (i + 1) * pair]
            total = mm(jnp.ones((8, slots), BF16), d, 1, 1)
            vec[pl.ds(VEC_Q * cols_of + j, 1), :] = total[:1, :pair]
            vec[pl.ds(VEC_V * cols_of + j, 1), :] = total[:1, 2 * pair :]
            w = jnp.concatenate([wq[...], wk[...], wv[...]], 1)
            dacc[...] += mm(d.T, w, 1, 1)

    @pl.when(step == heads_to)
    def _():
        totals = [jnp.zeros((1, width), F32) for _ in range(2)]
        for r in range(blk):
            at = slice(r * chunk, (r + 1) * chunk)
            grad = dacc[at, :]
            hat, sc = norm_parts(x0[at, :])
            dn = norm_back(grad, hat, sc, gain_one[...].astype(F32))
            din_s[at, :] = (x1[at, :] + dn).astype(BF16)
            for i, value in enumerate((grad * hat, grad)):
                totals[i] = totals[i] + jnp.sum(value, 0, keepdims=True)
        for s in range(1, blk):
            din_part(send_part, s).start()
        local_copy(din_s, din, move_sems.at[1, 0]).start()
        put_vec(VEC_G1, totals[0])
        put_vec(VEC_B1, totals[1])

    def vec_copy(b):
        bit = lax.rem(lax.div(f, 1 << b), 2)
        return pltpu.make_async_remote_copy(
            src_ref=vec,
            dst_ref=vec_recv.at[b],
            send_sem=vec_sems.at[0, b],
            recv_sem=vec_sems.at[1, b],
            device_id=(f + (1 << b) * (1 - 2 * bit), z),
            device_id_type=pl.DeviceIdType.MESH,
        )

    def vec_blk_copy(s):
        return pltpu.make_async_remote_copy(
            src_ref=vec,
            dst_ref=vec_recv_blk.at[s - 1],
            send_sem=vec_blk_sems.at[0, s - 1],
            recv_sem=vec_blk_sems.at[1, s - 1],
            device_id=(f, lax.rem(z + s, blk)),
            device_id_type=pl.DeviceIdType.MESH,
        )

    @pl.when(step == heads_to)
    def _():
        @pl.loop(1, tail)
        def _(i):
            sums.tick(first + i, done)

            for b in range(bits + 2):

                @pl.when(i == 1 + 2 * b)
                def _():
                    if 1 <= b <= bits:
                        vec_copy(b - 1).wait()
                        vec[...] += vec_recv[b - 1]
                    if b < bits:
                        vec_copy(b).start()
                    elif b == bits:
                        for s in range(1, blk):
                            vec_blk_copy(s).start()
                    else:
                        for s in range(1, blk):
                            vec_blk_copy(s).wait()
                        total = vec[...]
                        for s in range(1, blk):
                            total = total + vec_recv_blk[s - 1]
                        vec_out[...] = total

        @pl.loop(0, pieces * (blk - 1))
        def _(i):
            piece(send_part, i).wait_send()
            piece(part_came, i).wait_recv()

        for s in range(1, blk):
            din_part(send_part, s).wait_send()
            din_part(part_came, s).wait_recv()
        local_copy(out_s, out, move_sems.at[0, 0]).wait()
        local_copy(din_s, din, move_sems.at[1, 0]).wait()

        @pl.loop(0, sums.count)
        def _(block):
            flush(block, lambda c: c.wait())


def mega(mesh_shape, count, ot, x0, y, w_out, b_out, gain_two, bias_two, up, up_bias, down, down_bias,
         qt, k, kt, v, lse, a1t, w_qkv, gain_one, ff_block=256):
    fields, blk = mesh_shape
    slots, width = x0.shape
    pair = 2 * HEAD_DIM
    pairs = width // pair
    ff_steps = up.shape[1] // ff_block
    bits = fields.bit_length() - 1
    n = fields * blk
    assert ff_block == 2 * LANES
    rows = -(-2 * width // (16 * n)) * 16 * n
    blocks = 2 * (ff_steps + pairs)
    levels = n.bit_length() - 1
    last_tick = blocks - 1 + LAG * 2 * levels
    heads_to = ff_steps + 2 * pairs
    tail = max(last_tick - (ff_steps - 1 + ff_steps // 3 + 3 * pairs) + 1, 2 * bits + 4)
    vec_rows = (8 + up.shape[1] // width) * (width // LANES)
    chunk = slots // blk
    cols_of = width // LANES

    def ff_at(i):
        return jnp.minimum(i, ff_steps - 1)

    def pair_at(i):
        return jnp.clip((i - ff_steps) // 2, 0, pairs - 1)

    tra = pl.BlockSpec((pair, slots), lambda i: (pair_at(i), 0))
    nat = pl.BlockSpec((slots, pair), lambda i: (0, pair_at(i)))

    def cols(part):
        return pl.BlockSpec((width, pair), lambda i: (0, part * pairs + pair_at(i)))

    hbm = pl.BlockSpec(memory_space=pl.ANY)
    one = (1, width)
    dma = pltpu.SemaphoreType.DMA
    ahead = SLOTS_AHEAD
    flops = 12 * slots * width * up.shape[1] + 10 * slots * slots * width + 12 * slots * width * width
    return pl.pallas_call(
        partial(mega_kernel, fields, blk, rows, ff_steps, pairs, tail),
        grid=(heads_to + 1,),
        in_specs=[
            pl.BlockSpec(memory_space=pltpu.SMEM),
            whole((width, slots)),
            whole((slots, width)),
            whole((slots, width)),
            whole((width, width)),
            whole(one),
            whole(one),
            whole(one),
            pl.BlockSpec((width, ff_block), lambda i: (0, ff_at(i))),
            pl.BlockSpec((1, ff_block), lambda i: (0, ff_at(i))),
            pl.BlockSpec((ff_block, width), lambda i: (ff_at(i), 0)),
            whole(one),
            tra, nat, tra, nat,
            pl.BlockSpec((1, 2, slots), lambda i: (pair_at(i), 0, 0)),
            whole((width, slots)),
            cols(0), cols(1), cols(2),
            whole(one),
        ],
        out_specs=[hbm, hbm, hbm, hbm, hbm, hbm, whole((vec_rows, LANES))],
        out_shape=[
            jax.ShapeDtypeStruct((blk, chunk, width), BF16),
            jax.ShapeDtypeStruct((blk, chunk, width), BF16),
            jax.ShapeDtypeStruct((width, up.shape[1]), BF16),
            jax.ShapeDtypeStruct((up.shape[1], width), BF16),
            jax.ShapeDtypeStruct((width, 3 * width), BF16),
            jax.ShapeDtypeStruct((width, width), BF16),
            jax.ShapeDtypeStruct((vec_rows, LANES), F32),
        ],
        scratch_shapes=[
            pltpu.VMEM((slots, width), F32),
            pltpu.VMEM((slots, width), BF16),
            pltpu.VMEM((width, slots), BF16),
            pltpu.VMEM((slots, width), F32),
            pltpu.VMEM((slots, width), F32),
            pltpu.VMEM((slots, width), BF16),
            pltpu.VMEM((width, slots), BF16),
            pltpu.VMEM((3 * pair, slots), BF16),
            pltpu.VMEM((slots, width), BF16),
            pltpu.VMEM((blocks, rows, LANES), BF16),
            pltpu.VMEM((vec_rows, LANES), F32),
            pltpu.VMEM((bits, vec_rows, LANES), F32),
            pltpu.VMEM((blk - 1, vec_rows, LANES), F32),
            dma((levels, ahead)),
            dma((levels, ahead)),
            dma((levels, ahead)),
            dma((levels, ahead)),
            dma((2, bits)),
            dma((2, blk - 1)),
            dma((2, blk)),
            dma((2, 2 * pairs)),
            dma((blocks, cols_of)),
            *[pltpu.VMEM((2, ahead, rows >> (s + 1), LANES), BF16) for s in range(levels)],
        ],
        compiler_params=pltpu.CompilerParams(
            vmem_limit_bytes=67_000_000, collective_id=0, has_side_effects=True
        ),
        cost_estimate=pl.CostEstimate(flops=flops, bytes_accessed=60 * slots * width, transcendentals=0),
        name="mega",
    )(
        count, ot, x0, y, w_out, b_out[None], gain_two[None], bias_two[None], up, up_bias[None], down, down_bias[None],
        qt, k, kt, v, lse, a1t, w_qkv, w_qkv, w_qkv, gain_one[None],
    )


def tables(width):
    quarter = width // 4
    omega = 1.0 / 10000.0 ** (jnp.arange(quarter).astype(F32) / quarter)

    def table(length):
        ang = jnp.arange(length).astype(F32)[:, None] * omega
        return jnp.concatenate([jnp.sin(ang), jnp.cos(ang)], -1)

    return table(2048 // GRID_W), table(GRID_W)


def to_field(part):
    return lax.all_to_all(part, "blk", 0, 1, tiled=True)[0]


def per_device(
    mesh_shape, tokens, keep_index, counts, norm1_gain, norm1_bias, qkv_weight, query_bias, value_bias, out_weight,
    out_bias, norm2_gain, norm2_bias, up_weight, up_bias, down_weight, down_bias, cotangent,
):
    width = tokens.shape[2]
    count = lax.dynamic_slice(counts, (lax.axis_index("blk"),), (1,))[None]
    x0, a1t, qt, k, kt, v, vt = project(
        to_field(tokens), to_field(keep_index), tables(width), norm1_gain, norm1_bias, qkv_weight, query_bias, value_bias
    )
    y = to_field(cotangent)
    _, ot, lse = attend(count, qt, k, vt)
    output, input_grad, d_up, d_down, d_qkv, d_out, vecs = mega(
        mesh_shape, count, ot, x0, y, out_weight, out_bias, norm2_gain, norm2_bias, up_weight, up_bias, down_weight,
        down_bias, qt, k, kt, v, lse, a1t, qkv_weight, norm1_gain,
    )
    vec = vecs.reshape(-1, width)
    return (
        output,
        input_grad,
        vec[0],
        vec[1],
        d_qkv.astype(F32),
        vec[2],
        vec[3],
        d_out.astype(F32),
        vec[4],
        vec[5],
        vec[6],
        d_up.astype(F32),
        vec[8:].reshape(-1),
        d_down.astype(F32),
        vec[7],
    )


def solution(mesh):
    rows = P("fields", "blk", None)
    return jax.shard_map(
        partial(per_device, (mesh.shape["fields"], mesh.shape["blk"])),
        mesh=mesh,
        in_specs=(rows, P("fields", "blk"), P("fields"), *[P()] * 13, rows),
        out_specs=(rows, rows, *[P()] * 13),
        check_vma=False,
    )
```

```python
from functools import partial
import math
import jax
import jax.numpy as jnp
import numpy as np
from jax import lax
from jax.experimental import pallas as pl
from jax.experimental.pallas import tpu as pltpu
from jax.sharding import PartitionSpec as P

HEAD_DIM = 64
GRID_W = 64
PATCHES = 2048
epsilon = 1e-06
negative = -1e30
VMEM_BYTES = 60 * 1024 * 1024
LOG2E = math.log2(math.e)
F32 = jnp.float32
BF16 = jnp.bfloat16


def mm(a, b, ca, cb):
    return lax.dot_general(a, b, (((ca,), (cb,)), ((), ())), preferred_element_type=F32)


def row(ref):
    return ref[...].astype(F32)[None]


def whole(shape):
    return pl.BlockSpec(shape, lambda *_: (0,) * len(shape), pipeline_mode=pl.Buffered(1))


def norm_parts(values):
    centre = jnp.mean(values, -1, keepdims=True)
    centred = values - centre
    spread = jnp.mean(centred * centred, -1, keepdims=True)
    scale = lax.rsqrt(spread + epsilon)
    return centred * scale, scale


def norm_back(grad, hat, scale, gain):
    scaled = grad * gain
    return scale * (
        scaled
        - jnp.mean(scaled, -1, keepdims=True)
        - hat * jnp.mean(scaled * hat, -1, keepdims=True)
    )


def thirds(row):
    high = row.astype(BF16)
    rest = row - high.astype(F32)
    mid = rest.astype(BF16)
    low = (rest - mid.astype(F32)).astype(BF16)
    return high, mid, low


def tables(width):
    quarter = width // 4
    omega = 1.0 / 10000.0 ** (np.arange(quarter) / quarter)

    def table(length):
        ang = np.arange(length)[:, None] * omega
        return jnp.asarray(np.concatenate([np.sin(ang), np.cos(ang)], -1), F32)

    return table(PATCHES // GRID_W), table(GRID_W)


def place_kernel(tok, keep, row_table, col_table, x0):
    slots = tok.shape[1]
    patch = keep[pl.ds(pl.program_id(0), 1), :]
    parts = []
    for table, of in ((row_table, lax.div(patch, GRID_W)), (col_table, lax.rem(patch, GRID_W))):
        hot = (lax.broadcasted_iota(jnp.int32, (table.shape[0], slots), 0) == of).astype(F32)
        parts.append(jnp.dot(hot.T, table[...], precision=lax.Precision.HIGHEST, preferred_element_type=F32))
    x0[0] = (tok[0].astype(F32) + jnp.concatenate(parts, -1)).astype(BF16)


def place(tokens, keep):
    fields, slots, width = tokens.shape
    row_table, col_table = tables(width)
    block = pl.BlockSpec((1, slots, width), lambda i: (i, 0, 0))
    return pl.pallas_call(
        place_kernel,
        grid=(fields,),
        in_specs=[block, whole((fields, slots)), whole(row_table.shape), whole(col_table.shape)],
        out_specs=block,
        out_shape=jax.ShapeDtypeStruct(tokens.shape, BF16),
        name="place",
    )(tokens, keep, row_table, col_table)


def project_kernel(x0, gain, bias, weight, qb, vb, a1t, qt, k, kt, v, vt):
    width = x0.shape[1]
    hat, _ = norm_parts(x0[...].astype(F32))
    a = (hat * row(gain) + row(bias)).astype(BF16)
    a1t[...] = a.T
    q = (jnp.dot(a, weight[:, :width], preferred_element_type=F32) + row(qb)).astype(BF16)
    qt[...] = q.T
    kk = jnp.dot(a, weight[:, width : 2 * width], preferred_element_type=F32).astype(BF16)
    k[...] = kk
    kt[...] = kk.T
    vv = (jnp.dot(a, weight[:, 2 * width :], preferred_element_type=F32) + row(vb)).astype(BF16)
    v[...] = vv
    vt[...] = vv.T


def project(x0, gain, bias, weight, qb, vb, block=256):
    slots, width = x0.shape
    nat = pl.BlockSpec((block, width), lambda i: (i, 0))
    tra = pl.BlockSpec((width, block), lambda i: (0, i))
    sn = jax.ShapeDtypeStruct((slots, width), BF16)
    st = jax.ShapeDtypeStruct((width, slots), BF16)
    one = whole((width,))
    return pl.pallas_call(
        project_kernel,
        grid=(slots // block,),
        in_specs=[nat, one, one, whole(weight.shape), one, one],
        out_specs=[tra, tra, nat, tra, nat, tra],
        out_shape=[st, st, sn, st, sn, st],
        compiler_params=pltpu.CompilerParams(vmem_limit_bytes=VMEM_BYTES),
        cost_estimate=pl.CostEstimate(flops=2 * slots * width * 3 * width, bytes_accessed=20 * slots * width, transcendentals=0),
        name="project",
    )(x0, gain, bias, weight, qb, vb)


def augment_cols(block, extra, second):
    lane = lax.broadcasted_iota(jnp.int32, block.shape, 1)
    return jnp.where((lane >= HEAD_DIM) if second else (lane < HEAD_DIM), block, extra)


def augment_rows(block, extra, second):
    if second:
        return jnp.concatenate([extra, block[HEAD_DIM:]], 0)
    return jnp.concatenate([block[:HEAD_DIM], extra], 0)


def key_bias(count, slots):
    return jnp.where(lax.broadcasted_iota(jnp.int32, (slots, 1), 0) < count, 0.0, negative)


def attend_kernel(block, count, qt, k, vt, o, ot, lse):
    slots = k.shape[0]
    c = HEAD_DIM**-0.5 * LOG2E
    lane = lax.broadcasted_iota(jnp.int32, (slots, 2 * HEAD_DIM), 1)
    kb = key_bias(count[lax.axis_index("blk")], slots)
    extra_col = jnp.where(lane % HEAD_DIM == 0, kb, 0.0).astype(BF16)
    sub = lax.broadcasted_iota(jnp.int32, (HEAD_DIM, block), 0)
    extra_row = jnp.where(sub == 0, 1.0, 0.0).astype(BF16)
    subv = lax.broadcasted_iota(jnp.int32, (16, slots), 0)
    ones = jnp.where(subv == 0, 1.0, 0.0).astype(BF16)
    for head in range(2):
        ka = augment_cols(k[...], extra_col, head == 1)
        va = jnp.concatenate([vt[head * HEAD_DIM : (head + 1) * HEAD_DIM, :], ones], 0)
        for i in range(slots // block):
            cols = slice(i * block, (i + 1) * block)
            qa = augment_rows(qt[:, cols], extra_row, head == 1)
            s = mm(ka, qa, 1, 0)
            top = jnp.max(s, 0, keepdims=True)
            p = jnp.exp2((s - top) * c).astype(BF16)
            r = mm(va, p, 1, 0)
            total = r[HEAD_DIM : HEAD_DIM + 1]
            mixed = (r[:HEAD_DIM] / total).astype(BF16)
            ot[head * HEAD_DIM : (head + 1) * HEAD_DIM, cols] = mixed
            lse[0, head : head + 1, cols] = top * HEAD_DIM**-0.5 + jnp.log(total)
    o[...] = ot[...].T


def attend(count, qt, k, vt, block=256):
    slots, width = k.shape
    pairs = width // (2 * HEAD_DIM)
    tra = pl.BlockSpec((2 * HEAD_DIM, slots), lambda j: (j, 0))
    nat = pl.BlockSpec((slots, 2 * HEAD_DIM), lambda j: (0, j))
    return pl.pallas_call(
        partial(attend_kernel, block),
        grid=(pairs,),
        in_specs=[pl.BlockSpec(memory_space=pltpu.SMEM), tra, nat, tra],
        out_specs=[nat, tra, pl.BlockSpec((1, 2, slots), lambda j: (j, 0, 0))],
        out_shape=[
            jax.ShapeDtypeStruct((slots, width), BF16),
            jax.ShapeDtypeStruct((width, slots), BF16),
            jax.ShapeDtypeStruct((pairs, 2, slots), F32),
        ],
        compiler_params=pltpu.CompilerParams(vmem_limit_bytes=VMEM_BYTES),
        cost_estimate=pl.CostEstimate(flops=16 * slots * slots * width, bytes_accessed=12 * slots * width, transcendentals=slots * slots * 12),
        name="attend",
    )(count, qt, k, vt)


SLOTS_AHEAD = 8
LANES = 128
LAG_CORE, LAG_XY, LAG_Z = 2, 3, 3
DIN_EVERY = 2


def offsets(near, far):
    lags = [LAG_CORE] + [LAG_XY] * (near - 1) + [LAG_Z] * far
    ticks = [0]
    for lag in lags + lags[::-1]:
        ticks.append(ticks[-1] + lag)
    return ticks


class Sums:
    def __init__(self, fields, blk, rows, early, count, grads, recv, sems):
        self.rows, self.early, self.count = rows, early, count
        self.near, self.far = fields.bit_length() - 1, blk.bit_length() - 1
        self.bits = self.near + self.far
        self.grads, self.recv = grads, recv
        self.send_rs, self.recv_rs, self.send_ag, self.recv_ag = sems
        self.f, self.z = lax.axis_index("fields"), lax.axis_index("blk")
        self.actions = 2 * self.bits + 1
        self.own = [lax.rem(lax.div(self.f, 1 << k), 2) for k in range(self.near)]
        self.own += [lax.rem(lax.div(self.z, 1 << k), 2) for k in range(self.far)]

    def route(self, odd):
        keep, route = 0, []
        for stage in range(self.bits):
            bit = self.own[stage]
            if stage < self.near:
                other = stage if stage == 0 else self.near - stage
                bit = bit + odd * (self.own[other] - bit)
                width = (1 << stage) + odd * ((1 << other) - (1 << stage))
                partner = (self.f + width * (1 - 2 * bit), self.z)
            else:
                partner = (self.f, self.z + (1 << (stage - self.near)) * (1 - 2 * bit))
            size = self.rows >> (stage + 1)
            route.append((partner, keep + bit * size, keep + (1 - bit) * size))
            keep = keep + bit * size
        return route

    def copy(self, gather, block, slot, route, stage):
        partner, kept, sent = route[stage]
        part = pl.ds(pl.multiple_of(kept if gather else sent, 16), self.rows >> (stage + 1))
        send, recv = (self.send_ag, self.recv_ag) if gather else (self.send_rs, self.recv_rs)
        return pltpu.make_async_remote_copy(
            src_ref=self.grads.at[block, part],
            dst_ref=self.recv[stage].at[gather, slot],
            send_sem=send.at[stage, slot],
            recv_sem=recv.at[stage, slot],
            device_id=partner,
            device_id_type=pl.DeviceIdType.MESH,
        )

    def take(self, gather, block, slot, route, stage):
        size = self.rows >> (stage + 1)
        off = route[stage][2 if gather else 1]
        chunk = size
        while chunk > 384 or size % chunk:
            chunk -= 16
        came = self.recv[stage]

        @pl.loop(0, size // chunk)
        def _(i):
            at = pl.ds(pl.multiple_of(off + i * chunk, 16), chunk)
            got = came[gather, slot, pl.ds(pl.multiple_of(i * chunk, 16), chunk), :]
            self.grads[block, at, :] = got if gather else self.grads[block, at, :] + got

    def act(self, kind, block, slot, route):
        bits = self.bits
        if kind > 0:
            gather = int(kind > bits)
            stage = 2 * bits - kind if gather else kind - 1
            self.copy(gather, block, slot, route, stage).wait()
            self.take(gather, block, slot, route, stage)
        if kind < 2 * bits:
            gather = int(kind >= bits)
            self.copy(gather, block, slot, route, 2 * bits - 1 - kind if gather else kind).start()

    def tick(self, tick, done):
        routes = {}
        for odd_offset in (0, 1):
            turn = lax.rem(lax.div(tick + odd_offset, 2), 2)
            routes[odd_offset] = self.route(turn), self.route(1 - turn)
        for kind, offset in enumerate(offsets(self.near, self.far)):
            entry = tick - offset
            late = entry - self.early - 2
            block = jnp.where(late >= 0, self.early + lax.div(late, 2), entry)
            runs = jnp.where(late >= 0, (lax.rem(late, 2) == 0) & (block < self.count), (entry >= 0) & (entry < self.early))
            route = routes[offset % 2][(offset + 1) // 2 % 2]

            @pl.when(runs)
            def _():
                self.act(kind, block, lax.rem(block, SLOTS_AHEAD), route)
                if kind == self.actions - 1:
                    done(block)


def mega_kernel(
    fields, blk, rows, ff_steps, pairs, tail,
    count, ot, x0, y, w_out, b_out, gain_two, bias_two, up, up_bias, down, down_bias,
    qt, k, kt, v, lse, a1t, wq, wk, wv, gain_one,
    out, din, up_out, down_out, qkv_out, out_out, vec_out,
    x1, a2, a2t, acc, dacc, out_s, dot_s, dt, din_s, dvk, grads, vec, vec_recv, vec_recv_blk,
    send_rs, recv_rs, send_ag, recv_ag, vec_sems, vec_blk_sems, move_sems, piece_sems, flush_sems, *recv,
):
    step = pl.program_id(0)
    slots, width = x0.shape
    pair = 2 * HEAD_DIM
    chunk = slots // blk
    cols_of = width // LANES
    f, z = lax.axis_index("fields"), lax.axis_index("blk")
    bits = fields.bit_length() - 1
    ff = up.shape[1]
    heads_from, heads_to = ff_steps, ff_steps + 2 * pairs
    sums = Sums(
        fields, blk, rows, 2 * ff_steps, 2 * (ff_steps + pairs), grads, recv, (send_rs, recv_rs, send_ag, recv_ag)
    )
    VEC_G1, VEC_B1, VEC_Q, VEC_V, VEC_OUT, VEC_G2, VEC_B2, VEC_DOWN, VEC_UP = range(9)

    def put_vec(index, value):
        for i in range(cols_of):
            vec[index * cols_of + i : index * cols_of + i + 1, :] = value[:, i * LANES : (i + 1) * LANES]

    def local_copy(src, dst, sem):
        return pltpu.make_async_copy(src.at[pl.ds(pl.multiple_of(z * chunk, 16), chunk)], dst.at[z], sem)

    def send_part(src, dst, s, part, size, sems):
        to = lax.rem(z + s, blk)
        return pltpu.make_async_remote_copy(
            src_ref=src.at[pl.ds(pl.multiple_of(to * chunk + part * size, 16), size)],
            dst_ref=dst.at[z, pl.ds(pl.multiple_of(part * size, 16), size)],
            send_sem=sems[0],
            recv_sem=sems[1],
            device_id=(f, to),
            device_id_type=pl.DeviceIdType.MESH,
        )

    def part_came(src, dst, s, part, size, sems):
        came = lax.rem(z + blk - s, blk)
        return pltpu.make_async_remote_copy(
            src_ref=src.at[pl.ds(0, size)],
            dst_ref=dst.at[came, pl.ds(pl.multiple_of(part * size, 16), size)],
            send_sem=sems[0],
            recv_sem=sems[1],
            device_id=(f, came),
            device_id_type=pl.DeviceIdType.MESH,
        )

    pieces = 2 * pairs // (blk - 1)

    def piece(maker, i, kind):
        sems = piece_sems.at[kind, 0, i], piece_sems.at[kind, 1, i]
        src, dst = ((out_s, out), (din_s, din))[kind]
        return maker(src, dst, blk - 1 - lax.rem(i, blk - 1), lax.div(i, blk - 1), chunk // pieces, sems)

    @pl.when(step == 0)
    def _():
        barrier = pltpu.get_barrier_semaphore()
        for b in range(bits):
            bit = lax.rem(lax.div(f, 1 << b), 2)
            pl.semaphore_signal(
                barrier, 1, device_id=(f + (1 << b) * (1 - 2 * bit), z), device_id_type=pl.DeviceIdType.MESH
            )
        for s in range(1, blk):
            pl.semaphore_signal(barrier, 1, device_id=(f, lax.rem(z + s, blk)), device_id_type=pl.DeviceIdType.MESH)
        pl.semaphore_wait(barrier, bits + blk - 1)

        for r in range(blk):
            at = slice(r * chunk, (r + 1) * chunk)
            x = x0[at, :].astype(F32) + jnp.dot(ot[:, at].T, w_out[...], preferred_element_type=F32) + row(b_out)
            x1[at, :] = x
            hat, _ = norm_parts(x)
            a = (hat * row(gain_two) + row(bias_two)).astype(BF16)
            a2[at, :] = a
            a2t[:, at] = a.T
        acc[...] = jnp.zeros_like(acc)
        dacc[...] = jnp.zeros_like(dacc)

    def flush_copies(block, proj):
        half = lax.rem(block, 2)
        got = []
        if proj:
            j = lax.div(block, 2) - ff_steps
            for i in range(2):
                at = pl.ds(pl.multiple_of((j + i * pairs) * pair, pair), pair)
                got.append((grads.at[block, pl.ds(i * width, width)], qkv_out.at[:, at]))
            at = pl.ds(pl.multiple_of((j + 2 * pairs) * pair, pair), pair)
            more = [(grads.at[block, pl.ds(0, width)], qkv_out.at[:, at])]
            at = pl.ds(pl.multiple_of(j * pair, pair), pair)
            more.append((grads.at[block, pl.ds(width, width)], out_out.at[:, at]))
        else:
            step_of = lax.div(block, 2)
            for i in range(ff // LANES):
                at = pl.ds(pl.multiple_of(step_of * ff + i * LANES, LANES), LANES)
                got.append((grads.at[block, pl.ds(i * width, width)], up_out.at[:, at]))
            at = pl.ds(pl.multiple_of(step_of * ff, ff), ff)
            more = []
            for i in range(cols_of):
                more.append((grads.at[block, pl.ds(i * ff, ff)], down_out.at[at, pl.ds(i * LANES, LANES)]))
        pick = lambda some: [pltpu.make_async_copy(a, b, flush_sems.at[block, i]) for i, (a, b) in enumerate(some)]
        return half, pick, got, more

    def flush(block, act):
        for proj in (False, True):

            @pl.when((block >= 2 * ff_steps) if proj else (block < 2 * ff_steps))
            def _():
                half, pick, got, more = flush_copies(block, proj)

                @pl.when(half == 0)
                def _():
                    for c in pick(got):
                        act(c)

                @pl.when(half == 1)
                def _():
                    for c in pick(more):
                        act(c)

    def done(block):
        flush(block, lambda c: c.start())

    first = 2 * step - 2

    @pl.when(step >= 1)
    def _():
        @pl.loop(0, 2)
        def _(i):
            sums.tick(first + i, done)

    @pl.when(step < heads_from)
    def _():
        h = jnp.dot(a2[...], up[...], preferred_element_type=F32) + row(up_bias)
        phi = 0.5 + 0.5 * lax.erf(h * (0.5**0.5))
        slope = phi + h * (jnp.exp2(h * h * (-0.5 * LOG2E)) * (2 * math.pi) ** -0.5)
        g = (h * phi).astype(BF16)
        dg = mm(y[...], down[...], 1, 1)
        dh = (dg * slope).astype(BF16)
        sum_up = jnp.sum(dh.astype(F32), 0, keepdims=True)
        for i in range(ff // LANES):
            vec[pl.ds(VEC_UP * cols_of + step * (ff // LANES) + i, 1), :] = sum_up[:, i * LANES : (i + 1) * LANES]
        acc[...] += jnp.dot(g, down[...], preferred_element_type=F32)
        dacc[...] += mm(dh, up[...], 1, 1)
        d_up = jnp.dot(a2t[...], dh, preferred_element_type=F32).astype(BF16)
        for i in range(ff // LANES):
            grads[2 * step, i * width : (i + 1) * width, :] = d_up[:, i * LANES : (i + 1) * LANES]
        d_down = jnp.dot(g.T, y[...], preferred_element_type=F32).astype(BF16)
        for i in range(cols_of):
            grads[2 * step + 1, i * ff : (i + 1) * ff, :] = d_down[:, i * LANES : (i + 1) * LANES]
        if 2 * width < rows:
            for i in range(2):
                grads[2 * step + i, 2 * width :, :] = jnp.zeros((rows - 2 * width, LANES), BF16)

    @pl.when(step == heads_from - 1)
    def _():
        totals = [jnp.zeros((1, width), F32) for _ in range(4)]
        for r in range(blk):
            at = slice(r * chunk, (r + 1) * chunk)
            grad = dacc[at, :]
            yf = y[at, :].astype(F32)
            xs = x1[at, :]
            out_s[at, :] = (xs + acc[at, :] + row(down_bias)).astype(BF16)
            hat, sc = norm_parts(xs)
            dx = yf + norm_back(grad, hat, sc, row(gain_two))
            x1[at, :] = dx
            dz = dx.astype(BF16)
            a2[at, :] = dz
            dot_s[:, at] = mm(dz, w_out[...], 1, 1).astype(BF16).T
            for i, value in enumerate((grad * hat, grad, yf, dz.astype(F32))):
                totals[i] = totals[i] + jnp.sum(value, 0, keepdims=True)
        local_copy(out_s, out, move_sems.at[0]).start()
        for index, value in zip((VEC_G2, VEC_B2, VEC_DOWN, VEC_OUT), totals):
            put_vec(index, value)
        d_out = jnp.dot(ot[...], a2[...], preferred_element_type=F32).astype(BF16)
        for j in range(pairs):
            grads[2 * (ff_steps + j) + 1, width : 2 * width, :] = d_out[:, j * pair : (j + 1) * pair]
            if 2 * width < rows:
                for i in range(2):
                    grads[2 * (ff_steps + j) + i, 2 * width :, :] = jnp.zeros((rows - 2 * width, LANES), BF16)
        dacc[...] = jnp.zeros_like(dacc)

    @pl.when((step >= heads_from) & (step < heads_to))
    def _():
        index = step - heads_from
        j, head = lax.div(index, 2), lax.rem(index, 2)

        @pl.when(index < pieces * (blk - 1))
        def _():
            piece(send_part, index, 0).start()

        c = HEAD_DIM**-0.5 * LOG2E
        scale = HEAD_DIM**-0.5
        block = 256
        lane = lax.broadcasted_iota(jnp.int32, (slots, pair), 1)
        kb = key_bias(count[z], slots)
        mine = lane // HEAD_DIM == head
        lane = lane % HEAD_DIM
        ka = jnp.where(mine, k[...], jnp.where(lane == 0, kb, jnp.where(lane < 4, 1.0, 0.0)).astype(BF16))
        va = jnp.where(mine, v[...], jnp.where(lane < 3, 1.0, 0.0).astype(BF16))
        rows_of = pl.ds(pl.multiple_of(head * HEAD_DIM, HEAD_DIM), HEAD_DIM)
        rows_all = pl.ds(pl.multiple_of(index * HEAD_DIM, HEAD_DIM), HEAD_DIM)
        do_h = dot_s[rows_all, :]
        q_h = qt[rows_of, :]
        k_h = kt[rows_of, :]
        delta = jnp.sum(do_h.astype(F32) * ot[rows_all, :].astype(F32), 0, keepdims=True)
        l3 = [t.astype(F32) for t in thirds(lse[0, pl.ds(head, 1), :] * -(HEAD_DIM**0.5))]
        d3 = [t.astype(F32) for t in thirds(-delta)]
        zeros = jnp.zeros((HEAD_DIM - 4, slots), F32)
        one = jnp.ones((1, slots), F32)
        extra_q = jnp.concatenate([one, *l3, zeros], 0).astype(BF16)
        extra_d = jnp.concatenate([*d3, zeros, 0.0 * one], 0).astype(BF16)
        upper = lax.broadcasted_iota(jnp.int32, (pair, slots), 0) // HEAD_DIM == head
        qa = jnp.where(upper, jnp.concatenate([q_h, q_h], 0), jnp.concatenate([extra_q, extra_q], 0))
        da = jnp.where(upper, jnp.concatenate([do_h, do_h], 0), jnp.concatenate([extra_d, extra_d], 0))
        for i in range(slots // block):
            at = slice(i * block, (i + 1) * block)
            s = mm(ka, qa[:, at], 1, 0)
            dp = mm(va, da[:, at], 1, 0)
            p = jnp.exp2(s * c)
            ds = (p * dp).astype(BF16)
            p = p.astype(BF16)
            dt[rows_of, at] = (mm(k_h, ds, 1, 0) * scale).astype(BF16)
            dv = mm(do_h[:, at], p, 1, 1)
            dk = mm(q_h[:, at], ds, 1, 1)
            if i == 0:
                dvk[0] = dv
                dvk[1] = dk
            else:
                dvk[0] += dv
                dvk[1] += dk
        dt[pl.ds(pl.multiple_of(pair + head * HEAD_DIM, HEAD_DIM), HEAD_DIM), :] = (dvk[1] * scale).astype(BF16)
        dt[pl.ds(pl.multiple_of(2 * pair + head * HEAD_DIM, HEAD_DIM), HEAD_DIM), :] = dvk[0].astype(BF16)

        @pl.when(head == 1)
        def _():
            d = dt[...]
            part = mm(a1t[...], d, 1, 1).astype(BF16)
            for i in range(3):
                at = slice(i % 2 * width, (i % 2 + 1) * width)
                grads[2 * (ff_steps + j) + i // 2, at, :] = part[:, i * pair : (i + 1) * pair]
            total = mm(jnp.ones((8, slots), BF16), d, 1, 1)
            vec[pl.ds(VEC_Q * cols_of + j, 1), :] = total[:1, :pair]
            vec[pl.ds(VEC_V * cols_of + j, 1), :] = total[:1, 2 * pair :]
            w = jnp.concatenate([wq[...], wk[...], wv[...]], 1)
            dacc[...] += mm(d.T, w, 1, 1)

    @pl.when(step == heads_to)
    def _():
        totals = [jnp.zeros((1, width), F32) for _ in range(2)]
        for r in range(blk):
            at = slice(r * chunk, (r + 1) * chunk)
            grad = dacc[at, :]
            hat, sc = norm_parts(x0[at, :].astype(F32))
            dn = norm_back(grad, hat, sc, row(gain_one))
            din_s[at, :] = (x1[at, :] + dn).astype(BF16)
            for i, value in enumerate((grad * hat, grad)):
                totals[i] = totals[i] + jnp.sum(value, 0, keepdims=True)
        local_copy(din_s, din, move_sems.at[1]).start()
        put_vec(VEC_G1, totals[0])
        put_vec(VEC_B1, totals[1])

    def vec_copy(b):
        bit = lax.rem(lax.div(f, 1 << b), 2)
        return pltpu.make_async_remote_copy(
            src_ref=vec,
            dst_ref=vec_recv.at[b],
            send_sem=vec_sems.at[0, b],
            recv_sem=vec_sems.at[1, b],
            device_id=(f + (1 << b) * (1 - 2 * bit), z),
            device_id_type=pl.DeviceIdType.MESH,
        )

    def vec_blk_copy(s):
        return pltpu.make_async_remote_copy(
            src_ref=vec,
            dst_ref=vec_recv_blk.at[s - 1],
            send_sem=vec_blk_sems.at[0, s - 1],
            recv_sem=vec_blk_sems.at[1, s - 1],
            device_id=(f, lax.rem(z + s, blk)),
            device_id_type=pl.DeviceIdType.MESH,
        )

    @pl.when(step == heads_to)
    def _():
        @pl.loop(2, tail)
        def _(i):
            sums.tick(first + i, done)
            turn = lax.div(i - 2, DIN_EVERY)

            @pl.when((lax.rem(i - 2, DIN_EVERY) == 0) & (turn < pieces * (blk - 1)))
            def _():
                piece(send_part, turn, 1).start()

            for b in range(bits + 2):

                @pl.when(i == 2 + 2 * b)
                def _():
                    if 1 <= b <= bits:
                        vec_copy(b - 1).wait()
                        vec[...] += vec_recv[b - 1]
                    if b < bits:
                        vec_copy(b).start()
                    elif b == bits:
                        for s in range(1, blk):
                            vec_blk_copy(s).start()
                    else:
                        for s in range(1, blk):
                            vec_blk_copy(s).wait()
                        total = vec[...]
                        for s in range(1, blk):
                            total = total + vec_recv_blk[s - 1]
                        vec_out[...] = total

        @pl.loop(0, pieces * (blk - 1))
        def _(i):
            for kind in range(2):
                piece(send_part, i, kind).wait_send()
                piece(part_came, i, kind).wait_recv()

        local_copy(out_s, out, move_sems.at[0]).wait()
        local_copy(din_s, din, move_sems.at[1]).wait()

        @pl.loop(0, sums.count)
        def _(block):
            flush(block, lambda c: c.wait())


def mega(mesh_shape, count, ot, x0, y, w_out, b_out, gain_two, bias_two, up, up_bias, down, down_bias,
         qt, k, kt, v, lse, a1t, w_qkv, gain_one, ff_block=256):
    fields, blk = mesh_shape
    slots, width = x0.shape
    pair = 2 * HEAD_DIM
    pairs = width // pair
    ff_steps = up.shape[1] // ff_block
    bits = fields.bit_length() - 1
    n = fields * blk
    assert ff_block == 2 * LANES
    rows = -(-2 * width // (16 * n)) * 16 * n
    blocks = 2 * (ff_steps + pairs)
    levels = n.bit_length() - 1
    heads_to = ff_steps + 2 * pairs
    last_tick = 2 * ff_steps + 2 + 2 * (2 * pairs - 1) + offsets(bits, levels - bits)[-1]
    tail = last_tick + 1 - (2 * heads_to - 2)
    vec_rows = (8 + up.shape[1] // width) * (width // LANES)
    chunk = slots // blk
    cols_of = width // LANES

    def ff_at(i):
        return jnp.minimum(i, ff_steps - 1)

    def pair_at(i):
        return jnp.clip((i - ff_steps) // 2, 0, pairs - 1)

    tra = pl.BlockSpec((pair, slots), lambda i: (pair_at(i), 0))
    nat = pl.BlockSpec((slots, pair), lambda i: (0, pair_at(i)))

    def cols(part):
        return pl.BlockSpec((width, pair), lambda i: (0, part * pairs + pair_at(i)))

    hbm = pl.BlockSpec(memory_space=pl.ANY)
    one = (width,)
    dma = pltpu.SemaphoreType.DMA
    ahead = SLOTS_AHEAD
    flops = 12 * slots * width * up.shape[1] + 10 * slots * slots * width + 12 * slots * width * width
    return pl.pallas_call(
        partial(mega_kernel, fields, blk, rows, ff_steps, pairs, tail),
        grid=(heads_to + 1,),
        in_specs=[
            pl.BlockSpec(memory_space=pltpu.SMEM),
            whole((width, slots)),
            whole((slots, width)),
            whole((slots, width)),
            whole((width, width)),
            whole(one),
            whole(one),
            whole(one),
            pl.BlockSpec((width, ff_block), lambda i: (0, ff_at(i))),
            pl.BlockSpec((ff_block,), lambda i: (ff_at(i),)),
            pl.BlockSpec((ff_block, width), lambda i: (ff_at(i), 0)),
            whole(one),
            tra, nat, tra, nat,
            pl.BlockSpec((1, 2, slots), lambda i: (pair_at(i), 0, 0)),
            whole((width, slots)),
            cols(0), cols(1), cols(2),
            whole(one),
        ],
        out_specs=[hbm, hbm, hbm, hbm, hbm, hbm, whole((vec_rows, LANES))],
        out_shape=[
            jax.ShapeDtypeStruct((blk, chunk, width), BF16),
            jax.ShapeDtypeStruct((blk, chunk, width), BF16),
            jax.ShapeDtypeStruct((width, up.shape[1]), BF16),
            jax.ShapeDtypeStruct((up.shape[1], width), BF16),
            jax.ShapeDtypeStruct((width, 3 * width), BF16),
            jax.ShapeDtypeStruct((width, width), BF16),
            jax.ShapeDtypeStruct((vec_rows, LANES), F32),
        ],
        scratch_shapes=[
            pltpu.VMEM((slots, width), F32),
            pltpu.VMEM((slots, width), BF16),
            pltpu.VMEM((width, slots), BF16),
            pltpu.VMEM((slots, width), F32),
            pltpu.VMEM((slots, width), F32),
            pltpu.VMEM((slots, width), BF16),
            pltpu.VMEM((width, slots), BF16),
            pltpu.VMEM((3 * pair, slots), BF16),
            pltpu.VMEM((slots, width), BF16),
            pltpu.VMEM((2, HEAD_DIM, slots), F32),
            pltpu.VMEM((blocks, rows, LANES), BF16),
            pltpu.VMEM((vec_rows, LANES), F32),
            pltpu.VMEM((bits, vec_rows, LANES), F32),
            pltpu.VMEM((blk - 1, vec_rows, LANES), F32),
            dma((levels, ahead)),
            dma((levels, ahead)),
            dma((levels, ahead)),
            dma((levels, ahead)),
            dma((2, bits)),
            dma((2, blk - 1)),
            dma((2,)),
            dma((2, 2, 2 * pairs)),
            dma((blocks, cols_of)),
            *[pltpu.VMEM((2, ahead, rows >> (s + 1), LANES), BF16) for s in range(levels)],
        ],
        compiler_params=pltpu.CompilerParams(
            vmem_limit_bytes=67_000_000, collective_id=0, has_side_effects=True
        ),
        cost_estimate=pl.CostEstimate(flops=flops, bytes_accessed=60 * slots * width, transcendentals=0),
        name="mega",
    )(
        count, ot, x0, y, w_out, b_out, gain_two, bias_two, up, up_bias, down, down_bias,
        qt, k, kt, v, lse, a1t, w_qkv, w_qkv, w_qkv, gain_one,
    )


def widen(arrays, steps):
    def kernel(*refs):
        for src, dst in zip(refs[: len(arrays)], refs[len(arrays) :]):
            dst[...] = src[...].astype(F32)

    specs = [pl.BlockSpec((a.shape[0] // steps, a.shape[1]), lambda i: (i, 0)) for a in arrays]
    return pl.pallas_call(
        kernel,
        grid=(steps,),
        in_specs=specs,
        out_specs=specs,
        out_shape=[jax.ShapeDtypeStruct(a.shape, F32) for a in arrays],
        compiler_params=pltpu.CompilerParams(vmem_limit_bytes=VMEM_BYTES),
        name="widen",
    )(*arrays)


def to_field(part):
    return lax.all_to_all(part, "blk", 0, 1, tiled=True)[0]


def per_device(
    mesh_shape, tokens, keep_index, counts, norm1_gain, norm1_bias, qkv_weight, query_bias, value_bias, out_weight,
    out_bias, norm2_gain, norm2_bias, up_weight, up_bias, down_weight, down_bias, cotangent,
):
    width = tokens.shape[2]
    x0 = to_field(place(tokens, keep_index))
    a1t, qt, k, kt, v, vt = project(x0, norm1_gain, norm1_bias, qkv_weight, query_bias, value_bias)
    y = to_field(cotangent)
    _, ot, lse = attend(counts, qt, k, vt)
    output, input_grad, d_up, d_down, d_qkv, d_out, vecs = mega(
        mesh_shape, counts, ot, x0, y, out_weight, out_bias, norm2_gain, norm2_bias, up_weight, up_bias, down_weight,
        down_bias, qt, k, kt, v, lse, a1t, qkv_weight, norm1_gain,
    )
    d_up, d_down, d_qkv, d_out = widen((d_up, d_down, d_qkv, d_out), 12)
    vec = vecs.reshape(-1, width)
    return (
        output,
        input_grad,
        vec[0],
        vec[1],
        d_qkv,
        vec[2],
        vec[3],
        d_out,
        vec[4],
        vec[5],
        vec[6],
        d_up,
        vec[8:].reshape(-1),
        d_down,
        vec[7],
    )


def solution(mesh):
    rows = P("fields", "blk", None)
    return jax.shard_map(
        partial(per_device, (mesh.shape["fields"], mesh.shape["blk"])),
        mesh=mesh,
        in_specs=(rows, P("fields", "blk"), P("fields"), *[P()] * 13, rows),
        out_specs=(rows, rows, *[P()] * 13),
        check_vma=False,
    )
```

```python
from functools import partial
import math
import jax
import jax.numpy as jnp
import numpy as np
from jax import lax
from jax.experimental import pallas as pl
from jax.experimental.pallas import tpu as pltpu
from jax.sharding import PartitionSpec as P

HEAD_DIM = 64
GRID_W = 64
PATCHES = 2048
epsilon = 1e-06
negative = -1e30
VMEM_BYTES = 60 * 1024 * 1024
LOG2E = math.log2(math.e)
F32 = jnp.float32
BF16 = jnp.bfloat16


def mm(a, b, ca, cb):
    return lax.dot_general(a, b, (((ca,), (cb,)), ((), ())), preferred_element_type=F32)


def row(ref):
    return ref[...].astype(F32)[None]


def whole(shape):
    return pl.BlockSpec(shape, lambda *_: (0,) * len(shape), pipeline_mode=pl.Buffered(1))


def norm_parts(values):
    centre = jnp.mean(values, -1, keepdims=True)
    centred = values - centre
    spread = jnp.mean(centred * centred, -1, keepdims=True)
    scale = lax.rsqrt(spread + epsilon)
    return centred * scale, scale


def norm_back(grad, hat, scale, gain):
    scaled = grad * gain
    return scale * (
        scaled
        - jnp.mean(scaled, -1, keepdims=True)
        - hat * jnp.mean(scaled * hat, -1, keepdims=True)
    )


def thirds(row):
    high = row.astype(BF16)
    rest = row - high.astype(F32)
    mid = rest.astype(BF16)
    low = (rest - mid.astype(F32)).astype(BF16)
    return high, mid, low


def tables(width):
    quarter = width // 4
    omega = 1.0 / 10000.0 ** (np.arange(quarter) / quarter)

    def table(length):
        ang = np.arange(length)[:, None] * omega
        return jnp.asarray(np.concatenate([np.sin(ang), np.cos(ang)], -1), F32)

    return table(PATCHES // GRID_W), table(GRID_W)


def place_kernel(tok, keep, row_table, col_table, x0):
    slots = tok.shape[1]
    patch = keep[pl.ds(pl.program_id(0), 1), :]
    parts = []
    for table, of in ((row_table, lax.div(patch, GRID_W)), (col_table, lax.rem(patch, GRID_W))):
        hot = (lax.broadcasted_iota(jnp.int32, (table.shape[0], slots), 0) == of).astype(F32)
        parts.append(jnp.dot(hot.T, table[...], precision=lax.Precision.HIGHEST, preferred_element_type=F32))
    x0[0] = (tok[0].astype(F32) + jnp.concatenate(parts, -1)).astype(BF16)


def place(tokens, keep):
    fields, slots, width = tokens.shape
    row_table, col_table = tables(width)
    block = pl.BlockSpec((1, slots, width), lambda i: (i, 0, 0))
    return pl.pallas_call(
        place_kernel,
        grid=(fields,),
        in_specs=[block, whole((fields, slots)), whole(row_table.shape), whole(col_table.shape)],
        out_specs=block,
        out_shape=jax.ShapeDtypeStruct(tokens.shape, BF16),
        name="place",
    )(tokens, keep, row_table, col_table)


def project_kernel(x0, gain, bias, weight, qb, vb, a1t, qt, k, kt, v, vt):
    width = x0.shape[1]
    hat, _ = norm_parts(x0[...].astype(F32))
    a = (hat * row(gain) + row(bias)).astype(BF16)
    a1t[...] = a.T
    q = (jnp.dot(a, weight[:, :width], preferred_element_type=F32) + row(qb)).astype(BF16)
    qt[...] = q.T
    kk = jnp.dot(a, weight[:, width : 2 * width], preferred_element_type=F32).astype(BF16)
    k[...] = kk
    kt[...] = kk.T
    vv = (jnp.dot(a, weight[:, 2 * width :], preferred_element_type=F32) + row(vb)).astype(BF16)
    v[...] = vv
    vt[...] = vv.T


def project(x0, gain, bias, weight, qb, vb, block=256):
    slots, width = x0.shape
    nat = pl.BlockSpec((block, width), lambda i: (i, 0))
    tra = pl.BlockSpec((width, block), lambda i: (0, i))
    sn = jax.ShapeDtypeStruct((slots, width), BF16)
    st = jax.ShapeDtypeStruct((width, slots), BF16)
    one = whole((width,))
    return pl.pallas_call(
        project_kernel,
        grid=(slots // block,),
        in_specs=[nat, one, one, whole(weight.shape), one, one],
        out_specs=[tra, tra, nat, tra, nat, tra],
        out_shape=[st, st, sn, st, sn, st],
        compiler_params=pltpu.CompilerParams(vmem_limit_bytes=VMEM_BYTES),
        cost_estimate=pl.CostEstimate(flops=2 * slots * width * 3 * width, bytes_accessed=20 * slots * width, transcendentals=0),
        name="project",
    )(x0, gain, bias, weight, qb, vb)


def augment_cols(block, extra, second):
    lane = lax.broadcasted_iota(jnp.int32, block.shape, 1)
    return jnp.where((lane >= HEAD_DIM) if second else (lane < HEAD_DIM), block, extra)


def augment_rows(block, extra, second):
    if second:
        return jnp.concatenate([extra, block[HEAD_DIM:]], 0)
    return jnp.concatenate([block[:HEAD_DIM], extra], 0)


def key_bias(count, slots):
    return jnp.where(lax.broadcasted_iota(jnp.int32, (slots, 1), 0) < count, 0.0, negative)


def attend_kernel(block, count, qt, k, vt, o, ot, lse):
    slots = k.shape[0]
    c = HEAD_DIM**-0.5 * LOG2E
    lane = lax.broadcasted_iota(jnp.int32, (slots, 2 * HEAD_DIM), 1)
    kb = key_bias(count[lax.axis_index("blk")], slots)
    extra_col = jnp.where(lane % HEAD_DIM == 0, kb, 0.0).astype(BF16)
    sub = lax.broadcasted_iota(jnp.int32, (HEAD_DIM, block), 0)
    extra_row = jnp.where(sub == 0, 1.0, 0.0).astype(BF16)
    subv = lax.broadcasted_iota(jnp.int32, (16, slots), 0)
    ones = jnp.where(subv == 0, 1.0, 0.0).astype(BF16)
    work = []
    for head in range(2):
        ka = augment_cols(k[...], extra_col, head == 1)
        va = jnp.concatenate([vt[head * HEAD_DIM : (head + 1) * HEAD_DIM, :], ones], 0)
        for i in range(slots // block):
            work.append((head, ka, va, slice(i * block, (i + 1) * block)))

    def scores(item):
        head, ka, _, cols = item
        return mm(ka, augment_rows(qt[:, cols], extra_row, head == 1), 1, 0)

    s = scores(work[0])
    for n, (head, _, va, cols) in enumerate(work):
        later = scores(work[n + 1]) if n + 1 < len(work) else None
        top = jnp.max(s, 0, keepdims=True)
        p = jnp.exp2((s - top) * c).astype(BF16)
        r = mm(va, p, 1, 0)
        total = r[HEAD_DIM : HEAD_DIM + 1]
        mixed = (r[:HEAD_DIM] / total).astype(BF16)
        ot[head * HEAD_DIM : (head + 1) * HEAD_DIM, cols] = mixed
        lse[0, head : head + 1, cols] = top * HEAD_DIM**-0.5 + jnp.log(total)
        s = later
    o[...] = ot[...].T


def attend(count, qt, k, vt, block=512):
    slots, width = k.shape
    pairs = width // (2 * HEAD_DIM)
    tra = pl.BlockSpec((2 * HEAD_DIM, slots), lambda j: (j, 0))
    nat = pl.BlockSpec((slots, 2 * HEAD_DIM), lambda j: (0, j))
    return pl.pallas_call(
        partial(attend_kernel, block),
        grid=(pairs,),
        in_specs=[pl.BlockSpec(memory_space=pltpu.SMEM), tra, nat, tra],
        out_specs=[nat, tra, pl.BlockSpec((1, 2, slots), lambda j: (j, 0, 0))],
        out_shape=[
            jax.ShapeDtypeStruct((slots, width), BF16),
            jax.ShapeDtypeStruct((width, slots), BF16),
            jax.ShapeDtypeStruct((pairs, 2, slots), F32),
        ],
        compiler_params=pltpu.CompilerParams(vmem_limit_bytes=VMEM_BYTES),
        cost_estimate=pl.CostEstimate(flops=16 * slots * slots * width, bytes_accessed=12 * slots * width, transcendentals=slots * slots * 12),
        name="attend",
    )(count, qt, k, vt)


SLOTS_AHEAD = 8
LANES = 128
LAG_CORE, LAG_XY, LAG_Z = 2, 3, 3
DIN_EVERY = 2


def offsets(near, far):
    lags = [LAG_CORE] + [LAG_XY] * (near - 1) + [LAG_Z] * far
    ticks = [0]
    for lag in lags + lags[::-1]:
        ticks.append(ticks[-1] + lag)
    return ticks


class Sums:
    def __init__(self, fields, blk, rows, early, count, grads, recv, sems):
        self.rows, self.early, self.count = rows, early, count
        self.near, self.far = fields.bit_length() - 1, blk.bit_length() - 1
        self.bits = self.near + self.far
        self.grads, self.recv = grads, recv
        self.send_rs, self.recv_rs, self.send_ag, self.recv_ag = sems
        self.f, self.z = lax.axis_index("fields"), lax.axis_index("blk")
        self.actions = 2 * self.bits + 1
        self.own = [lax.rem(lax.div(self.f, 1 << k), 2) for k in range(self.near)]
        self.own += [lax.rem(lax.div(self.z, 1 << k), 2) for k in range(self.far)]

    def route(self, odd):
        keep, route = 0, []
        for stage in range(self.bits):
            bit = self.own[stage]
            if stage < self.near:
                other = stage if stage == 0 else self.near - stage
                bit = bit + odd * (self.own[other] - bit)
                width = (1 << stage) + odd * ((1 << other) - (1 << stage))
                partner = (self.f + width * (1 - 2 * bit), self.z)
            else:
                partner = (self.f, self.z + (1 << (stage - self.near)) * (1 - 2 * bit))
            size = self.rows >> (stage + 1)
            route.append((partner, keep + bit * size, keep + (1 - bit) * size))
            keep = keep + bit * size
        return route

    def copy(self, gather, block, slot, route, stage):
        partner, kept, sent = route[stage]
        part = pl.ds(pl.multiple_of(kept if gather else sent, 16), self.rows >> (stage + 1))
        send, recv = (self.send_ag, self.recv_ag) if gather else (self.send_rs, self.recv_rs)
        return pltpu.make_async_remote_copy(
            src_ref=self.grads.at[block, part],
            dst_ref=self.recv[stage].at[gather, slot],
            send_sem=send.at[stage, slot],
            recv_sem=recv.at[stage, slot],
            device_id=partner,
            device_id_type=pl.DeviceIdType.MESH,
        )

    def take(self, gather, block, slot, route, stage):
        size = self.rows >> (stage + 1)
        off = route[stage][2 if gather else 1]
        chunk = size
        while chunk > 384 or size % chunk:
            chunk -= 16
        came = self.recv[stage]

        @pl.loop(0, size // chunk)
        def _(i):
            at = pl.ds(pl.multiple_of(off + i * chunk, 16), chunk)
            got = came[gather, slot, pl.ds(pl.multiple_of(i * chunk, 16), chunk), :]
            self.grads[block, at, :] = got if gather else self.grads[block, at, :] + got

    def act(self, kind, block, slot, route):
        bits = self.bits
        if kind > 0:
            gather = int(kind > bits)
            stage = 2 * bits - kind if gather else kind - 1
            self.copy(gather, block, slot, route, stage).wait()
            self.take(gather, block, slot, route, stage)
        if kind < 2 * bits:
            gather = int(kind >= bits)
            self.copy(gather, block, slot, route, 2 * bits - 1 - kind if gather else kind).start()

    def tick(self, tick, done):
        routes = {}
        for odd_offset in (0, 1):
            turn = lax.rem(lax.div(tick + odd_offset, 2), 2)
            routes[odd_offset] = self.route(turn), self.route(1 - turn)
        for kind, offset in enumerate(offsets(self.near, self.far)):
            entry = tick - offset
            late = entry - self.early - 2
            block = jnp.where(late >= 0, self.early + lax.div(late, 2), entry)
            runs = jnp.where(late >= 0, (lax.rem(late, 2) == 0) & (block < self.count), (entry >= 0) & (entry < self.early))
            route = routes[offset % 2][(offset + 1) // 2 % 2]

            @pl.when(runs)
            def _():
                self.act(kind, block, lax.rem(block, SLOTS_AHEAD), route)
                if kind == self.actions - 1:
                    done(block)


def mega_kernel(
    fields, blk, rows, ff_steps, pairs, tail,
    count, ot, x0, y, w_out, b_out, gain_two, bias_two, up, up_bias, down, down_bias,
    qt, k, kt, v, lse, a1t, wq, wk, wv, gain_one,
    out, din, up_out, down_out, qkv_out, out_out, vec_out,
    x1, a2, a2t, acc, dacc, out_s, dot_s, dt, din_s, dvk, grads, vec, vec_recv, vec_recv_blk,
    send_rs, recv_rs, send_ag, recv_ag, vec_sems, vec_blk_sems, move_sems, piece_sems, flush_sems, *recv,
):
    step = pl.program_id(0)
    slots, width = x0.shape
    pair = 2 * HEAD_DIM
    chunk = slots // blk
    cols_of = width // LANES
    f, z = lax.axis_index("fields"), lax.axis_index("blk")
    bits = fields.bit_length() - 1
    ff = up.shape[1]
    heads_from, heads_to = ff_steps, ff_steps + 2 * pairs
    sums = Sums(
        fields, blk, rows, 2 * ff_steps, 2 * (ff_steps + pairs), grads, recv, (send_rs, recv_rs, send_ag, recv_ag)
    )
    VEC_G1, VEC_B1, VEC_Q, VEC_V, VEC_OUT, VEC_G2, VEC_B2, VEC_DOWN, VEC_UP = range(9)

    def put_vec(index, value):
        for i in range(cols_of):
            vec[index * cols_of + i : index * cols_of + i + 1, :] = value[:, i * LANES : (i + 1) * LANES]

    def local_copy(src, dst, sem):
        return pltpu.make_async_copy(src.at[pl.ds(pl.multiple_of(z * chunk, 16), chunk)], dst.at[z], sem)

    def send_part(src, dst, s, part, size, sems):
        to = lax.rem(z + s, blk)
        return pltpu.make_async_remote_copy(
            src_ref=src.at[pl.ds(pl.multiple_of(to * chunk + part * size, 16), size)],
            dst_ref=dst.at[z, pl.ds(pl.multiple_of(part * size, 16), size)],
            send_sem=sems[0],
            recv_sem=sems[1],
            device_id=(f, to),
            device_id_type=pl.DeviceIdType.MESH,
        )

    def part_came(src, dst, s, part, size, sems):
        came = lax.rem(z + blk - s, blk)
        return pltpu.make_async_remote_copy(
            src_ref=src.at[pl.ds(0, size)],
            dst_ref=dst.at[came, pl.ds(pl.multiple_of(part * size, 16), size)],
            send_sem=sems[0],
            recv_sem=sems[1],
            device_id=(f, came),
            device_id_type=pl.DeviceIdType.MESH,
        )

    pieces = 2 * pairs // (blk - 1)

    def piece(maker, i, kind):
        sems = piece_sems.at[kind, 0, i], piece_sems.at[kind, 1, i]
        src, dst = ((out_s, out), (din_s, din))[kind]
        return maker(src, dst, blk - 1 - lax.rem(i, blk - 1), lax.div(i, blk - 1), chunk // pieces, sems)

    @pl.when(step == 0)
    def _():
        barrier = pltpu.get_barrier_semaphore()
        for b in range(bits):
            bit = lax.rem(lax.div(f, 1 << b), 2)
            pl.semaphore_signal(
                barrier, 1, device_id=(f + (1 << b) * (1 - 2 * bit), z), device_id_type=pl.DeviceIdType.MESH
            )
        for s in range(1, blk):
            pl.semaphore_signal(barrier, 1, device_id=(f, lax.rem(z + s, blk)), device_id_type=pl.DeviceIdType.MESH)
        pl.semaphore_wait(barrier, bits + blk - 1)

        for r in range(blk):
            at = slice(r * chunk, (r + 1) * chunk)
            x = x0[at, :].astype(F32) + jnp.dot(ot[:, at].T, w_out[...], preferred_element_type=F32) + row(b_out)
            x1[at, :] = x
            hat, _ = norm_parts(x)
            a = (hat * row(gain_two) + row(bias_two)).astype(BF16)
            a2[at, :] = a
            a2t[:, at] = a.T
        acc[...] = jnp.zeros_like(acc)
        dacc[...] = jnp.zeros_like(dacc)

    def flush_copies(block, proj):
        half = lax.rem(block, 2)
        got = []
        if proj:
            j = lax.div(block, 2) - ff_steps
            for i in range(2):
                at = pl.ds(pl.multiple_of((j + i * pairs) * pair, pair), pair)
                got.append((grads.at[block, pl.ds(i * width, width)], qkv_out.at[:, at]))
            at = pl.ds(pl.multiple_of((j + 2 * pairs) * pair, pair), pair)
            more = [(grads.at[block, pl.ds(0, width)], qkv_out.at[:, at])]
            at = pl.ds(pl.multiple_of(j * pair, pair), pair)
            more.append((grads.at[block, pl.ds(width, width)], out_out.at[:, at]))
        else:
            step_of = lax.div(block, 2)
            for i in range(ff // LANES):
                at = pl.ds(pl.multiple_of(step_of * ff + i * LANES, LANES), LANES)
                got.append((grads.at[block, pl.ds(i * width, width)], up_out.at[:, at]))
            at = pl.ds(pl.multiple_of(step_of * ff, ff), ff)
            more = []
            for i in range(cols_of):
                more.append((grads.at[block, pl.ds(i * ff, ff)], down_out.at[at, pl.ds(i * LANES, LANES)]))
        pick = lambda some: [pltpu.make_async_copy(a, b, flush_sems.at[block, i]) for i, (a, b) in enumerate(some)]
        return half, pick, got, more

    def flush(block, act):
        for proj in (False, True):

            @pl.when((block >= 2 * ff_steps) if proj else (block < 2 * ff_steps))
            def _():
                half, pick, got, more = flush_copies(block, proj)

                @pl.when(half == 0)
                def _():
                    for c in pick(got):
                        act(c)

                @pl.when(half == 1)
                def _():
                    for c in pick(more):
                        act(c)

    def done(block):
        flush(block, lambda c: c.start())

    first = 2 * step - 2

    @pl.when(step >= 1)
    def _():
        @pl.loop(0, 2)
        def _(i):
            sums.tick(first + i, done)

    @pl.when(step < heads_from)
    def _():
        half = slots // 2
        parts = [slice(0, half), slice(half, slots)]
        ahead = []
        for at in parts:
            h = jnp.dot(a2[at, :], up[...], preferred_element_type=F32) + row(up_bias)
            ahead.append((h, mm(y[at, :], down[...], 1, 1)))
        sum_up = d_up = d_down = 0.0
        for at, (h, dg) in zip(parts, ahead):
            phi = 0.5 + 0.5 * lax.erf(h * (0.5**0.5))
            slope = phi + h * (jnp.exp2(h * h * (-0.5 * LOG2E)) * (2 * math.pi) ** -0.5)
            g = (h * phi).astype(BF16)
            dh = (dg * slope).astype(BF16)
            acc[at, :] += jnp.dot(g, down[...], preferred_element_type=F32)
            dacc[at, :] += mm(dh, up[...], 1, 1)
            sum_up = sum_up + jnp.sum(dh.astype(F32), 0, keepdims=True)
            d_up = d_up + jnp.dot(a2t[:, at], dh, preferred_element_type=F32)
            d_down = d_down + jnp.dot(g.T, y[at, :], preferred_element_type=F32)
        d_up, d_down = d_up.astype(BF16), d_down.astype(BF16)
        for i in range(ff // LANES):
            vec[pl.ds(VEC_UP * cols_of + step * (ff // LANES) + i, 1), :] = sum_up[:, i * LANES : (i + 1) * LANES]
        for i in range(ff // LANES):
            grads[2 * step, i * width : (i + 1) * width, :] = d_up[:, i * LANES : (i + 1) * LANES]
        for i in range(cols_of):
            grads[2 * step + 1, i * ff : (i + 1) * ff, :] = d_down[:, i * LANES : (i + 1) * LANES]
        if 2 * width < rows:
            for i in range(2):
                grads[2 * step + i, 2 * width :, :] = jnp.zeros((rows - 2 * width, LANES), BF16)

    @pl.when(step == heads_from - 1)
    def _():
        totals = [jnp.zeros((1, width), F32) for _ in range(4)]
        for r in range(blk):
            at = slice(r * chunk, (r + 1) * chunk)
            grad = dacc[at, :]
            yf = y[at, :].astype(F32)
            xs = x1[at, :]
            out_s[at, :] = (xs + acc[at, :] + row(down_bias)).astype(BF16)
            hat, sc = norm_parts(xs)
            dx = yf + norm_back(grad, hat, sc, row(gain_two))
            x1[at, :] = dx
            dz = dx.astype(BF16)
            a2[at, :] = dz
            dot_s[:, at] = mm(dz, w_out[...], 1, 1).astype(BF16).T
            for i, value in enumerate((grad * hat, grad, yf, dz.astype(F32))):
                totals[i] = totals[i] + jnp.sum(value, 0, keepdims=True)
        local_copy(out_s, out, move_sems.at[0]).start()
        for index, value in zip((VEC_G2, VEC_B2, VEC_DOWN, VEC_OUT), totals):
            put_vec(index, value)
        d_out = jnp.dot(ot[...], a2[...], preferred_element_type=F32).astype(BF16)
        for j in range(pairs):
            grads[2 * (ff_steps + j) + 1, width : 2 * width, :] = d_out[:, j * pair : (j + 1) * pair]
            if 2 * width < rows:
                for i in range(2):
                    grads[2 * (ff_steps + j) + i, 2 * width :, :] = jnp.zeros((rows - 2 * width, LANES), BF16)
        dacc[...] = jnp.zeros_like(dacc)

    @pl.when((step >= heads_from) & (step < heads_to))
    def _():
        index = step - heads_from
        j, head = lax.div(index, 2), lax.rem(index, 2)

        @pl.when(index < pieces * (blk - 1))
        def _():
            piece(send_part, index, 0).start()

        c = HEAD_DIM**-0.5 * LOG2E
        scale = HEAD_DIM**-0.5
        block = 256
        lane = lax.broadcasted_iota(jnp.int32, (slots, pair), 1)
        kb = key_bias(count[z], slots)
        mine = lane // HEAD_DIM == head
        lane = lane % HEAD_DIM
        ka = jnp.where(mine, k[...], jnp.where(lane == 0, kb, jnp.where(lane < 4, 1.0, 0.0)).astype(BF16))
        va = jnp.where(mine, v[...], jnp.where(lane < 3, 1.0, 0.0).astype(BF16))
        rows_of = pl.ds(pl.multiple_of(head * HEAD_DIM, HEAD_DIM), HEAD_DIM)
        rows_all = pl.ds(pl.multiple_of(index * HEAD_DIM, HEAD_DIM), HEAD_DIM)
        do_h = dot_s[rows_all, :]
        q_h = qt[rows_of, :]
        k_h = kt[rows_of, :]
        delta = jnp.sum(do_h.astype(F32) * ot[rows_all, :].astype(F32), 0, keepdims=True)
        l3 = [t.astype(F32) for t in thirds(lse[0, pl.ds(head, 1), :] * -(HEAD_DIM**0.5))]
        d3 = [t.astype(F32) for t in thirds(-delta)]
        zeros = jnp.zeros((HEAD_DIM - 4, slots), F32)
        one = jnp.ones((1, slots), F32)
        extra_q = jnp.concatenate([one, *l3, zeros], 0).astype(BF16)
        extra_d = jnp.concatenate([*d3, zeros, 0.0 * one], 0).astype(BF16)
        upper = lax.broadcasted_iota(jnp.int32, (pair, slots), 0) // HEAD_DIM == head
        qa = jnp.where(upper, jnp.concatenate([q_h, q_h], 0), jnp.concatenate([extra_q, extra_q], 0))
        da = jnp.where(upper, jnp.concatenate([do_h, do_h], 0), jnp.concatenate([extra_d, extra_d], 0))
        def scores(i):
            at = slice(i * block, (i + 1) * block)
            return mm(ka, qa[:, at], 1, 0), mm(va, da[:, at], 1, 0)

        ready = scores(0)
        for i in range(slots // block):
            at = slice(i * block, (i + 1) * block)
            s, dp = ready
            if i + 1 < slots // block:
                ready = scores(i + 1)
            p = jnp.exp2(s * c)
            ds = (p * dp).astype(BF16)
            p = p.astype(BF16)
            dt[rows_of, at] = (mm(k_h, ds, 1, 0) * scale).astype(BF16)
            dv = mm(do_h[:, at], p, 1, 1)
            dk = mm(q_h[:, at], ds, 1, 1)
            if i == 0:
                dvk[0] = dv
                dvk[1] = dk
            else:
                dvk[0] += dv
                dvk[1] += dk
        dt[pl.ds(pl.multiple_of(pair + head * HEAD_DIM, HEAD_DIM), HEAD_DIM), :] = (dvk[1] * scale).astype(BF16)
        dt[pl.ds(pl.multiple_of(2 * pair + head * HEAD_DIM, HEAD_DIM), HEAD_DIM), :] = dvk[0].astype(BF16)

        @pl.when(head == 1)
        def _():
            d = dt[...]
            part = mm(a1t[...], d, 1, 1).astype(BF16)
            for i in range(3):
                at = slice(i % 2 * width, (i % 2 + 1) * width)
                grads[2 * (ff_steps + j) + i // 2, at, :] = part[:, i * pair : (i + 1) * pair]
            total = mm(jnp.ones((8, slots), BF16), d, 1, 1)
            vec[pl.ds(VEC_Q * cols_of + j, 1), :] = total[:1, :pair]
            vec[pl.ds(VEC_V * cols_of + j, 1), :] = total[:1, 2 * pair :]
            w = jnp.concatenate([wq[...], wk[...], wv[...]], 1)
            dacc[...] += mm(d.T, w, 1, 1)

    @pl.when(step == heads_to)
    def _():
        totals = [jnp.zeros((1, width), F32) for _ in range(2)]
        for r in range(blk):
            at = slice(r * chunk, (r + 1) * chunk)
            grad = dacc[at, :]
            hat, sc = norm_parts(x0[at, :].astype(F32))
            dn = norm_back(grad, hat, sc, row(gain_one))
            din_s[at, :] = (x1[at, :] + dn).astype(BF16)
            for i, value in enumerate((grad * hat, grad)):
                totals[i] = totals[i] + jnp.sum(value, 0, keepdims=True)
        local_copy(din_s, din, move_sems.at[1]).start()
        put_vec(VEC_G1, totals[0])
        put_vec(VEC_B1, totals[1])

    def vec_copy(b):
        bit = lax.rem(lax.div(f, 1 << b), 2)
        return pltpu.make_async_remote_copy(
            src_ref=vec,
            dst_ref=vec_recv.at[b],
            send_sem=vec_sems.at[0, b],
            recv_sem=vec_sems.at[1, b],
            device_id=(f + (1 << b) * (1 - 2 * bit), z),
            device_id_type=pl.DeviceIdType.MESH,
        )

    def vec_blk_copy(s):
        return pltpu.make_async_remote_copy(
            src_ref=vec,
            dst_ref=vec_recv_blk.at[s - 1],
            send_sem=vec_blk_sems.at[0, s - 1],
            recv_sem=vec_blk_sems.at[1, s - 1],
            device_id=(f, lax.rem(z + s, blk)),
            device_id_type=pl.DeviceIdType.MESH,
        )

    @pl.when(step == heads_to)
    def _():
        @pl.loop(2, tail)
        def _(i):
            sums.tick(first + i, done)
            turn = lax.div(i - 2, DIN_EVERY)

            @pl.when((lax.rem(i - 2, DIN_EVERY) == 0) & (turn < pieces * (blk - 1)))
            def _():
                piece(send_part, turn, 1).start()

            for b in range(bits + 2):

                @pl.when(i == 2 + 2 * b)
                def _():
                    if 1 <= b <= bits:
                        vec_copy(b - 1).wait()
                        vec[...] += vec_recv[b - 1]
                    if b < bits:
                        vec_copy(b).start()
                    elif b == bits:
                        for s in range(1, blk):
                            vec_blk_copy(s).start()
                    else:
                        for s in range(1, blk):
                            vec_blk_copy(s).wait()
                        total = vec[...]
                        for s in range(1, blk):
                            total = total + vec_recv_blk[s - 1]
                        vec_out[...] = total

        @pl.loop(0, pieces * (blk - 1))
        def _(i):
            for kind in range(2):
                piece(send_part, i, kind).wait_send()
                piece(part_came, i, kind).wait_recv()

        local_copy(out_s, out, move_sems.at[0]).wait()
        local_copy(din_s, din, move_sems.at[1]).wait()

        @pl.loop(0, sums.count)
        def _(block):
            flush(block, lambda c: c.wait())


def mega(mesh_shape, count, ot, x0, y, w_out, b_out, gain_two, bias_two, up, up_bias, down, down_bias,
         qt, k, kt, v, lse, a1t, w_qkv, gain_one, ff_block=256):
    fields, blk = mesh_shape
    slots, width = x0.shape
    pair = 2 * HEAD_DIM
    pairs = width // pair
    ff_steps = up.shape[1] // ff_block
    bits = fields.bit_length() - 1
    n = fields * blk
    assert ff_block == 2 * LANES
    rows = -(-2 * width // (16 * n)) * 16 * n
    blocks = 2 * (ff_steps + pairs)
    levels = n.bit_length() - 1
    heads_to = ff_steps + 2 * pairs
    last_tick = 2 * ff_steps + 2 + 2 * (2 * pairs - 1) + offsets(bits, levels - bits)[-1]
    tail = last_tick + 1 - (2 * heads_to - 2)
    vec_rows = (8 + up.shape[1] // width) * (width // LANES)
    chunk = slots // blk
    cols_of = width // LANES

    def ff_at(i):
        return jnp.minimum(i, ff_steps - 1)

    def pair_at(i):
        return jnp.clip((i - ff_steps) // 2, 0, pairs - 1)

    tra = pl.BlockSpec((pair, slots), lambda i: (pair_at(i), 0))
    nat = pl.BlockSpec((slots, pair), lambda i: (0, pair_at(i)))

    def cols(part):
        return pl.BlockSpec((width, pair), lambda i: (0, part * pairs + pair_at(i)))

    hbm = pl.BlockSpec(memory_space=pl.ANY)
    one = (width,)
    dma = pltpu.SemaphoreType.DMA
    ahead = SLOTS_AHEAD
    flops = 12 * slots * width * up.shape[1] + 10 * slots * slots * width + 12 * slots * width * width
    return pl.pallas_call(
        partial(mega_kernel, fields, blk, rows, ff_steps, pairs, tail),
        grid=(heads_to + 1,),
        in_specs=[
            pl.BlockSpec(memory_space=pltpu.SMEM),
            whole((width, slots)),
            whole((slots, width)),
            whole((slots, width)),
            whole((width, width)),
            whole(one),
            whole(one),
            whole(one),
            pl.BlockSpec((width, ff_block), lambda i: (0, ff_at(i))),
            pl.BlockSpec((ff_block,), lambda i: (ff_at(i),)),
            pl.BlockSpec((ff_block, width), lambda i: (ff_at(i), 0)),
            whole(one),
            tra, nat, tra, nat,
            pl.BlockSpec((1, 2, slots), lambda i: (pair_at(i), 0, 0)),
            whole((width, slots)),
            cols(0), cols(1), cols(2),
            whole(one),
        ],
        out_specs=[hbm, hbm, hbm, hbm, hbm, hbm, whole((vec_rows, LANES))],
        out_shape=[
            jax.ShapeDtypeStruct((blk, chunk, width), BF16),
            jax.ShapeDtypeStruct((blk, chunk, width), BF16),
            jax.ShapeDtypeStruct((width, up.shape[1]), BF16),
            jax.ShapeDtypeStruct((up.shape[1], width), BF16),
            jax.ShapeDtypeStruct((width, 3 * width), BF16),
            jax.ShapeDtypeStruct((width, width), BF16),
            jax.ShapeDtypeStruct((vec_rows, LANES), F32),
        ],
        scratch_shapes=[
            pltpu.VMEM((slots, width), F32),
            pltpu.VMEM((slots, width), BF16),
            pltpu.VMEM((width, slots), BF16),
            pltpu.VMEM((slots, width), F32),
            pltpu.VMEM((slots, width), F32),
            pltpu.VMEM((slots, width), BF16),
            pltpu.VMEM((width, slots), BF16),
            pltpu.VMEM((3 * pair, slots), BF16),
            pltpu.VMEM((slots, width), BF16),
            pltpu.VMEM((2, HEAD_DIM, slots), F32),
            pltpu.VMEM((blocks, rows, LANES), BF16),
            pltpu.VMEM((vec_rows, LANES), F32),
            pltpu.VMEM((bits, vec_rows, LANES), F32),
            pltpu.VMEM((blk - 1, vec_rows, LANES), F32),
            dma((levels, ahead)),
            dma((levels, ahead)),
            dma((levels, ahead)),
            dma((levels, ahead)),
            dma((2, bits)),
            dma((2, blk - 1)),
            dma((2,)),
            dma((2, 2, 2 * pairs)),
            dma((blocks, cols_of)),
            *[pltpu.VMEM((2, ahead, rows >> (s + 1), LANES), BF16) for s in range(levels)],
        ],
        compiler_params=pltpu.CompilerParams(
            vmem_limit_bytes=67_000_000, collective_id=0, has_side_effects=True
        ),
        cost_estimate=pl.CostEstimate(flops=flops, bytes_accessed=60 * slots * width, transcendentals=0),
        name="mega",
    )(
        count, ot, x0, y, w_out, b_out, gain_two, bias_two, up, up_bias, down, down_bias,
        qt, k, kt, v, lse, a1t, w_qkv, w_qkv, w_qkv, gain_one,
    )


def widen(arrays, steps):
    def kernel(*refs):
        for src, dst in zip(refs[: len(arrays)], refs[len(arrays) :]):
            dst[...] = src[...].astype(F32)

    specs = [pl.BlockSpec((a.shape[0] // steps, a.shape[1]), lambda i: (i, 0)) for a in arrays]
    return pl.pallas_call(
        kernel,
        grid=(steps,),
        in_specs=specs,
        out_specs=specs,
        out_shape=[jax.ShapeDtypeStruct(a.shape, F32) for a in arrays],
        compiler_params=pltpu.CompilerParams(vmem_limit_bytes=VMEM_BYTES),
        name="widen",
    )(*arrays)


def to_field(part):
    return lax.all_to_all(part, "blk", 0, 1, tiled=True)[0]


def per_device(
    mesh_shape, tokens, keep_index, counts, norm1_gain, norm1_bias, qkv_weight, query_bias, value_bias, out_weight,
    out_bias, norm2_gain, norm2_bias, up_weight, up_bias, down_weight, down_bias, cotangent,
):
    width = tokens.shape[2]
    x0 = to_field(place(tokens, keep_index))
    a1t, qt, k, kt, v, vt = project(x0, norm1_gain, norm1_bias, qkv_weight, query_bias, value_bias)
    y = to_field(cotangent)
    _, ot, lse = attend(counts, qt, k, vt)
    output, input_grad, d_up, d_down, d_qkv, d_out, vecs = mega(
        mesh_shape, counts, ot, x0, y, out_weight, out_bias, norm2_gain, norm2_bias, up_weight, up_bias, down_weight,
        down_bias, qt, k, kt, v, lse, a1t, qkv_weight, norm1_gain,
    )
    d_up, d_down, d_qkv, d_out = widen((d_up, d_down, d_qkv, d_out), 12)
    vec = vecs.reshape(-1, width)
    return (
        output,
        input_grad,
        vec[0],
        vec[1],
        d_qkv,
        vec[2],
        vec[3],
        d_out,
        vec[4],
        vec[5],
        vec[6],
        d_up,
        vec[8:].reshape(-1),
        d_down,
        vec[7],
    )


def solution(mesh):
    rows = P("fields", "blk", None)
    return jax.shard_map(
        partial(per_device, (mesh.shape["fields"], mesh.shape["blk"])),
        mesh=mesh,
        in_specs=(rows, P("fields", "blk"), P("fields"), *[P()] * 13, rows),
        out_specs=(rows, rows, *[P()] * 13),
        check_vma=False,
    )
```

```python
from functools import partial
import math
import jax
import jax.numpy as jnp
import ml_dtypes
import numpy as np
from jax import lax
from jax.experimental import pallas as pl
from jax.experimental.pallas import tpu as pltpu
from jax.sharding import PartitionSpec as P

HEAD_DIM = 64
GRID_W = 64
PATCHES = 2048
epsilon = 1e-06
negative = -1e30
VMEM_BYTES = 60 * 1024 * 1024
LOG2E = math.log2(math.e)
F32 = jnp.float32
BF16 = jnp.bfloat16


def mm(a, b, ca, cb):
    return lax.dot_general(a, b, (((ca,), (cb,)), ((), ())), preferred_element_type=F32)


def row(ref):
    return ref[...].astype(F32)[None]


def whole(shape):
    return pl.BlockSpec(shape, lambda *_: (0,) * len(shape), pipeline_mode=pl.Buffered(1))


def norm_parts(values):
    centre = jnp.mean(values, -1, keepdims=True)
    centred = values - centre
    spread = jnp.mean(centred * centred, -1, keepdims=True)
    scale = lax.rsqrt(spread + epsilon)
    return centred * scale, scale


def norm_back(grad, hat, scale, gain):
    scaled = grad * gain
    return scale * (
        scaled
        - jnp.mean(scaled, -1, keepdims=True)
        - hat * jnp.mean(scaled * hat, -1, keepdims=True)
    )


def thirds(row):
    high = row.astype(BF16)
    rest = row - high.astype(F32)
    mid = rest.astype(BF16)
    low = (rest - mid.astype(F32)).astype(BF16)
    return high, mid, low


def tables(width):
    quarter = width // 4
    omega = 1.0 / 10000.0 ** (np.arange(quarter) / quarter)

    def table(length):
        ang = np.arange(length)[:, None] * omega
        rest = np.concatenate([np.sin(ang), np.cos(ang)], -1).astype(np.float32)
        parts = []
        for _ in range(3):
            parts.append(rest.astype(ml_dtypes.bfloat16))
            rest = rest - parts[-1].astype(np.float32)
        return jnp.asarray(np.concatenate(parts, 0))

    return table(PATCHES // GRID_W), table(GRID_W)


def place_kernel(blk, tok, keep, row_table, col_table, x0, placed, sems):
    slots = tok.shape[1]
    f, z = lax.axis_index("fields"), lax.axis_index("blk")
    barrier = pltpu.get_barrier_semaphore()
    for s in range(1, blk):
        pl.semaphore_signal(barrier, 1, device_id=(f, lax.rem(z + s, blk)), device_id_type=pl.DeviceIdType.MESH)
    pl.semaphore_wait(barrier, blk - 1)

    def copy(s):
        to = lax.rem(z + s, blk)
        return pltpu.make_async_remote_copy(
            src_ref=placed.at[to],
            dst_ref=x0.at[z],
            send_sem=sems.at[0, s],
            recv_sem=sems.at[1, s],
            device_id=(f, to),
            device_id_type=pl.DeviceIdType.MESH,
        )

    def came(s):
        source = lax.rem(z + blk - s, blk)
        return pltpu.make_async_remote_copy(
            src_ref=placed.at[source],
            dst_ref=x0.at[source],
            send_sem=sems.at[0, s],
            recv_sem=sems.at[1, s],
            device_id=(f, source),
            device_id_type=pl.DeviceIdType.MESH,
        )

    for s in range(blk - 1, -1, -1):
        to = lax.rem(z + s, blk)
        patch = keep[pl.ds(to, 1), :]
        parts = []
        for table, of in ((row_table, lax.div(patch, GRID_W)), (col_table, lax.rem(patch, GRID_W))):
            size = table.shape[0] // 3
            index = lax.broadcasted_iota(jnp.int32, (size, slots), 0)
            hot = jnp.where(index == of, 1.0, 0.0).astype(BF16)
            hot = jnp.concatenate([hot, hot, hot], 0).T
            parts.append(jnp.dot(hot, table[...], preferred_element_type=F32))
        here = (tok[to].astype(F32) + jnp.concatenate(parts, -1)).astype(BF16)
        if s > 0:
            placed[to] = here
            copy(s).start()
        else:
            x0[z] = here
    for s in range(blk - 1, 0, -1):
        copy(s).wait_send()
        came(s).wait_recv()


def place(blk, tokens, keep):
    fields, slots, width = tokens.shape
    row_table, col_table = tables(width)
    vmem = pl.BlockSpec(memory_space=pltpu.VMEM)
    return pl.pallas_call(
        partial(place_kernel, blk),
        in_specs=[vmem] * 4,
        out_specs=vmem,
        out_shape=jax.ShapeDtypeStruct(tokens.shape, BF16),
        scratch_shapes=[pltpu.VMEM(tokens.shape, BF16), pltpu.SemaphoreType.DMA((2, blk))],
        compiler_params=pltpu.CompilerParams(collective_id=1, has_side_effects=True),
        name="place",
    )(tokens, keep, row_table, col_table).reshape(fields * slots, width)


def project_kernel(x0, gain, bias, weight, qb, vb, a1t, qt, k, kt, v, vt):
    width = x0.shape[1]
    hat, _ = norm_parts(x0[...].astype(F32))
    a = (hat * row(gain) + row(bias)).astype(BF16)
    a1t[...] = a.T
    q = (jnp.dot(a, weight[:, :width], preferred_element_type=F32) + row(qb)).astype(BF16)
    qt[...] = q.T
    kk = jnp.dot(a, weight[:, width : 2 * width], preferred_element_type=F32).astype(BF16)
    k[...] = kk
    kt[...] = kk.T
    vv = (jnp.dot(a, weight[:, 2 * width :], preferred_element_type=F32) + row(vb)).astype(BF16)
    v[...] = vv
    vt[...] = vv.T


def project(x0, gain, bias, weight, qb, vb, block=256):
    slots, width = x0.shape
    nat = pl.BlockSpec((block, width), lambda i: (i, 0))
    tra = pl.BlockSpec((width, block), lambda i: (0, i))
    sn = jax.ShapeDtypeStruct((slots, width), BF16)
    st = jax.ShapeDtypeStruct((width, slots), BF16)
    one = whole((width,))
    return pl.pallas_call(
        project_kernel,
        grid=(slots // block,),
        in_specs=[nat, one, one, whole(weight.shape), one, one],
        out_specs=[tra, tra, nat, tra, nat, tra],
        out_shape=[st, st, sn, st, sn, st],
        compiler_params=pltpu.CompilerParams(vmem_limit_bytes=VMEM_BYTES),
        cost_estimate=pl.CostEstimate(flops=2 * slots * width * 3 * width, bytes_accessed=20 * slots * width, transcendentals=0),
        name="project",
    )(x0, gain, bias, weight, qb, vb)


def augment_cols(block, extra, second):
    lane = lax.broadcasted_iota(jnp.int32, block.shape, 1)
    return jnp.where((lane >= HEAD_DIM) if second else (lane < HEAD_DIM), block, extra)


def augment_rows(block, extra, second):
    if second:
        return jnp.concatenate([extra, block[HEAD_DIM:]], 0)
    return jnp.concatenate([block[:HEAD_DIM], extra], 0)


def key_bias(count, slots):
    return jnp.where(lax.broadcasted_iota(jnp.int32, (slots, 1), 0) < count, 0.0, negative)


def attend_kernel(block, count, qt, k, vt, o, ot, lse):
    slots = k.shape[0]
    c = HEAD_DIM**-0.5 * LOG2E
    lane = lax.broadcasted_iota(jnp.int32, (slots, 2 * HEAD_DIM), 1)
    kb = key_bias(count[lax.axis_index("blk")], slots)
    extra_col = jnp.where(lane % HEAD_DIM == 0, kb, 0.0).astype(BF16)
    sub = lax.broadcasted_iota(jnp.int32, (HEAD_DIM, block), 0)
    extra_row = jnp.where(sub == 0, 1.0, 0.0).astype(BF16)
    subv = lax.broadcasted_iota(jnp.int32, (16, slots), 0)
    ones = jnp.where(subv == 0, 1.0, 0.0).astype(BF16)
    work = []
    for head in range(2):
        ka = augment_cols(k[...], extra_col, head == 1)
        va = jnp.concatenate([vt[head * HEAD_DIM : (head + 1) * HEAD_DIM, :], ones], 0)
        for i in range(slots // block):
            work.append((head, ka, va, slice(i * block, (i + 1) * block)))

    def scores(item):
        head, ka, _, cols = item
        return mm(ka, augment_rows(qt[:, cols], extra_row, head == 1), 1, 0)

    s = scores(work[0])
    for n, (head, _, va, cols) in enumerate(work):
        later = scores(work[n + 1]) if n + 1 < len(work) else None
        top = jnp.max(s, 0, keepdims=True)
        p = jnp.exp2((s - top) * c).astype(BF16)
        r = mm(va, p, 1, 0)
        total = r[HEAD_DIM : HEAD_DIM + 1]
        mixed = (r[:HEAD_DIM] / total).astype(BF16)
        ot[head * HEAD_DIM : (head + 1) * HEAD_DIM, cols] = mixed
        lse[0, head : head + 1, cols] = top * HEAD_DIM**-0.5 + jnp.log(total)
        s = later
    o[...] = ot[...].T


def attend(count, qt, k, vt, block=512):
    slots, width = k.shape
    pairs = width // (2 * HEAD_DIM)
    tra = pl.BlockSpec((2 * HEAD_DIM, slots), lambda j: (j, 0))
    nat = pl.BlockSpec((slots, 2 * HEAD_DIM), lambda j: (0, j))
    return pl.pallas_call(
        partial(attend_kernel, block),
        grid=(pairs,),
        in_specs=[pl.BlockSpec(memory_space=pltpu.SMEM), tra, nat, tra],
        out_specs=[nat, tra, pl.BlockSpec((1, 2, slots), lambda j: (j, 0, 0))],
        out_shape=[
            jax.ShapeDtypeStruct((slots, width), BF16),
            jax.ShapeDtypeStruct((width, slots), BF16),
            jax.ShapeDtypeStruct((pairs, 2, slots), F32),
        ],
        compiler_params=pltpu.CompilerParams(vmem_limit_bytes=VMEM_BYTES),
        cost_estimate=pl.CostEstimate(flops=16 * slots * slots * width, bytes_accessed=12 * slots * width, transcendentals=slots * slots * 12),
        name="attend",
    )(count, qt, k, vt)


SLOTS_AHEAD = 8
LANES = 128
LAG_CORE, LAG_XY, LAG_Z = 2, 3, 3
DIN_EVERY = 2


def offsets(near, far):
    lags = [LAG_CORE] + [LAG_XY] * (near - 1) + [LAG_Z] * far
    ticks = [0]
    for lag in lags + lags[::-1]:
        ticks.append(ticks[-1] + lag)
    return ticks


class Sums:
    def __init__(self, fields, blk, rows, early, count, grads, recv, sems):
        self.rows, self.early, self.count = rows, early, count
        self.near, self.far = fields.bit_length() - 1, blk.bit_length() - 1
        self.bits = self.near + self.far
        self.grads, self.recv = grads, recv
        self.send_rs, self.recv_rs, self.send_ag, self.recv_ag = sems
        self.f, self.z = lax.axis_index("fields"), lax.axis_index("blk")
        self.actions = 2 * self.bits + 1
        self.own = [lax.rem(lax.div(self.f, 1 << k), 2) for k in range(self.near)]
        self.own += [lax.rem(lax.div(self.z, 1 << k), 2) for k in range(self.far)]

    def route(self, odd):
        keep, route = 0, []
        for stage in range(self.bits):
            bit = self.own[stage]
            if stage < self.near:
                other = stage if stage == 0 else self.near - stage
                bit = bit + odd * (self.own[other] - bit)
                width = (1 << stage) + odd * ((1 << other) - (1 << stage))
                partner = (self.f + width * (1 - 2 * bit), self.z)
            else:
                partner = (self.f, self.z + (1 << (stage - self.near)) * (1 - 2 * bit))
            size = self.rows >> (stage + 1)
            route.append((partner, keep + bit * size, keep + (1 - bit) * size))
            keep = keep + bit * size
        return route

    def copy(self, gather, block, slot, route, stage):
        partner, kept, sent = route[stage]
        part = pl.ds(pl.multiple_of(kept if gather else sent, 16), self.rows >> (stage + 1))
        send, recv = (self.send_ag, self.recv_ag) if gather else (self.send_rs, self.recv_rs)
        return pltpu.make_async_remote_copy(
            src_ref=self.grads.at[block, part],
            dst_ref=self.recv[stage].at[gather, slot],
            send_sem=send.at[stage, slot],
            recv_sem=recv.at[stage, slot],
            device_id=partner,
            device_id_type=pl.DeviceIdType.MESH,
        )

    def take(self, gather, block, slot, route, stage):
        size = self.rows >> (stage + 1)
        off = route[stage][2 if gather else 1]
        chunk = size
        while chunk > 384 or size % chunk:
            chunk -= 16
        came = self.recv[stage]

        @pl.loop(0, size // chunk)
        def _(i):
            at = pl.ds(pl.multiple_of(off + i * chunk, 16), chunk)
            got = came[gather, slot, pl.ds(pl.multiple_of(i * chunk, 16), chunk), :]
            self.grads[block, at, :] = got if gather else self.grads[block, at, :] + got

    def act(self, kind, block, slot, route):
        bits = self.bits
        if kind > 0:
            gather = int(kind > bits)
            stage = 2 * bits - kind if gather else kind - 1
            self.copy(gather, block, slot, route, stage).wait()
            self.take(gather, block, slot, route, stage)
        if kind < 2 * bits:
            gather = int(kind >= bits)
            self.copy(gather, block, slot, route, 2 * bits - 1 - kind if gather else kind).start()

    def tick(self, tick, done):
        routes = {}
        for odd_offset in (0, 1):
            turn = lax.rem(lax.div(tick + odd_offset, 2), 2)
            routes[odd_offset] = self.route(turn), self.route(1 - turn)
        for kind, offset in enumerate(offsets(self.near, self.far)):
            entry = tick - offset
            late = entry - self.early - 2
            block = jnp.where(late >= 0, self.early + lax.div(late, 2), entry)
            runs = jnp.where(late >= 0, (lax.rem(late, 2) == 0) & (block < self.count), (entry >= 0) & (entry < self.early))
            route = routes[offset % 2][(offset + 1) // 2 % 2]

            @pl.when(runs)
            def _():
                self.act(kind, block, lax.rem(block, SLOTS_AHEAD), route)
                if kind == self.actions - 1:
                    done(block)


def mega_kernel(
    fields, blk, rows, ff_steps, pairs, tail,
    count, ot, x0, y, w_out, b_out, gain_two, bias_two, up, up_bias, down, down_bias,
    qt, k, kt, v, lse, a1t, wq, wk, wv, gain_one,
    out, din, up_out, down_out, qkv_out, out_out, vec_out,
    x1, a2, a2t, acc, dacc, out_s, dot_s, dt, din_s, dvk, grads, vec, vec_recv, vec_recv_blk,
    send_rs, recv_rs, send_ag, recv_ag, vec_sems, vec_blk_sems, move_sems, piece_sems, flush_sems, *recv,
):
    step = pl.program_id(0)
    slots, width = x0.shape
    pair = 2 * HEAD_DIM
    chunk = slots // blk
    cols_of = width // LANES
    f, z = lax.axis_index("fields"), lax.axis_index("blk")
    bits = fields.bit_length() - 1
    ff = up.shape[1]
    heads_from, heads_to = ff_steps, ff_steps + 2 * pairs
    sums = Sums(
        fields, blk, rows, 2 * ff_steps, 2 * (ff_steps + pairs), grads, recv, (send_rs, recv_rs, send_ag, recv_ag)
    )
    VEC_G1, VEC_B1, VEC_Q, VEC_V, VEC_OUT, VEC_G2, VEC_B2, VEC_DOWN, VEC_UP = range(9)

    def put_vec(index, value):
        for i in range(cols_of):
            vec[index * cols_of + i : index * cols_of + i + 1, :] = value[:, i * LANES : (i + 1) * LANES]

    def local_copy(src, dst, sem):
        return pltpu.make_async_copy(src.at[pl.ds(pl.multiple_of(z * chunk, 16), chunk)], dst.at[z], sem)

    def send_part(src, dst, s, part, size, sems):
        to = lax.rem(z + s, blk)
        return pltpu.make_async_remote_copy(
            src_ref=src.at[pl.ds(pl.multiple_of(to * chunk + part * size, 16), size)],
            dst_ref=dst.at[z, pl.ds(pl.multiple_of(part * size, 16), size)],
            send_sem=sems[0],
            recv_sem=sems[1],
            device_id=(f, to),
            device_id_type=pl.DeviceIdType.MESH,
        )

    def part_came(src, dst, s, part, size, sems):
        came = lax.rem(z + blk - s, blk)
        return pltpu.make_async_remote_copy(
            src_ref=src.at[pl.ds(0, size)],
            dst_ref=dst.at[came, pl.ds(pl.multiple_of(part * size, 16), size)],
            send_sem=sems[0],
            recv_sem=sems[1],
            device_id=(f, came),
            device_id_type=pl.DeviceIdType.MESH,
        )

    pieces = 2 * pairs // (blk - 1)

    def piece(maker, i, kind):
        sems = piece_sems.at[kind, 0, i], piece_sems.at[kind, 1, i]
        src, dst = ((out_s, out), (din_s, din))[kind]
        return maker(src, dst, blk - 1 - lax.rem(i, blk - 1), lax.div(i, blk - 1), chunk // pieces, sems)

    @pl.when(step == 0)
    def _():
        barrier = pltpu.get_barrier_semaphore()
        for b in range(bits):
            bit = lax.rem(lax.div(f, 1 << b), 2)
            pl.semaphore_signal(
                barrier, 1, device_id=(f + (1 << b) * (1 - 2 * bit), z), device_id_type=pl.DeviceIdType.MESH
            )
        for s in range(1, blk):
            pl.semaphore_signal(barrier, 1, device_id=(f, lax.rem(z + s, blk)), device_id_type=pl.DeviceIdType.MESH)
        pl.semaphore_wait(barrier, bits + blk - 1)

        for r in range(blk):
            at = slice(r * chunk, (r + 1) * chunk)
            x = x0[at, :].astype(F32) + jnp.dot(ot[:, at].T, w_out[...], preferred_element_type=F32) + row(b_out)
            x1[at, :] = x
            hat, _ = norm_parts(x)
            a = (hat * row(gain_two) + row(bias_two)).astype(BF16)
            a2[at, :] = a
            a2t[:, at] = a.T
        acc[...] = jnp.zeros_like(acc)
        dacc[...] = jnp.zeros_like(dacc)

    def flush_copies(block, proj):
        half = lax.rem(block, 2)
        got = []
        if proj:
            j = lax.div(block, 2) - ff_steps
            for i in range(2):
                at = pl.ds(pl.multiple_of((j + i * pairs) * pair, pair), pair)
                got.append((grads.at[block, pl.ds(i * width, width)], qkv_out.at[:, at]))
            at = pl.ds(pl.multiple_of((j + 2 * pairs) * pair, pair), pair)
            more = [(grads.at[block, pl.ds(0, width)], qkv_out.at[:, at])]
            at = pl.ds(pl.multiple_of(j * pair, pair), pair)
            more.append((grads.at[block, pl.ds(width, width)], out_out.at[:, at]))
        else:
            step_of = lax.div(block, 2)
            for i in range(ff // LANES):
                at = pl.ds(pl.multiple_of(step_of * ff + i * LANES, LANES), LANES)
                got.append((grads.at[block, pl.ds(i * width, width)], up_out.at[:, at]))
            at = pl.ds(pl.multiple_of(step_of * ff, ff), ff)
            more = []
            for i in range(cols_of):
                more.append((grads.at[block, pl.ds(i * ff, ff)], down_out.at[at, pl.ds(i * LANES, LANES)]))
        pick = lambda some: [pltpu.make_async_copy(a, b, flush_sems.at[block, i]) for i, (a, b) in enumerate(some)]
        return half, pick, got, more

    def flush(block, act):
        for proj in (False, True):

            @pl.when((block >= 2 * ff_steps) if proj else (block < 2 * ff_steps))
            def _():
                half, pick, got, more = flush_copies(block, proj)

                @pl.when(half == 0)
                def _():
                    for c in pick(got):
                        act(c)

                @pl.when(half == 1)
                def _():
                    for c in pick(more):
                        act(c)

    def done(block):
        flush(block, lambda c: c.start())

    first = 2 * step - 2

    @pl.when(step >= 1)
    def _():
        @pl.loop(0, 2)
        def _(i):
            sums.tick(first + i, done)

    @pl.when(step < heads_from)
    def _():
        half = slots // 2
        parts = [slice(0, half), slice(half, slots)]
        ahead = []
        for at in parts:
            h = jnp.dot(a2[at, :], up[...], preferred_element_type=F32) + row(up_bias)
            ahead.append((h, mm(y[at, :], down[...], 1, 1)))
        sum_up = d_up = d_down = 0.0
        for at, (h, dg) in zip(parts, ahead):
            phi = 0.5 + 0.5 * lax.erf(h * (0.5**0.5))
            slope = phi + h * (jnp.exp2(h * h * (-0.5 * LOG2E)) * (2 * math.pi) ** -0.5)
            g = (h * phi).astype(BF16)
            dh = (dg * slope).astype(BF16)
            acc[at, :] += jnp.dot(g, down[...], preferred_element_type=F32)
            dacc[at, :] += mm(dh, up[...], 1, 1)
            sum_up = sum_up + jnp.sum(dh.astype(F32), 0, keepdims=True)
            d_up = d_up + jnp.dot(a2t[:, at], dh, preferred_element_type=F32)
            d_down = d_down + jnp.dot(g.T, y[at, :], preferred_element_type=F32)
        d_up, d_down = d_up.astype(BF16), d_down.astype(BF16)
        for i in range(ff // LANES):
            vec[pl.ds(VEC_UP * cols_of + step * (ff // LANES) + i, 1), :] = sum_up[:, i * LANES : (i + 1) * LANES]
        for i in range(ff // LANES):
            grads[2 * step, i * width : (i + 1) * width, :] = d_up[:, i * LANES : (i + 1) * LANES]
        for i in range(cols_of):
            grads[2 * step + 1, i * ff : (i + 1) * ff, :] = d_down[:, i * LANES : (i + 1) * LANES]
        if 2 * width < rows:
            for i in range(2):
                grads[2 * step + i, 2 * width :, :] = jnp.zeros((rows - 2 * width, LANES), BF16)

    @pl.when(step == heads_from - 1)
    def _():
        totals = [jnp.zeros((1, width), F32) for _ in range(4)]
        for r in range(blk):
            at = slice(r * chunk, (r + 1) * chunk)
            grad = dacc[at, :]
            yf = y[at, :].astype(F32)
            xs = x1[at, :]
            out_s[at, :] = (xs + acc[at, :] + row(down_bias)).astype(BF16)
            hat, sc = norm_parts(xs)
            dx = yf + norm_back(grad, hat, sc, row(gain_two))
            x1[at, :] = dx
            dz = dx.astype(BF16)
            a2[at, :] = dz
            dot_s[:, at] = mm(dz, w_out[...], 1, 1).astype(BF16).T
            for i, value in enumerate((grad * hat, grad, yf, dz.astype(F32))):
                totals[i] = totals[i] + jnp.sum(value, 0, keepdims=True)
        local_copy(out_s, out, move_sems.at[0]).start()
        for index, value in zip((VEC_G2, VEC_B2, VEC_DOWN, VEC_OUT), totals):
            put_vec(index, value)
        d_out = jnp.dot(ot[...], a2[...], preferred_element_type=F32).astype(BF16)
        for j in range(pairs):
            grads[2 * (ff_steps + j) + 1, width : 2 * width, :] = d_out[:, j * pair : (j + 1) * pair]
            if 2 * width < rows:
                for i in range(2):
                    grads[2 * (ff_steps + j) + i, 2 * width :, :] = jnp.zeros((rows - 2 * width, LANES), BF16)
        dacc[...] = jnp.zeros_like(dacc)

    @pl.when((step >= heads_from) & (step < heads_to))
    def _():
        index = step - heads_from
        j, head = lax.div(index, 2), lax.rem(index, 2)

        @pl.when(index < pieces * (blk - 1))
        def _():
            piece(send_part, index, 0).start()

        c = HEAD_DIM**-0.5 * LOG2E
        scale = HEAD_DIM**-0.5
        block = 256
        lane = lax.broadcasted_iota(jnp.int32, (slots, pair), 1)
        kb = key_bias(count[z], slots)
        mine = lane // HEAD_DIM == head
        lane = lane % HEAD_DIM
        ka = jnp.where(mine, k[...], jnp.where(lane == 0, kb, jnp.where(lane < 4, 1.0, 0.0)).astype(BF16))
        va = jnp.where(mine, v[...], jnp.where(lane < 3, 1.0, 0.0).astype(BF16))
        rows_of = pl.ds(pl.multiple_of(head * HEAD_DIM, HEAD_DIM), HEAD_DIM)
        rows_all = pl.ds(pl.multiple_of(index * HEAD_DIM, HEAD_DIM), HEAD_DIM)
        do_h = dot_s[rows_all, :]
        q_h = qt[rows_of, :]
        k_h = kt[rows_of, :]
        delta = jnp.sum(do_h.astype(F32) * ot[rows_all, :].astype(F32), 0, keepdims=True)
        l3 = [t.astype(F32) for t in thirds(lse[0, pl.ds(head, 1), :] * -(HEAD_DIM**0.5))]
        d3 = [t.astype(F32) for t in thirds(-delta)]
        zeros = jnp.zeros((HEAD_DIM - 4, slots), F32)
        one = jnp.ones((1, slots), F32)
        extra_q = jnp.concatenate([one, *l3, zeros], 0).astype(BF16)
        extra_d = jnp.concatenate([*d3, zeros, 0.0 * one], 0).astype(BF16)
        upper = lax.broadcasted_iota(jnp.int32, (pair, slots), 0) // HEAD_DIM == head
        qa = jnp.where(upper, jnp.concatenate([q_h, q_h], 0), jnp.concatenate([extra_q, extra_q], 0))
        da = jnp.where(upper, jnp.concatenate([do_h, do_h], 0), jnp.concatenate([extra_d, extra_d], 0))
        def scores(i):
            at = slice(i * block, (i + 1) * block)
            return mm(ka, qa[:, at], 1, 0), mm(va, da[:, at], 1, 0)

        ready = scores(0)
        for i in range(slots // block):
            at = slice(i * block, (i + 1) * block)
            s, dp = ready
            if i + 1 < slots // block:
                ready = scores(i + 1)
            p = jnp.exp2(s * c)
            ds = (p * dp).astype(BF16)
            p = p.astype(BF16)
            dt[rows_of, at] = (mm(k_h, ds, 1, 0) * scale).astype(BF16)
            dv = mm(do_h[:, at], p, 1, 1)
            dk = mm(q_h[:, at], ds, 1, 1)
            if i == 0:
                dvk[0] = dv
                dvk[1] = dk
            else:
                dvk[0] += dv
                dvk[1] += dk
        dt[pl.ds(pl.multiple_of(pair + head * HEAD_DIM, HEAD_DIM), HEAD_DIM), :] = (dvk[1] * scale).astype(BF16)
        dt[pl.ds(pl.multiple_of(2 * pair + head * HEAD_DIM, HEAD_DIM), HEAD_DIM), :] = dvk[0].astype(BF16)

        @pl.when(head == 1)
        def _():
            d = dt[...]
            part = mm(a1t[...], d, 1, 1).astype(BF16)
            for i in range(3):
                at = slice(i % 2 * width, (i % 2 + 1) * width)
                grads[2 * (ff_steps + j) + i // 2, at, :] = part[:, i * pair : (i + 1) * pair]
            total = mm(jnp.ones((8, slots), BF16), d, 1, 1)
            vec[pl.ds(VEC_Q * cols_of + j, 1), :] = total[:1, :pair]
            vec[pl.ds(VEC_V * cols_of + j, 1), :] = total[:1, 2 * pair :]
            w = jnp.concatenate([wq[...], wk[...], wv[...]], 1)
            dacc[...] += mm(d.T, w, 1, 1)

    @pl.when(step == heads_to)
    def _():
        totals = [jnp.zeros((1, width), F32) for _ in range(2)]
        for r in range(blk):
            at = slice(r * chunk, (r + 1) * chunk)
            grad = dacc[at, :]
            hat, sc = norm_parts(x0[at, :].astype(F32))
            dn = norm_back(grad, hat, sc, row(gain_one))
            din_s[at, :] = (x1[at, :] + dn).astype(BF16)
            for i, value in enumerate((grad * hat, grad)):
                totals[i] = totals[i] + jnp.sum(value, 0, keepdims=True)
        local_copy(din_s, din, move_sems.at[1]).start()
        put_vec(VEC_G1, totals[0])
        put_vec(VEC_B1, totals[1])

    def vec_copy(b):
        bit = lax.rem(lax.div(f, 1 << b), 2)
        return pltpu.make_async_remote_copy(
            src_ref=vec,
            dst_ref=vec_recv.at[b],
            send_sem=vec_sems.at[0, b],
            recv_sem=vec_sems.at[1, b],
            device_id=(f + (1 << b) * (1 - 2 * bit), z),
            device_id_type=pl.DeviceIdType.MESH,
        )

    def vec_blk_copy(s):
        return pltpu.make_async_remote_copy(
            src_ref=vec,
            dst_ref=vec_recv_blk.at[s - 1],
            send_sem=vec_blk_sems.at[0, s - 1],
            recv_sem=vec_blk_sems.at[1, s - 1],
            device_id=(f, lax.rem(z + s, blk)),
            device_id_type=pl.DeviceIdType.MESH,
        )

    @pl.when(step == heads_to)
    def _():
        @pl.loop(2, tail)
        def _(i):
            sums.tick(first + i, done)
            turn = lax.div(i - 2, DIN_EVERY)

            @pl.when((lax.rem(i - 2, DIN_EVERY) == 0) & (turn < pieces * (blk - 1)))
            def _():
                piece(send_part, turn, 1).start()

            for b in range(bits + 2):

                @pl.when(i == 2 + 2 * b)
                def _():
                    if 1 <= b <= bits:
                        vec_copy(b - 1).wait()
                        vec[...] += vec_recv[b - 1]
                    if b < bits:
                        vec_copy(b).start()
                    elif b == bits:
                        for s in range(1, blk):
                            vec_blk_copy(s).start()
                    else:
                        for s in range(1, blk):
                            vec_blk_copy(s).wait()
                        total = vec[...]
                        for s in range(1, blk):
                            total = total + vec_recv_blk[s - 1]
                        vec_out[...] = total

        @pl.loop(0, pieces * (blk - 1))
        def _(i):
            for kind in range(2):
                piece(send_part, i, kind).wait_send()
                piece(part_came, i, kind).wait_recv()

        local_copy(out_s, out, move_sems.at[0]).wait()
        local_copy(din_s, din, move_sems.at[1]).wait()

        @pl.loop(0, sums.count)
        def _(block):
            flush(block, lambda c: c.wait())


def mega(mesh_shape, count, ot, x0, y, w_out, b_out, gain_two, bias_two, up, up_bias, down, down_bias,
         qt, k, kt, v, lse, a1t, w_qkv, gain_one, ff_block=256):
    fields, blk = mesh_shape
    slots, width = x0.shape
    pair = 2 * HEAD_DIM
    pairs = width // pair
    ff_steps = up.shape[1] // ff_block
    bits = fields.bit_length() - 1
    n = fields * blk
    assert ff_block == 2 * LANES
    rows = -(-2 * width // (16 * n)) * 16 * n
    blocks = 2 * (ff_steps + pairs)
    levels = n.bit_length() - 1
    heads_to = ff_steps + 2 * pairs
    last_tick = 2 * ff_steps + 2 + 2 * (2 * pairs - 1) + offsets(bits, levels - bits)[-1]
    tail = last_tick + 1 - (2 * heads_to - 2)
    vec_rows = (8 + up.shape[1] // width) * (width // LANES)
    chunk = slots // blk
    cols_of = width // LANES

    def ff_at(i):
        return jnp.minimum(i, ff_steps - 1)

    def pair_at(i):
        return jnp.clip((i - ff_steps) // 2, 0, pairs - 1)

    tra = pl.BlockSpec((pair, slots), lambda i: (pair_at(i), 0))
    nat = pl.BlockSpec((slots, pair), lambda i: (0, pair_at(i)))

    def cols(part):
        return pl.BlockSpec((width, pair), lambda i: (0, part * pairs + pair_at(i)))

    hbm = pl.BlockSpec(memory_space=pl.ANY)
    one = (width,)
    dma = pltpu.SemaphoreType.DMA
    ahead = SLOTS_AHEAD
    flops = 12 * slots * width * up.shape[1] + 10 * slots * slots * width + 12 * slots * width * width
    return pl.pallas_call(
        partial(mega_kernel, fields, blk, rows, ff_steps, pairs, tail),
        grid=(heads_to + 1,),
        in_specs=[
            pl.BlockSpec(memory_space=pltpu.SMEM),
            whole((width, slots)),
            whole((slots, width)),
            whole((slots, width)),
            whole((width, width)),
            whole(one),
            whole(one),
            whole(one),
            pl.BlockSpec((width, ff_block), lambda i: (0, ff_at(i))),
            pl.BlockSpec((ff_block,), lambda i: (ff_at(i),)),
            pl.BlockSpec((ff_block, width), lambda i: (ff_at(i), 0)),
            whole(one),
            tra, nat, tra, nat,
            pl.BlockSpec((1, 2, slots), lambda i: (pair_at(i), 0, 0)),
            whole((width, slots)),
            cols(0), cols(1), cols(2),
            whole(one),
        ],
        out_specs=[hbm, hbm, hbm, hbm, hbm, hbm, whole((vec_rows, LANES))],
        out_shape=[
            jax.ShapeDtypeStruct((blk, chunk, width), BF16),
            jax.ShapeDtypeStruct((blk, chunk, width), BF16),
            jax.ShapeDtypeStruct((width, up.shape[1]), BF16),
            jax.ShapeDtypeStruct((up.shape[1], width), BF16),
            jax.ShapeDtypeStruct((width, 3 * width), BF16),
            jax.ShapeDtypeStruct((width, width), BF16),
            jax.ShapeDtypeStruct((vec_rows, LANES), F32),
        ],
        scratch_shapes=[
            pltpu.VMEM((slots, width), F32),
            pltpu.VMEM((slots, width), BF16),
            pltpu.VMEM((width, slots), BF16),
            pltpu.VMEM((slots, width), F32),
            pltpu.VMEM((slots, width), F32),
            pltpu.VMEM((slots, width), BF16),
            pltpu.VMEM((width, slots), BF16),
            pltpu.VMEM((3 * pair, slots), BF16),
            pltpu.VMEM((slots, width), BF16),
            pltpu.VMEM((2, HEAD_DIM, slots), F32),
            pltpu.VMEM((blocks, rows, LANES), BF16),
            pltpu.VMEM((vec_rows, LANES), F32),
            pltpu.VMEM((bits, vec_rows, LANES), F32),
            pltpu.VMEM((blk - 1, vec_rows, LANES), F32),
            dma((levels, ahead)),
            dma((levels, ahead)),
            dma((levels, ahead)),
            dma((levels, ahead)),
            dma((2, bits)),
            dma((2, blk - 1)),
            dma((2,)),
            dma((2, 2, 2 * pairs)),
            dma((blocks, cols_of)),
            *[pltpu.VMEM((2, ahead, rows >> (s + 1), LANES), BF16) for s in range(levels)],
        ],
        compiler_params=pltpu.CompilerParams(
            vmem_limit_bytes=67_000_000, collective_id=0, has_side_effects=True
        ),
        cost_estimate=pl.CostEstimate(flops=flops, bytes_accessed=60 * slots * width, transcendentals=0),
        name="mega",
    )(
        count, ot, x0, y, w_out, b_out, gain_two, bias_two, up, up_bias, down, down_bias,
        qt, k, kt, v, lse, a1t, w_qkv, w_qkv, w_qkv, gain_one,
    )


def widen(arrays, vecs, lengths, steps):
    count = len(arrays)

    def kernel(*refs):
        for src, dst in zip(refs[:count], refs[count + 1 : 2 * count + 1]):
            dst[...] = src[...].astype(F32)

        @pl.when(pl.program_id(0) == 0)
        def _():
            at = 0
            for dst, length in zip(refs[2 * count + 1 :], lengths):
                for i in range(length // LANES):
                    dst[i * LANES : (i + 1) * LANES] = refs[count][at + i, :]
                at += length // LANES

    specs = [pl.BlockSpec((a.shape[0] // steps, a.shape[1]), lambda i: (i, 0)) for a in arrays]
    return pl.pallas_call(
        kernel,
        grid=(steps,),
        in_specs=[*specs, whole(vecs.shape)],
        out_specs=[*specs, *[whole((n,)) for n in lengths]],
        out_shape=[
            *[jax.ShapeDtypeStruct(a.shape, F32) for a in arrays],
            *[jax.ShapeDtypeStruct((n,), F32) for n in lengths],
        ],
        compiler_params=pltpu.CompilerParams(vmem_limit_bytes=VMEM_BYTES),
        name="widen",
    )(*arrays, vecs)


def to_field(part):
    return lax.all_to_all(part, "blk", 0, 1, tiled=True)[0]


def per_device(
    mesh_shape, tokens, keep_index, counts, norm1_gain, norm1_bias, qkv_weight, query_bias, value_bias, out_weight,
    out_bias, norm2_gain, norm2_bias, up_weight, up_bias, down_weight, down_bias, cotangent,
):
    width = tokens.shape[2]
    x0 = place(mesh_shape[1], tokens, keep_index)
    a1t, qt, k, kt, v, vt = project(x0, norm1_gain, norm1_bias, qkv_weight, query_bias, value_bias)
    _, later = lax.optimization_barrier((x0, cotangent))
    y = to_field(later)
    _, ot, lse = attend(counts, qt, k, vt)
    output, input_grad, d_up, d_down, d_qkv, d_out, vecs = mega(
        mesh_shape, counts, ot, x0, y, out_weight, out_bias, norm2_gain, norm2_bias, up_weight, up_bias, down_weight,
        down_bias, qt, k, kt, v, lse, a1t, qkv_weight, norm1_gain,
    )
    lengths = [width] * 8 + [up_weight.shape[1]]
    d_up, d_down, d_qkv, d_out, *vec = widen((d_up, d_down, d_qkv, d_out), vecs, lengths, 6)
    return (
        output,
        input_grad,
        vec[0],
        vec[1],
        d_qkv,
        vec[2],
        vec[3],
        d_out,
        vec[4],
        vec[5],
        vec[6],
        d_up,
        vec[8],
        d_down,
        vec[7],
    )


def solution(mesh):
    rows = P("fields", "blk", None)
    return jax.shard_map(
        partial(per_device, (mesh.shape["fields"], mesh.shape["blk"])),
        mesh=mesh,
        in_specs=(rows, P("fields", "blk"), P("fields"), *[P()] * 13, rows),
        out_specs=(rows, rows, *[P()] * 13),
        check_vma=False,
    )
```

```python
from functools import partial
import math
import jax
import jax.numpy as jnp
import ml_dtypes
import numpy as np
from jax import lax
from jax.experimental import pallas as pl
from jax.experimental.pallas import tpu as pltpu
from jax.sharding import PartitionSpec as P

HEAD_DIM = 64
GRID_W = 64
PATCHES = 2048
epsilon = 1e-06
negative = -1e30
VMEM_BYTES = 60 * 1024 * 1024
LOG2E = math.log2(math.e)
F32 = jnp.float32
BF16 = jnp.bfloat16


def mm(a, b, ca, cb):
    return lax.dot_general(a, b, (((ca,), (cb,)), ((), ())), preferred_element_type=F32)


def row(ref):
    return ref[...].astype(F32)[None]


def whole(shape):
    return pl.BlockSpec(shape, lambda *_: (0,) * len(shape), pipeline_mode=pl.Buffered(1))


def norm_parts(values):
    centre = jnp.mean(values, -1, keepdims=True)
    centred = values - centre
    spread = jnp.mean(centred * centred, -1, keepdims=True)
    scale = lax.rsqrt(spread + epsilon)
    return centred * scale, scale


def norm_back(grad, hat, scale, gain):
    scaled = grad * gain
    return scale * (
        scaled
        - jnp.mean(scaled, -1, keepdims=True)
        - hat * jnp.mean(scaled * hat, -1, keepdims=True)
    )


def thirds(row):
    high = row.astype(BF16)
    rest = row - high.astype(F32)
    mid = rest.astype(BF16)
    low = (rest - mid.astype(F32)).astype(BF16)
    return high, mid, low


def tables(width):
    quarter = width // 4
    omega = 1.0 / 10000.0 ** (np.arange(quarter) / quarter)

    def table(length):
        ang = np.arange(length)[:, None] * omega
        rest = np.concatenate([np.sin(ang), np.cos(ang)], -1).astype(np.float32)
        parts = []
        for _ in range(3):
            parts.append(rest.astype(ml_dtypes.bfloat16))
            rest = rest - parts[-1].astype(np.float32)
        return jnp.asarray(np.concatenate(parts, 0))

    return table(PATCHES // GRID_W), table(GRID_W)


def place_kernel(blk, tok, keep, row_table, col_table, x0, placed, sems):
    slots = tok.shape[1]
    f, z = lax.axis_index("fields"), lax.axis_index("blk")
    barrier = pltpu.get_barrier_semaphore()
    for s in range(1, blk):
        pl.semaphore_signal(barrier, 1, device_id=(f, lax.rem(z + s, blk)), device_id_type=pl.DeviceIdType.MESH)
    pl.semaphore_wait(barrier, blk - 1)

    def copy(s):
        to = lax.rem(z + s, blk)
        return pltpu.make_async_remote_copy(
            src_ref=placed.at[to],
            dst_ref=x0.at[z],
            send_sem=sems.at[0, s],
            recv_sem=sems.at[1, s],
            device_id=(f, to),
            device_id_type=pl.DeviceIdType.MESH,
        )

    def came(s):
        source = lax.rem(z + blk - s, blk)
        return pltpu.make_async_remote_copy(
            src_ref=placed.at[source],
            dst_ref=x0.at[source],
            send_sem=sems.at[0, s],
            recv_sem=sems.at[1, s],
            device_id=(f, source),
            device_id_type=pl.DeviceIdType.MESH,
        )

    for s in range(blk - 1, -1, -1):
        to = lax.rem(z + s, blk)
        patch = keep[pl.ds(to, 1), :]
        parts = []
        for table, of in ((row_table, lax.div(patch, GRID_W)), (col_table, lax.rem(patch, GRID_W))):
            size = table.shape[0] // 3
            index = lax.broadcasted_iota(jnp.int32, (size, slots), 0)
            hot = jnp.where(index == of, 1.0, 0.0).astype(BF16)
            hot = jnp.concatenate([hot, hot, hot], 0).T
            parts.append(jnp.dot(hot, table[...], preferred_element_type=F32))
        here = (tok[to].astype(F32) + jnp.concatenate(parts, -1)).astype(BF16)
        if s > 0:
            placed[to] = here
            copy(s).start()
        else:
            x0[z] = here
    for s in range(blk - 1, 0, -1):
        copy(s).wait_send()
        came(s).wait_recv()


def place(blk, tokens, keep):
    fields, slots, width = tokens.shape
    row_table, col_table = tables(width)
    vmem = pl.BlockSpec(memory_space=pltpu.VMEM)
    return pl.pallas_call(
        partial(place_kernel, blk),
        in_specs=[vmem] * 4,
        out_specs=vmem,
        out_shape=jax.ShapeDtypeStruct(tokens.shape, BF16),
        scratch_shapes=[pltpu.VMEM(tokens.shape, BF16), pltpu.SemaphoreType.DMA((2, blk))],
        compiler_params=pltpu.CompilerParams(collective_id=1, has_side_effects=True),
        name="place",
    )(tokens, keep, row_table, col_table).reshape(fields * slots, width)


def project_kernel(x0, gain, bias, weight, qb, vb, a1t, qt, k, kt, v, vt):
    width = x0.shape[1]
    hat, _ = norm_parts(x0[...].astype(F32))
    a = (hat * row(gain) + row(bias)).astype(BF16)
    a1t[...] = a.T
    q = (jnp.dot(a, weight[:, :width], preferred_element_type=F32) + row(qb)).astype(BF16)
    qt[...] = q.T
    kk = jnp.dot(a, weight[:, width : 2 * width], preferred_element_type=F32).astype(BF16)
    k[...] = kk
    kt[...] = kk.T
    vv = (jnp.dot(a, weight[:, 2 * width :], preferred_element_type=F32) + row(vb)).astype(BF16)
    v[...] = vv
    vt[...] = vv.T


def project(x0, gain, bias, weight, qb, vb, block=256):
    slots, width = x0.shape
    nat = pl.BlockSpec((block, width), lambda i: (i, 0))
    tra = pl.BlockSpec((width, block), lambda i: (0, i))
    sn = jax.ShapeDtypeStruct((slots, width), BF16)
    st = jax.ShapeDtypeStruct((width, slots), BF16)
    one = whole((width,))
    return pl.pallas_call(
        project_kernel,
        grid=(slots // block,),
        in_specs=[nat, one, one, whole(weight.shape), one, one],
        out_specs=[tra, tra, nat, tra, nat, tra],
        out_shape=[st, st, sn, st, sn, st],
        compiler_params=pltpu.CompilerParams(vmem_limit_bytes=VMEM_BYTES),
        cost_estimate=pl.CostEstimate(flops=2 * slots * width * 3 * width, bytes_accessed=20 * slots * width, transcendentals=0),
        name="project",
    )(x0, gain, bias, weight, qb, vb)


def augment_cols(block, extra, second):
    lane = lax.broadcasted_iota(jnp.int32, block.shape, 1)
    return jnp.where((lane >= HEAD_DIM) if second else (lane < HEAD_DIM), block, extra)


def augment_rows(block, extra, second):
    if second:
        return jnp.concatenate([extra, block[HEAD_DIM:]], 0)
    return jnp.concatenate([block[:HEAD_DIM], extra], 0)


def key_bias(count, slots):
    return jnp.where(lax.broadcasted_iota(jnp.int32, (slots, 1), 0) < count, 0.0, negative)


def attend_kernel(block, count, qt, k, vt, o, ot, lse):
    slots = k.shape[0]
    c = HEAD_DIM**-0.5 * LOG2E
    lane = lax.broadcasted_iota(jnp.int32, (slots, 2 * HEAD_DIM), 1)
    kb = key_bias(count[lax.axis_index("blk")], slots)
    extra_col = jnp.where(lane % HEAD_DIM == 0, kb, 0.0).astype(BF16)
    sub = lax.broadcasted_iota(jnp.int32, (HEAD_DIM, block), 0)
    extra_row = jnp.where(sub == 0, 1.0, 0.0).astype(BF16)
    subv = lax.broadcasted_iota(jnp.int32, (16, slots), 0)
    ones = jnp.where(subv == 0, 1.0, 0.0).astype(BF16)
    work = []
    for head in range(2):
        ka = augment_cols(k[...], extra_col, head == 1)
        va = jnp.concatenate([vt[head * HEAD_DIM : (head + 1) * HEAD_DIM, :], ones], 0)
        for i in range(slots // block):
            work.append((head, ka, va, slice(i * block, (i + 1) * block)))

    def scores(item):
        head, ka, _, cols = item
        return mm(ka, augment_rows(qt[:, cols], extra_row, head == 1), 1, 0)

    s = scores(work[0])
    for n, (head, _, va, cols) in enumerate(work):
        later = scores(work[n + 1]) if n + 1 < len(work) else None
        top = jnp.max(s, 0, keepdims=True)
        p = jnp.exp2((s - top) * c).astype(BF16)
        r = mm(va, p, 1, 0)
        total = r[HEAD_DIM : HEAD_DIM + 1]
        mixed = (r[:HEAD_DIM] / total).astype(BF16)
        ot[head * HEAD_DIM : (head + 1) * HEAD_DIM, cols] = mixed
        lse[0, head : head + 1, cols] = top * HEAD_DIM**-0.5 + jnp.log(total)
        s = later
    o[...] = ot[...].T


def attend(count, qt, k, vt, block=512):
    slots, width = k.shape
    pairs = width // (2 * HEAD_DIM)
    tra = pl.BlockSpec((2 * HEAD_DIM, slots), lambda j: (j, 0))
    nat = pl.BlockSpec((slots, 2 * HEAD_DIM), lambda j: (0, j))
    return pl.pallas_call(
        partial(attend_kernel, block),
        grid=(pairs,),
        in_specs=[pl.BlockSpec(memory_space=pltpu.SMEM), tra, nat, tra],
        out_specs=[nat, tra, pl.BlockSpec((1, 2, slots), lambda j: (j, 0, 0))],
        out_shape=[
            jax.ShapeDtypeStruct((slots, width), BF16),
            jax.ShapeDtypeStruct((width, slots), BF16),
            jax.ShapeDtypeStruct((pairs, 2, slots), F32),
        ],
        compiler_params=pltpu.CompilerParams(vmem_limit_bytes=VMEM_BYTES),
        cost_estimate=pl.CostEstimate(flops=16 * slots * slots * width, bytes_accessed=12 * slots * width, transcendentals=slots * slots * 12),
        name="attend",
    )(count, qt, k, vt)


SLOTS_AHEAD = 10
LANES = 128
LAG_CORE, LAG_XY, LAG_Z = 2, 4, 4
DIN_EVERY = 2


def offsets(near, far):
    lags = [LAG_CORE] + [LAG_XY] * (near - 1) + [LAG_Z] * far
    ticks = [0]
    for lag in lags + lags[::-1]:
        ticks.append(ticks[-1] + lag)
    return ticks


class Sums:
    def __init__(self, fields, blk, rows, early, count, grads, recv, sems):
        self.rows, self.early, self.count = rows, early, count
        self.near, self.far = fields.bit_length() - 1, blk.bit_length() - 1
        self.bits = self.near + self.far
        self.grads, self.recv = grads, recv
        self.send_rs, self.recv_rs, self.send_ag, self.recv_ag = sems
        self.f, self.z = lax.axis_index("fields"), lax.axis_index("blk")
        self.actions = 2 * self.bits + 1
        self.own = [lax.rem(lax.div(self.f, 1 << k), 2) for k in range(self.near)]
        self.own += [lax.rem(lax.div(self.z, 1 << k), 2) for k in range(self.far)]

    def route(self, odd):
        keep, route = 0, []
        for stage in range(self.bits):
            bit = self.own[stage]
            if stage < self.near:
                other = stage if stage == 0 else self.near - stage
                bit = bit + odd * (self.own[other] - bit)
                width = (1 << stage) + odd * ((1 << other) - (1 << stage))
                partner = (self.f + width * (1 - 2 * bit), self.z)
            else:
                partner = (self.f, self.z + (1 << (stage - self.near)) * (1 - 2 * bit))
            size = self.rows >> (stage + 1)
            route.append((partner, keep + bit * size, keep + (1 - bit) * size))
            keep = keep + bit * size
        return route

    def copy(self, gather, block, slot, route, stage):
        partner, kept, sent = route[stage]
        part = pl.ds(pl.multiple_of(kept if gather else sent, 16), self.rows >> (stage + 1))
        send, recv = (self.send_ag, self.recv_ag) if gather else (self.send_rs, self.recv_rs)
        return pltpu.make_async_remote_copy(
            src_ref=self.grads.at[block, part],
            dst_ref=self.recv[stage].at[gather, slot],
            send_sem=send.at[stage, slot],
            recv_sem=recv.at[stage, slot],
            device_id=partner,
            device_id_type=pl.DeviceIdType.MESH,
        )

    def take(self, gather, block, slot, route, stage):
        size = self.rows >> (stage + 1)
        off = route[stage][2 if gather else 1]
        chunk = size
        while chunk > 384 or size % chunk:
            chunk -= 16
        came = self.recv[stage]

        @pl.loop(0, size // chunk)
        def _(i):
            at = pl.ds(pl.multiple_of(off + i * chunk, 16), chunk)
            got = came[gather, slot, pl.ds(pl.multiple_of(i * chunk, 16), chunk), :]
            self.grads[block, at, :] = got if gather else self.grads[block, at, :] + got

    def act(self, kind, block, slot, route):
        bits = self.bits
        if kind > 0:
            gather = int(kind > bits)
            stage = 2 * bits - kind if gather else kind - 1
            self.copy(gather, block, slot, route, stage).wait()
            self.take(gather, block, slot, route, stage)
        if kind < 2 * bits:
            gather = int(kind >= bits)
            self.copy(gather, block, slot, route, 2 * bits - 1 - kind if gather else kind).start()

    def tick(self, tick, done):
        routes = {}
        for odd_offset in (0, 1):
            turn = lax.rem(lax.div(tick + odd_offset, 2), 2)
            routes[odd_offset] = self.route(turn), self.route(1 - turn)
        for kind, offset in enumerate(offsets(self.near, self.far)):
            entry = tick - offset
            late = entry - self.early - 2
            block = jnp.where(late >= 0, self.early + lax.div(late, 2), entry)
            runs = jnp.where(late >= 0, (lax.rem(late, 2) == 0) & (block < self.count), (entry >= 0) & (entry < self.early))
            route = routes[offset % 2][(offset + 1) // 2 % 2]

            @pl.when(runs)
            def _():
                self.act(kind, block, lax.rem(block, SLOTS_AHEAD), route)
                if kind == self.actions - 1:
                    done(block)


def mega_kernel(
    fields, blk, rows, ff_steps, pairs, tail,
    count, ot, x0, y, w_out, b_out, gain_two, bias_two, up, up_bias, down, down_bias,
    qt, k, kt, v, lse, a1t, wq, wk, wv, gain_one,
    out, din, up_out, down_out, qkv_out, out_out, vec_out,
    x1, a2, a2t, acc, dacc, out_s, dot_s, dt, din_s, dvk, grads, vec, vec_recv, vec_recv_blk,
    send_rs, recv_rs, send_ag, recv_ag, vec_sems, vec_blk_sems, move_sems, piece_sems, flush_sems, *recv,
):
    step = pl.program_id(0)
    slots, width = x0.shape
    pair = 2 * HEAD_DIM
    chunk = slots // blk
    cols_of = width // LANES
    f, z = lax.axis_index("fields"), lax.axis_index("blk")
    bits = fields.bit_length() - 1
    ff = up.shape[1]
    heads_from, heads_to = ff_steps, ff_steps + 2 * pairs
    sums = Sums(
        fields, blk, rows, 2 * ff_steps, 2 * (ff_steps + pairs), grads, recv, (send_rs, recv_rs, send_ag, recv_ag)
    )
    VEC_G1, VEC_B1, VEC_Q, VEC_V, VEC_OUT, VEC_G2, VEC_B2, VEC_DOWN, VEC_UP = range(9)

    def put_vec(index, value):
        for i in range(cols_of):
            vec[index * cols_of + i : index * cols_of + i + 1, :] = value[:, i * LANES : (i + 1) * LANES]

    def local_copy(src, dst, sem):
        return pltpu.make_async_copy(src.at[pl.ds(pl.multiple_of(z * chunk, 16), chunk)], dst.at[z], sem)

    def send_part(src, dst, s, part, size, sems):
        to = lax.rem(z + s, blk)
        return pltpu.make_async_remote_copy(
            src_ref=src.at[pl.ds(pl.multiple_of(to * chunk + part * size, 16), size)],
            dst_ref=dst.at[z, pl.ds(pl.multiple_of(part * size, 16), size)],
            send_sem=sems[0],
            recv_sem=sems[1],
            device_id=(f, to),
            device_id_type=pl.DeviceIdType.MESH,
        )

    def part_came(src, dst, s, part, size, sems):
        came = lax.rem(z + blk - s, blk)
        return pltpu.make_async_remote_copy(
            src_ref=src.at[pl.ds(0, size)],
            dst_ref=dst.at[came, pl.ds(pl.multiple_of(part * size, 16), size)],
            send_sem=sems[0],
            recv_sem=sems[1],
            device_id=(f, came),
            device_id_type=pl.DeviceIdType.MESH,
        )

    pieces = 2 * pairs // (blk - 1)

    def piece(maker, i, kind):
        sems = piece_sems.at[kind, 0, i], piece_sems.at[kind, 1, i]
        src, dst = ((out_s, out), (din_s, din))[kind]
        return maker(src, dst, blk - 1 - lax.rem(i, blk - 1), lax.div(i, blk - 1), chunk // pieces, sems)

    @pl.when(step == 0)
    def _():
        barrier = pltpu.get_barrier_semaphore()
        for b in range(bits):
            bit = lax.rem(lax.div(f, 1 << b), 2)
            pl.semaphore_signal(
                barrier, 1, device_id=(f + (1 << b) * (1 - 2 * bit), z), device_id_type=pl.DeviceIdType.MESH
            )
        for s in range(1, blk):
            pl.semaphore_signal(barrier, 1, device_id=(f, lax.rem(z + s, blk)), device_id_type=pl.DeviceIdType.MESH)
        pl.semaphore_wait(barrier, bits + blk - 1)

        for r in range(blk):
            at = slice(r * chunk, (r + 1) * chunk)
            x = x0[at, :].astype(F32) + jnp.dot(ot[:, at].T, w_out[...], preferred_element_type=F32) + row(b_out)
            x1[at, :] = x
            hat, _ = norm_parts(x)
            a = (hat * row(gain_two) + row(bias_two)).astype(BF16)
            a2[at, :] = a
            a2t[:, at] = a.T
        acc[...] = jnp.zeros_like(acc)
        dacc[...] = jnp.zeros_like(dacc)

    def flush_copies(block, proj):
        half = lax.rem(block, 2)
        got = []
        if proj:
            j = lax.div(block, 2) - ff_steps
            for i in range(2):
                at = pl.ds(pl.multiple_of((j + i * pairs) * pair, pair), pair)
                got.append((grads.at[block, pl.ds(i * width, width)], qkv_out.at[:, at]))
            at = pl.ds(pl.multiple_of((j + 2 * pairs) * pair, pair), pair)
            more = [(grads.at[block, pl.ds(0, width)], qkv_out.at[:, at])]
            at = pl.ds(pl.multiple_of(j * pair, pair), pair)
            more.append((grads.at[block, pl.ds(width, width)], out_out.at[:, at]))
        else:
            step_of = lax.div(block, 2)
            for i in range(ff // LANES):
                at = pl.ds(pl.multiple_of(step_of * ff + i * LANES, LANES), LANES)
                got.append((grads.at[block, pl.ds(i * width, width)], up_out.at[:, at]))
            at = pl.ds(pl.multiple_of(step_of * ff, ff), ff)
            more = []
            for i in range(cols_of):
                more.append((grads.at[block, pl.ds(i * ff, ff)], down_out.at[at, pl.ds(i * LANES, LANES)]))
        pick = lambda some: [pltpu.make_async_copy(a, b, flush_sems.at[block, i]) for i, (a, b) in enumerate(some)]
        return half, pick, got, more

    def flush(block, act):
        for proj in (False, True):

            @pl.when((block >= 2 * ff_steps) if proj else (block < 2 * ff_steps))
            def _():
                half, pick, got, more = flush_copies(block, proj)

                @pl.when(half == 0)
                def _():
                    for c in pick(got):
                        act(c)

                @pl.when(half == 1)
                def _():
                    for c in pick(more):
                        act(c)

    def done(block):
        flush(block, lambda c: c.start())

    first = 2 * step - 2

    @pl.when(step >= 1)
    def _():
        @pl.loop(0, 2)
        def _(i):
            sums.tick(first + i, done)

    @pl.when(step < heads_from)
    def _():
        half = slots // 2
        parts = [slice(0, half), slice(half, slots)]
        ahead = []
        for at in parts:
            h = jnp.dot(a2[at, :], up[...], preferred_element_type=F32) + row(up_bias)
            ahead.append((h, mm(y[at, :], down[...], 1, 1)))
        sum_up = d_up = d_down = 0.0
        for at, (h, dg) in zip(parts, ahead):
            phi = 0.5 + 0.5 * lax.erf(h * (0.5**0.5))
            slope = phi + h * (jnp.exp2(h * h * (-0.5 * LOG2E)) * (2 * math.pi) ** -0.5)
            g = (h * phi).astype(BF16)
            dh = (dg * slope).astype(BF16)
            acc[at, :] += jnp.dot(g, down[...], preferred_element_type=F32)
            dacc[at, :] += mm(dh, up[...], 1, 1)
            sum_up = sum_up + jnp.sum(dh.astype(F32), 0, keepdims=True)
            d_up = d_up + jnp.dot(a2t[:, at], dh, preferred_element_type=F32)
            d_down = d_down + jnp.dot(g.T, y[at, :], preferred_element_type=F32)
        d_up, d_down = d_up.astype(BF16), d_down.astype(BF16)
        for i in range(ff // LANES):
            vec[pl.ds(VEC_UP * cols_of + step * (ff // LANES) + i, 1), :] = sum_up[:, i * LANES : (i + 1) * LANES]
        for i in range(ff // LANES):
            grads[2 * step, i * width : (i + 1) * width, :] = d_up[:, i * LANES : (i + 1) * LANES]
        for i in range(cols_of):
            grads[2 * step + 1, i * ff : (i + 1) * ff, :] = d_down[:, i * LANES : (i + 1) * LANES]
        if 2 * width < rows:
            for i in range(2):
                grads[2 * step + i, 2 * width :, :] = jnp.zeros((rows - 2 * width, LANES), BF16)

    @pl.when(step == heads_from - 1)
    def _():
        totals = [jnp.zeros((1, width), F32) for _ in range(4)]
        for r in range(blk):
            at = slice(r * chunk, (r + 1) * chunk)
            grad = dacc[at, :]
            yf = y[at, :].astype(F32)
            xs = x1[at, :]
            out_s[at, :] = (xs + acc[at, :] + row(down_bias)).astype(BF16)
            hat, sc = norm_parts(xs)
            dx = yf + norm_back(grad, hat, sc, row(gain_two))
            x1[at, :] = dx
            dz = dx.astype(BF16)
            a2[at, :] = dz
            dot_s[:, at] = mm(dz, w_out[...], 1, 1).astype(BF16).T
            for i, value in enumerate((grad * hat, grad, yf, dz.astype(F32))):
                totals[i] = totals[i] + jnp.sum(value, 0, keepdims=True)
        local_copy(out_s, out, move_sems.at[0]).start()
        for index, value in zip((VEC_G2, VEC_B2, VEC_DOWN, VEC_OUT), totals):
            put_vec(index, value)
        d_out = jnp.dot(ot[...], a2[...], preferred_element_type=F32).astype(BF16)
        for j in range(pairs):
            grads[2 * (ff_steps + j) + 1, width : 2 * width, :] = d_out[:, j * pair : (j + 1) * pair]
            if 2 * width < rows:
                for i in range(2):
                    grads[2 * (ff_steps + j) + i, 2 * width :, :] = jnp.zeros((rows - 2 * width, LANES), BF16)
        dacc[...] = jnp.zeros_like(dacc)

    @pl.when((step >= heads_from) & (step < heads_to))
    def _():
        index = step - heads_from
        j, head = lax.div(index, 2), lax.rem(index, 2)

        @pl.when(index < pieces * (blk - 1))
        def _():
            piece(send_part, index, 0).start()

        c = HEAD_DIM**-0.5 * LOG2E
        scale = HEAD_DIM**-0.5
        block = 256
        lane = lax.broadcasted_iota(jnp.int32, (slots, pair), 1)
        kb = key_bias(count[z], slots)
        mine = lane // HEAD_DIM == head
        lane = lane % HEAD_DIM
        ka = jnp.where(mine, k[...], jnp.where(lane == 0, kb, jnp.where(lane < 4, 1.0, 0.0)).astype(BF16))
        va = jnp.where(mine, v[...], jnp.where(lane < 3, 1.0, 0.0).astype(BF16))
        rows_of = pl.ds(pl.multiple_of(head * HEAD_DIM, HEAD_DIM), HEAD_DIM)
        rows_all = pl.ds(pl.multiple_of(index * HEAD_DIM, HEAD_DIM), HEAD_DIM)
        do_h = dot_s[rows_all, :]
        q_h = qt[rows_of, :]
        k_h = kt[rows_of, :]
        delta = jnp.sum(do_h.astype(F32) * ot[rows_all, :].astype(F32), 0, keepdims=True)
        l3 = [t.astype(F32) for t in thirds(lse[0, pl.ds(head, 1), :] * -(HEAD_DIM**0.5))]
        d3 = [t.astype(F32) for t in thirds(-delta)]
        zeros = jnp.zeros((HEAD_DIM - 4, slots), F32)
        one = jnp.ones((1, slots), F32)
        extra_q = jnp.concatenate([one, *l3, zeros], 0).astype(BF16)
        extra_d = jnp.concatenate([*d3, zeros, 0.0 * one], 0).astype(BF16)
        upper = lax.broadcasted_iota(jnp.int32, (pair, slots), 0) // HEAD_DIM == head
        qa = jnp.where(upper, jnp.concatenate([q_h, q_h], 0), jnp.concatenate([extra_q, extra_q], 0))
        da = jnp.where(upper, jnp.concatenate([do_h, do_h], 0), jnp.concatenate([extra_d, extra_d], 0))
        def scores(i):
            at = slice(i * block, (i + 1) * block)
            return mm(ka, qa[:, at], 1, 0), mm(va, da[:, at], 1, 0)

        ready = scores(0)
        for i in range(slots // block):
            at = slice(i * block, (i + 1) * block)
            s, dp = ready
            if i + 1 < slots // block:
                ready = scores(i + 1)
            p = jnp.exp2(s * c)
            ds = (p * dp).astype(BF16)
            p = p.astype(BF16)
            dt[rows_of, at] = (mm(k_h, ds, 1, 0) * scale).astype(BF16)
            dv = mm(do_h[:, at], p, 1, 1)
            dk = mm(q_h[:, at], ds, 1, 1)
            if i == 0:
                dvk[0] = dv
                dvk[1] = dk
            else:
                dvk[0] += dv
                dvk[1] += dk
        dt[pl.ds(pl.multiple_of(pair + head * HEAD_DIM, HEAD_DIM), HEAD_DIM), :] = (dvk[1] * scale).astype(BF16)
        dt[pl.ds(pl.multiple_of(2 * pair + head * HEAD_DIM, HEAD_DIM), HEAD_DIM), :] = dvk[0].astype(BF16)

        @pl.when(head == 1)
        def _():
            d = dt[...]
            part = mm(a1t[...], d, 1, 1).astype(BF16)
            for i in range(3):
                at = slice(i % 2 * width, (i % 2 + 1) * width)
                grads[2 * (ff_steps + j) + i // 2, at, :] = part[:, i * pair : (i + 1) * pair]
            total = mm(jnp.ones((8, slots), BF16), d, 1, 1)
            vec[pl.ds(VEC_Q * cols_of + j, 1), :] = total[:1, :pair]
            vec[pl.ds(VEC_V * cols_of + j, 1), :] = total[:1, 2 * pair :]
            w = jnp.concatenate([wq[...], wk[...], wv[...]], 1)
            dacc[...] += mm(d.T, w, 1, 1)

    @pl.when(step == heads_to)
    def _():
        totals = [jnp.zeros((1, width), F32) for _ in range(2)]
        for r in range(blk):
            at = slice(r * chunk, (r + 1) * chunk)
            grad = dacc[at, :]
            hat, sc = norm_parts(x0[at, :].astype(F32))
            dn = norm_back(grad, hat, sc, row(gain_one))
            din_s[at, :] = (x1[at, :] + dn).astype(BF16)
            for i, value in enumerate((grad * hat, grad)):
                totals[i] = totals[i] + jnp.sum(value, 0, keepdims=True)
        local_copy(din_s, din, move_sems.at[1]).start()
        put_vec(VEC_G1, totals[0])
        put_vec(VEC_B1, totals[1])

    def vec_copy(b):
        bit = lax.rem(lax.div(f, 1 << b), 2)
        return pltpu.make_async_remote_copy(
            src_ref=vec,
            dst_ref=vec_recv.at[b],
            send_sem=vec_sems.at[0, b],
            recv_sem=vec_sems.at[1, b],
            device_id=(f + (1 << b) * (1 - 2 * bit), z),
            device_id_type=pl.DeviceIdType.MESH,
        )

    def vec_blk_copy(s):
        return pltpu.make_async_remote_copy(
            src_ref=vec,
            dst_ref=vec_recv_blk.at[s - 1],
            send_sem=vec_blk_sems.at[0, s - 1],
            recv_sem=vec_blk_sems.at[1, s - 1],
            device_id=(f, lax.rem(z + s, blk)),
            device_id_type=pl.DeviceIdType.MESH,
        )

    @pl.when(step == heads_to)
    def _():
        @pl.loop(2, tail)
        def _(i):
            sums.tick(first + i, done)
            turn = lax.div(i - 2, DIN_EVERY)

            @pl.when((lax.rem(i - 2, DIN_EVERY) == 0) & (turn < pieces * (blk - 1)))
            def _():
                piece(send_part, turn, 1).start()

            for b in range(bits + 2):

                @pl.when(i == 2 + 2 * b)
                def _():
                    if 1 <= b <= bits:
                        vec_copy(b - 1).wait()
                        vec[...] += vec_recv[b - 1]
                    if b < bits:
                        vec_copy(b).start()
                    elif b == bits:
                        for s in range(1, blk):
                            vec_blk_copy(s).start()
                    else:
                        for s in range(1, blk):
                            vec_blk_copy(s).wait()
                        total = vec[...]
                        for s in range(1, blk):
                            total = total + vec_recv_blk[s - 1]
                        vec_out[...] = total

        @pl.loop(0, pieces * (blk - 1))
        def _(i):
            for kind in range(2):
                piece(send_part, i, kind).wait_send()
                piece(part_came, i, kind).wait_recv()

        local_copy(out_s, out, move_sems.at[0]).wait()
        local_copy(din_s, din, move_sems.at[1]).wait()

        @pl.loop(0, sums.count)
        def _(block):
            flush(block, lambda c: c.wait())


def mega(mesh_shape, count, ot, x0, y, w_out, b_out, gain_two, bias_two, up, up_bias, down, down_bias,
         qt, k, kt, v, lse, a1t, w_qkv, gain_one, ff_block=256):
    fields, blk = mesh_shape
    slots, width = x0.shape
    pair = 2 * HEAD_DIM
    pairs = width // pair
    ff_steps = up.shape[1] // ff_block
    bits = fields.bit_length() - 1
    n = fields * blk
    assert ff_block == 2 * LANES
    rows = -(-2 * width // (16 * n)) * 16 * n
    blocks = 2 * (ff_steps + pairs)
    levels = n.bit_length() - 1
    heads_to = ff_steps + 2 * pairs
    last_tick = 2 * ff_steps + 2 + 2 * (2 * pairs - 1) + offsets(bits, levels - bits)[-1]
    tail = last_tick + 1 - (2 * heads_to - 2)
    vec_rows = (8 + up.shape[1] // width) * (width // LANES)
    chunk = slots // blk
    cols_of = width // LANES

    def ff_at(i):
        return jnp.minimum(i, ff_steps - 1)

    def pair_at(i):
        return jnp.clip((i - ff_steps) // 2, 0, pairs - 1)

    tra = pl.BlockSpec((pair, slots), lambda i: (pair_at(i), 0))
    nat = pl.BlockSpec((slots, pair), lambda i: (0, pair_at(i)))

    def cols(part):
        return pl.BlockSpec((width, pair), lambda i: (0, part * pairs + pair_at(i)))

    hbm = pl.BlockSpec(memory_space=pl.ANY)
    one = (width,)
    dma = pltpu.SemaphoreType.DMA
    ahead = SLOTS_AHEAD
    flops = 12 * slots * width * up.shape[1] + 10 * slots * slots * width + 12 * slots * width * width
    return pl.pallas_call(
        partial(mega_kernel, fields, blk, rows, ff_steps, pairs, tail),
        grid=(heads_to + 1,),
        in_specs=[
            pl.BlockSpec(memory_space=pltpu.SMEM),
            whole((width, slots)),
            whole((slots, width)),
            whole((slots, width)),
            whole((width, width)),
            whole(one),
            whole(one),
            whole(one),
            pl.BlockSpec((width, ff_block), lambda i: (0, ff_at(i))),
            pl.BlockSpec((ff_block,), lambda i: (ff_at(i),)),
            pl.BlockSpec((ff_block, width), lambda i: (ff_at(i), 0)),
            whole(one),
            tra, nat, tra, nat,
            pl.BlockSpec((1, 2, slots), lambda i: (pair_at(i), 0, 0)),
            whole((width, slots)),
            cols(0), cols(1), cols(2),
            whole(one),
        ],
        out_specs=[hbm, hbm, hbm, hbm, hbm, hbm, whole((vec_rows, LANES))],
        out_shape=[
            jax.ShapeDtypeStruct((blk, chunk, width), BF16),
            jax.ShapeDtypeStruct((blk, chunk, width), BF16),
            jax.ShapeDtypeStruct((width, up.shape[1]), BF16),
            jax.ShapeDtypeStruct((up.shape[1], width), BF16),
            jax.ShapeDtypeStruct((width, 3 * width), BF16),
            jax.ShapeDtypeStruct((width, width), BF16),
            jax.ShapeDtypeStruct((vec_rows, LANES), F32),
        ],
        scratch_shapes=[
            pltpu.VMEM((slots, width), F32),
            pltpu.VMEM((slots, width), BF16),
            pltpu.VMEM((width, slots), BF16),
            pltpu.VMEM((slots, width), F32),
            pltpu.VMEM((slots, width), F32),
            pltpu.VMEM((slots, width), BF16),
            pltpu.VMEM((width, slots), BF16),
            pltpu.VMEM((3 * pair, slots), BF16),
            pltpu.VMEM((slots, width), BF16),
            pltpu.VMEM((2, HEAD_DIM, slots), F32),
            pltpu.VMEM((blocks, rows, LANES), BF16),
            pltpu.VMEM((vec_rows, LANES), F32),
            pltpu.VMEM((bits, vec_rows, LANES), F32),
            pltpu.VMEM((blk - 1, vec_rows, LANES), F32),
            dma((levels, ahead)),
            dma((levels, ahead)),
            dma((levels, ahead)),
            dma((levels, ahead)),
            dma((2, bits)),
            dma((2, blk - 1)),
            dma((2,)),
            dma((2, 2, 2 * pairs)),
            dma((blocks, cols_of)),
            *[pltpu.VMEM((2, ahead, rows >> (s + 1), LANES), BF16) for s in range(levels)],
        ],
        compiler_params=pltpu.CompilerParams(
            vmem_limit_bytes=67_000_000, collective_id=0, has_side_effects=True
        ),
        cost_estimate=pl.CostEstimate(flops=flops, bytes_accessed=60 * slots * width, transcendentals=0),
        name="mega",
    )(
        count, ot, x0, y, w_out, b_out, gain_two, bias_two, up, up_bias, down, down_bias,
        qt, k, kt, v, lse, a1t, w_qkv, w_qkv, w_qkv, gain_one,
    )


def widen(arrays, vecs, lengths, steps):
    count = len(arrays)

    def kernel(*refs):
        for src, dst in zip(refs[:count], refs[count + 1 : 2 * count + 1]):
            dst[...] = src[...].astype(F32)

        @pl.when(pl.program_id(0) == 0)
        def _():
            at = 0
            for dst, length in zip(refs[2 * count + 1 :], lengths):
                for i in range(length // LANES):
                    dst[i * LANES : (i + 1) * LANES] = refs[count][at + i, :]
                at += length // LANES

    specs = [pl.BlockSpec((a.shape[0] // steps, a.shape[1]), lambda i: (i, 0)) for a in arrays]
    return pl.pallas_call(
        kernel,
        grid=(steps,),
        in_specs=[*specs, whole(vecs.shape)],
        out_specs=[*specs, *[whole((n,)) for n in lengths]],
        out_shape=[
            *[jax.ShapeDtypeStruct(a.shape, F32) for a in arrays],
            *[jax.ShapeDtypeStruct((n,), F32) for n in lengths],
        ],
        compiler_params=pltpu.CompilerParams(vmem_limit_bytes=VMEM_BYTES),
        name="widen",
    )(*arrays, vecs)


def to_field(part):
    return lax.all_to_all(part, "blk", 0, 1, tiled=True)[0]


def per_device(
    mesh_shape, tokens, keep_index, counts, norm1_gain, norm1_bias, qkv_weight, query_bias, value_bias, out_weight,
    out_bias, norm2_gain, norm2_bias, up_weight, up_bias, down_weight, down_bias, cotangent,
):
    width = tokens.shape[2]
    x0 = place(mesh_shape[1], tokens, keep_index)
    a1t, qt, k, kt, v, vt = project(x0, norm1_gain, norm1_bias, qkv_weight, query_bias, value_bias)
    _, later = lax.optimization_barrier((x0, cotangent))
    y = to_field(later)
    _, ot, lse = attend(counts, qt, k, vt)
    output, input_grad, d_up, d_down, d_qkv, d_out, vecs = mega(
        mesh_shape, counts, ot, x0, y, out_weight, out_bias, norm2_gain, norm2_bias, up_weight, up_bias, down_weight,
        down_bias, qt, k, kt, v, lse, a1t, qkv_weight, norm1_gain,
    )
    lengths = [width] * 8 + [up_weight.shape[1]]
    d_up, d_down, d_qkv, d_out, *vec = widen((d_up, d_down, d_qkv, d_out), vecs, lengths, 6)
    return (
        output,
        input_grad,
        vec[0],
        vec[1],
        d_qkv,
        vec[2],
        vec[3],
        d_out,
        vec[4],
        vec[5],
        vec[6],
        d_up,
        vec[8],
        d_down,
        vec[7],
    )


def solution(mesh):
    rows = P("fields", "blk", None)
    return jax.shard_map(
        partial(per_device, (mesh.shape["fields"], mesh.shape["blk"])),
        mesh=mesh,
        in_specs=(rows, P("fields", "blk"), P("fields"), *[P()] * 13, rows),
        out_specs=(rows, rows, *[P()] * 13),
        check_vma=False,
    )
```
